32 devices in a mesh: dp: 4 (over x, core), fsdp: 8 (over z, y).
Axes of the slice: x: 2, y: 2, z: 4, core: 2. Of those that a mesh axis runs over, the one named last changes fastest.
Arguments:
- tokens: bfloat16 [224, 128, 768], P(('dp', 'fsdp')), may hold values from -6 to 6
- lengths: int32 [224], P(('dp', 'fsdp')), may hold values from 5 to 128, as said below
- pooled_grad: float32 [224, 768], P(('dp', 'fsdp')), may hold values from -5 to 5
- w_qkv: bfloat16 [768, 2304], P('fsdp'), may hold values from -0.21875 to 0.21875
- bias_query: bfloat16 [768], P('fsdp'), may hold values from -3 to 3
- bias_value: bfloat16 [768], P('fsdp'), may hold values from -3 to 3
- w_out: bfloat16 [768, 768], P('fsdp'), may hold values from -0.875 to 0.875
- bias_out: bfloat16 [768], P('fsdp'), may hold values from -3 to 3
- gain_attn: bfloat16 [768], P('fsdp'), may hold values from 0.099609375 to 1.8984375
- shift_attn: bfloat16 [768], P('fsdp'), may hold values from -3 to 3
- w_in: bfloat16 [768, 3072], P('fsdp'), may hold values from -0.21875 to 0.21875
- bias_in: bfloat16 [3072], P('fsdp'), may hold values from -3 to 3
- w_down: bfloat16 [3072, 768], P('fsdp'), may hold values from -0.109375 to 0.109375
- bias_down: bfloat16 [768], P('fsdp'), may hold values from -2 to 2
- gain_ffn: bfloat16 [768], P('fsdp'), may hold values from 0.099609375 to 1.8984375
- shift_ffn: bfloat16 [768], P('fsdp'), may hold values from -3 to 3
Outputs:
- pooled: float32 [224, 768], P(('dp', 'fsdp'))
- grad_tokens: float32 [224, 128, 768], P(('dp', 'fsdp'))
- grad_w_qkv: float32 [768, 2304], P('fsdp')
- grad_bias_query: float32 [768], P('fsdp')
- grad_bias_value: float32 [768], P('fsdp')
- grad_w_out: float32 [768, 768], P('fsdp')
- grad_bias_out: float32 [768], P('fsdp')
- grad_gain_attn: float32 [768], P('fsdp')
- grad_shift_attn: float32 [768], P('fsdp')
- grad_w_in: float32 [768, 3072], P('fsdp')
- grad_bias_in: float32 [3072], P('fsdp')
- grad_w_down: float32 [3072, 768], P('fsdp')
- grad_bias_down: float32 [768], P('fsdp')
- grad_gain_ffn: float32 [768], P('fsdp')
- grad_shift_ffn: float32 [768], P('fsdp')
The draws below stay inside these ranges and needn't reach their ends.
Inputs may be any that keep to these rules, and one draw needn't show every extreme that they name: `lengths`: some sentence has 128 real tokens and some has 5.
All inputs are finite; a program needn't handle non-finite values.
Results may differ from the reference program's by a relative error of at most 0.019.
Values may be sent and summed in bfloat16 or wider, within the bound.
No kernel may reach another device: no remote copies, remote signals or barrier semaphores. Data moves between devices by JAX's collectives and lax.ppermute only.
A program may use at most 192 MiB of HBM per device.

```python
import math
import jax
import jax.numpy as jnp
from jax import lax

D = 768
HEADS = 12
HEAD = 64
FF = 3072
L = 128
SENTS = 224


def draw_lengths(key, part):
    key_list = jax.random.split(key, 6)
    draw_one = jax.random.randint(key_list[0], (SENTS,), 1, L - 3)
    draw_two = jax.random.randint(key_list[1], (SENTS,), 1, L - 3)
    draw_three = jax.random.randint(key_list[2], (SENTS,), 1, L - 3)
    draw_four = jax.random.randint(key_list[3], (SENTS,), 1, L - 3)
    lengths_drawn = 4 + jnp.maximum(jnp.minimum(draw_one, draw_two), jnp.minimum(draw_three, draw_four))
    longest = jax.random.randint(key_list[4], (), 0, SENTS)
    shortest = jax.random.randint(key_list[5], (), 0, SENTS - 1)
    shortest = jnp.where(shortest >= longest, shortest + 1, shortest)
    places = jnp.arange(SENTS)
    lengths_drawn = jnp.where(places == longest, L, lengths_drawn)
    lengths_drawn = jnp.where(places == shortest, 5, lengths_drawn)
    return lengths_drawn.astype(jnp.int32)


def column_pattern(key):
    pattern_key = jax.random.fold_in(key, 4242)
    sign_key, size_key = jax.random.split(pattern_key)
    signs = jnp.where(jax.random.bernoulli(sign_key, 0.5, (D,)), 1.0, -1.0).astype(jnp.float32)
    magnitudes = jax.random.uniform(size_key, (D,), jnp.float32, 1.0, 2.0)
    return signs * magnitudes


def draw_bias_down(key, part):
    return column_pattern(key).astype(jnp.bfloat16)


def draw_pooled_grad(key, part):
    pattern = column_pattern(key)
    own_key = jax.random.fold_in(key, 5151)
    sign_key, noise_key = jax.random.split(own_key)
    sentence_sign = jnp.where(jax.random.bernoulli(sign_key, 0.5, (SENTS, 1)), 1.0, -1.0).astype(jnp.float32)
    noise = 0.6 * jax.random.truncated_normal(noise_key, -5.0, 5.0, (SENTS, D), jnp.float32)
    values = sentence_sign * pattern[None, :] + noise
    return jnp.clip(values, -5.0, 5.0).astype(jnp.float32)


def shard_levels(key, shape, cuts, smallest, high):
    level, own = 1.0, jax.random.fold_in(key, 6)
    for axis_at, parts in cuts:
        heights = jnp.exp(jax.random.uniform(jax.random.fold_in(own, axis_at), (parts,), jnp.float32, smallest / len(cuts), high / len(cuts)))
        level = level * jnp.repeat(heights, shape[axis_at] // parts).reshape([-1 if axis == axis_at else 1 for axis in range(len(shape))])
    return level


def gaussian(rng, extent, deviation, reach, cuts=(), held_as=jnp.bfloat16):
    values = deviation * jax.random.normal(rng, extent, jnp.float32)
    if cuts:
        values = values * shard_levels(rng, extent, cuts, -0.22, 0.18)
    return jnp.clip(values, -reach, reach).astype(held_as)


def setup_inputs(seed: int = 0) -> dict:
    arg_keys = jax.random.split(jax.random.key(seed), 17)
    tokens = gaussian(arg_keys[0], (SENTS, L, D), 1.0, 6.0, ((0, 32),))
    lengths = draw_lengths(jax.random.fold_in(arg_keys[16], 71), 0)
    pooled_grad = draw_pooled_grad(jax.random.fold_in(arg_keys[16], 71), 0)
    w_qkv = gaussian(arg_keys[3], (D, 3 * D), D ** -0.5, 0.21875, ((0, 8),))
    bias_query = gaussian(arg_keys[4], (D,), 0.5, 3.0, ((0, 8),))
    bias_value = gaussian(arg_keys[5], (D,), 0.5, 3.0, ((0, 8),))
    w_out = gaussian(arg_keys[6], (D, D), (D // 16) ** -0.5, 0.875, ((0, 8),))
    bias_out = gaussian(arg_keys[7], (D,), 0.5, 3.0, ((0, 8),))
    gain_attn = jnp.clip(1.0 + 0.18 * jax.random.normal(arg_keys[8], (D,), jnp.float32), 0.099609375, 1.8984375).astype(jnp.bfloat16)
    shift_attn = gaussian(arg_keys[9], (D,), 0.5, 3.0, ((0, 8),))
    w_in = gaussian(arg_keys[10], (D, FF), D ** -0.5, 0.21875, ((0, 8),))
    bias_in = gaussian(arg_keys[11], (FF,), 0.5, 3.0, ((0, 8),))
    w_down = gaussian(arg_keys[12], (FF, D), FF ** -0.5, 0.109375, ((0, 8),))
    bias_down = draw_bias_down(jax.random.fold_in(arg_keys[16], 71), 0)
    gain_ffn = jnp.clip(1.0 + 0.18 * jax.random.normal(arg_keys[14], (D,), jnp.float32), 0.099609375, 1.8984375).astype(jnp.bfloat16)
    shift_ffn = gaussian(arg_keys[15], (D,), 0.5, 3.0, ((0, 8),))
    return {"tokens": tokens, "lengths": lengths, "pooled_grad": pooled_grad, "w_qkv": w_qkv, "bias_query": bias_query, "bias_value": bias_value, "w_out": w_out, "bias_out": bias_out, "gain_attn": gain_attn, "shift_attn": shift_attn, "w_in": w_in, "bias_in": bias_in, "w_down": w_down, "bias_down": bias_down, "gain_ffn": gain_ffn, "shift_ffn": shift_ffn}


norm_eps = 1e-06
highest = lax.Precision.HIGHEST

@jax.custom_vjp
def low(v):
    return lax.optimization_barrier(v.astype(jnp.bfloat16)).astype(jnp.float32)

@jax.custom_vjp
def low_back(v):
    return v

def low_keep(v):
    return (low(v), None)

def low_pass(kept, grad):
    return (grad,)

def back_keep(v):
    return (v, None)

def back_low(kept, grad):
    return (low(grad),)
low.defvjp(low_keep, low_pass)
low_back.defvjp(back_keep, back_low)

def matmul_high(lhs_mat, rhs_mat):
    return jnp.dot(lhs_mat, rhs_mat, precision=highest, preferred_element_type=jnp.float32)

def layer_norm(token_rows, gain_vec, shift_vec):
    row_mean = lax.optimization_barrier(jnp.mean(token_rows, -1, keepdims=True))
    centred = token_rows - row_mean
    variance = lax.optimization_barrier(jnp.mean(centred * centred, -1, keepdims=True))
    return centred * lax.rsqrt(variance + norm_eps) * gain_vec + shift_vec

def layer_block(params, block_tokens, block_lengths):
    w_qkv, bias_query, bias_value, w_out, bias_out, gain_attn, shift_attn, w_in, bias_in, w_down, bias_down, gain_ffn, shift_ffn = params
    sentences = block_tokens.shape[0]
    token_rows = block_tokens.reshape(sentences * L, D)
    bias_qkv = jnp.concatenate([bias_query, jnp.zeros_like(bias_query), bias_value])
    packed = low_back(low(matmul_high(token_rows, w_qkv) + bias_qkv))
    packed = packed.reshape(sentences, L, 3, HEADS, HEAD)
    query_rows = packed[:, :, 0]
    key_rows = packed[:, :, 1]
    value_rows = packed[:, :, 2]
    key_valid = jnp.arange(L)[None, :] < block_lengths[:, None]
    scores = jnp.einsum('sqhd,skhd->shqk', query_rows, key_rows, precision=highest) * HEAD ** (-0.5)
    scores = low_back(jnp.where(key_valid[:, None, None, :], scores, -1000000000.0))
    attn_probs = low(jax.nn.softmax(scores, axis=-1))
    context = jnp.einsum('shqk,skhd->sqhd', attn_probs, value_rows, precision=highest)
    context = low_back(low(context.reshape(sentences * L, D)))
    attn_out = low_back(matmul_high(context, w_out) + bias_out)
    hidden = layer_norm(token_rows + attn_out, gain_attn, shift_attn)
    up_rows = low_back(matmul_high(low(hidden), w_in) + bias_in)
    active = low(jax.nn.gelu(up_rows, approximate=False))
    ffn_out = low_back(matmul_high(active, w_down) + bias_down)
    output = layer_norm(hidden + ffn_out, gain_ffn, shift_ffn).reshape(sentences, L, D)
    valid_mask = key_valid.astype(jnp.float32)
    return lax.optimization_barrier(jnp.sum(output * valid_mask[:, :, None], 1)) / block_lengths[:, None].astype(jnp.float32)

def reference(tokens, lengths, pooled_grad, w_qkv, bias_query, bias_value, w_out, bias_out, gain_attn, shift_attn, w_in, bias_in, w_down, bias_down, gain_ffn, shift_ffn):
    params = tuple((weight.astype(jnp.float32) for weight in (w_qkv, bias_query, bias_value, w_out, bias_out, gain_attn, shift_attn, w_in, bias_in, w_down, bias_down, gain_ffn, shift_ffn)))
    group_size = math.gcd(SENTS, 32)
    block_count = SENTS // group_size
    length_blocks = lengths.reshape(block_count, group_size)
    step_fn = jax.checkpoint(layer_block)

    def whole_layer(param_set, token_set):
        token_blocks = token_set.reshape(block_count, group_size, L, D)
        pooled_blocks = lax.map(lambda block_pair: step_fn(param_set, block_pair[0], block_pair[1]), (token_blocks, length_blocks))
        return pooled_blocks.reshape(SENTS, D)
    pooled, pull_back = jax.vjp(whole_layer, params, tokens.astype(jnp.float32))
    param_grads, grad_tokens = pull_back(pooled_grad.astype(jnp.float32))
    return (pooled, grad_tokens, param_grads[0], param_grads[1], param_grads[2], param_grads[3], param_grads[4], param_grads[5], param_grads[6], param_grads[7], param_grads[8], param_grads[9], param_grads[10], param_grads[11], param_grads[12])
```

```python
from functools import partial

import jax
import jax.numpy as jnp
from jax import lax
from jax.experimental import pallas as pl
from jax.experimental.pallas import tpu as pltpu
from jax.sharding import PartitionSpec as P

norm_eps = 1e-06

HEAD = 64
NORM_EPS = 1e-06
BF = jnp.bfloat16
F32 = jnp.float32
VMEM_LIMIT = 60 * 1024 * 1024


def dot(a, b):
    return lax.dot_general(a, b, (((1,), (0,)), ((), ())), preferred_element_type=F32)


def dot_nt(a, b):
    return lax.dot_general(a, b, (((1,), (1,)), ((), ())), preferred_element_type=F32)


def dot_tn(a, b):
    return lax.dot_general(a, b, (((0,), (0,)), ((), ())), preferred_element_type=F32)


def aligned(value, step):
    return pl.multiple_of(value, step)


class Place:
    def __init__(self, ids_ref):
        self.z, self.y, self.x, self.c = ids_ref[0], ids_ref[1], ids_ref[2], ids_ref[3]

    def shard(self, k, yy):
        return lax.bitwise_xor(self.z, k) * 2 + lax.bitwise_xor(self.y, yy)


def piece_copies(place, bufs, dst, sems, shard_rows, split_x):
    half = shard_rows // 2
    copies = []
    at = 0
    for cc in range(2):
        core = lax.bitwise_xor(place.c, cc)
        for xx in range(2 if split_x else 1):
            for yy in range(2):
                buf = bufs[at]
                at += 1
                width = buf.shape[-1]
                for k in range(4):
                    row = aligned(place.shard(k, yy) * shard_rows + core * half, 16)
                    if split_x:
                        col = aligned(lax.bitwise_xor(place.x, xx) * width, 128)
                        target = dst.at[pl.ds(row, half), pl.ds(col, width)]
                    else:
                        target = dst.at[pl.ds(row, half), :]
                    copies.append(
                        pltpu.make_async_copy(buf.at[k], target, sems.at[len(copies)])
                    )
    return copies


def emit_blocks(place, acc, send, keep, shard_rows, split_x):
    half = shard_rows // 2
    nx = 2 if split_x else 1
    width = acc.shape[1] // nx
    for cc, out in ((0, keep), (1, send)):
        core = lax.bitwise_xor(place.c, cc)
        for xx in range(nx):
            for yy in range(2):

                def step(k, carry, cc=cc, xx=xx, yy=yy, out=out, core=core):
                    row = aligned(place.shard(k, yy) * shard_rows + core * half, 16)
                    if split_x:
                        col = aligned(lax.bitwise_xor(place.x, xx) * width, 128)
                        block = acc[pl.ds(row, half), pl.ds(col, width)]
                    else:
                        block = acc[pl.ds(row, half), :]
                    out[xx, yy, k] = block.astype(BF)
                    return carry

                lax.fori_loop(0, 4, step, 0)


def call(body, name, ins, outs, scratch, flops, transcendentals=0):
    spaces = {
        "s": pl.BlockSpec(memory_space=pltpu.SMEM),
        "v": pl.BlockSpec(memory_space=pltpu.VMEM),
        "a": pl.BlockSpec(memory_space=pl.ANY),
    }
    moved = sum(a.size * a.dtype.itemsize for a, _ in ins) + sum(
        o.size * o.dtype.itemsize for o in outs
    )
    return pl.pallas_call(
        body,
        name=name,
        out_shape=tuple(outs),
        in_specs=[spaces[s] for _, s in ins],
        out_specs=tuple(spaces["v"] for _ in outs),
        scratch_shapes=scratch,
        compiler_params=pltpu.CompilerParams(vmem_limit_bytes=VMEM_LIMIT),
        cost_estimate=pl.CostEstimate(
            flops=flops, transcendentals=transcendentals, bytes_accessed=moved
        ),
    )(*[a for a, _ in ins])


def struct(shape, dtype):
    return jax.ShapeDtypeStruct(shape, dtype)


def two_heads(block):
    low = lax.broadcasted_iota(jnp.int32, block.shape, 1) < HEAD
    zero = jnp.zeros_like(block)
    return jnp.concatenate([jnp.where(low, block, zero), jnp.where(low, zero, block)], axis=0)


def one_of_two(stacked):
    rows = stacked.shape[0] // 2
    low = lax.broadcasted_iota(jnp.int32, (rows, stacked.shape[1]), 1) < HEAD
    return jnp.where(low, stacked[:rows], stacked[rows:])


def masked_scores(query, keys2, count, length):
    scores = dot_nt(query, keys2)
    slot = lax.broadcasted_iota(jnp.int32, scores.shape, 1)
    slot = jnp.where(slot >= length, slot - length, slot)
    return jnp.where(slot < count, scores, -1000000000.0)


def halves(stat_a, stat_b, length):
    rows = stat_a.shape[0]
    return jnp.concatenate(
        [jnp.broadcast_to(stat_a, (rows, length)), jnp.broadcast_to(stat_b, (rows, length))], axis=1
    )


def attend_forward(tokens, counts, ids, bufs, sentences, length):
    rows, width = tokens.shape
    pairs = width // 128
    group = 256

    def body(ids_ref, counts_ref, x_ref, b0, b1, b2, b3, qkv_ref, ctx_ref, lse_ref, vec_ref, w_ref, sems):
        place = Place(ids_ref)
        copies = piece_copies(place, (b0, b1, b2, b3), w_ref, sems, width // 8, False)
        for copy in copies:
            copy.start()
        for copy in copies:
            copy.wait()
        vec_ref[...] = w_ref[:, 3 * width :].astype(F32).T[: vec_ref.shape[0]]
        x = x_ref[...]
        for part in range(3):
            for g in range(width // group):
                col = part * width + g * group
                y = dot(x, w_ref[:, col : col + group])
                if part != 1:
                    bias = vec_ref[part // 2 : part // 2 + 1, g * group : (g + 1) * group]
                    y = y + bias
                qkv_ref[:, col : col + group] = y.astype(BF)

        def sentence(s, carry):
            row = aligned(s * length, length)
            count = counts_ref[s]
            lane = lax.broadcasted_iota(jnp.int32, (length, 128), 1)
            lse_all = jnp.zeros((length, 128), F32)
            for p in range(pairs):
                here = pl.ds(row, length)
                query = qkv_ref[here, p * 128 : (p + 1) * 128] * jnp.asarray(HEAD**-0.5, BF)
                keys2 = two_heads(qkv_ref[here, width + p * 128 : width + (p + 1) * 128])
                values2 = two_heads(qkv_ref[here, 2 * width + p * 128 : 2 * width + (p + 1) * 128])
                scores = masked_scores(query, keys2, count, length)
                a, b = scores[:, :length], scores[:, length:]
                max_a = jnp.max(a, -1, keepdims=True)
                max_b = jnp.max(b, -1, keepdims=True)
                e_a, e_b = jnp.exp(a - max_a), jnp.exp(b - max_b)
                sum_a = jnp.sum(e_a, -1, keepdims=True)
                sum_b = jnp.sum(e_b, -1, keepdims=True)
                lse_all = jnp.where(lane == 2 * p, max_a + jnp.log(sum_a), lse_all)
                lse_all = jnp.where(lane == 2 * p + 1, max_b + jnp.log(sum_b), lse_all)
                probs = jnp.concatenate([e_a * (1.0 / sum_a), e_b * (1.0 / sum_b)], axis=1).astype(BF)
                ctx_ref[here, p * 128 : (p + 1) * 128] = dot(probs, values2).astype(BF)
            lse_ref[pl.ds(row, length), :] = lse_all
            return carry

        lax.fori_loop(0, sentences, sentence, 0)

    return call(
        body,
        "qkv_attention",
        [(ids, "s"), (counts, "s"), (tokens, "v")] + [(b, "a") for b in bufs],
        [
            struct((rows, 3 * width), BF),
            struct((rows, width), BF),
            struct((rows, 128), F32),
            struct((16, width), F32),
        ],
        [pltpu.VMEM((width, 3 * width + 128), BF), pltpu.SemaphoreType.DMA((16,))],
        2 * rows * width * 3 * width + 8 * rows * length * width,
        rows * length * width // HEAD,
    )


def layer_norm(v):
    centred = v - jnp.mean(v, -1, keepdims=True)
    inverse = lax.rsqrt(jnp.mean(centred * centred, -1, keepdims=True) + NORM_EPS)
    return centred * inverse, inverse


def norm_back(grad, normed, inverse, gain):
    scaled = grad * gain
    return inverse * (
        scaled
        - jnp.mean(scaled, -1, keepdims=True)
        - normed * jnp.mean(scaled * normed, -1, keepdims=True)
    )


def row(vec_ref, at):
    return vec_ref[at : at + 1, :]


def up_forward(context, tokens, vec, bias_in, ids, bufs, length):
    rows, width = tokens.shape
    wide = bias_in.shape[1]
    group = 256

    def body(ids_ref, ctx_ref, x_ref, vec_ref, bin_ref, *rest):
        bufs_ref = rest[: len(bufs)]
        n_ref, inv_ref, low_ref, act_ref, slope_ref, w_ref, sems = rest[len(bufs) :]
        place = Place(ids_ref)
        copies = piece_copies(place, bufs_ref, w_ref, sems, width // 8, True)
        for copy in copies:
            copy.start()
        for copy in copies:
            copy.wait()
        n_ref[...] = dot(ctx_ref[...], w_ref[:, :width])

        def norm_rows(s, carry):
            here = pl.ds(aligned(s * length, length), length)
            v = x_ref[here, :].astype(F32) + (n_ref[here, :] + row(vec_ref, 2))
            normed, inverse = layer_norm(v)
            n_ref[here, :] = normed
            inv_ref[here, :] = jnp.broadcast_to(inverse, (length, 128))
            low_ref[here, :] = (normed * row(vec_ref, 3) + row(vec_ref, 4)).astype(BF)
            return carry

        lax.fori_loop(0, rows // length, norm_rows, 0)

        def columns(g, carry):
            col = aligned(g * group, group)
            u = dot(low_ref[...], w_ref[:, pl.ds(width + col, group)]) + bin_ref[:, pl.ds(col, group)]
            cdf = 0.5 * (1.0 + lax.erf(u * (0.5**0.5)))
            pdf = jnp.exp(-0.5 * u * u) * 0.3989422804014327
            act_ref[:, pl.ds(col, group)] = (u * cdf).astype(BF)
            slope_ref[:, pl.ds(col, group)] = (cdf + u * pdf).astype(BF)
            return carry

        lax.fori_loop(0, wide // group, columns, 0)

    return call(
        body,
        "out_norm_up",
        [(ids, "s"), (context, "v"), (tokens, "v"), (vec, "v"), (bias_in, "v")]
        + [(b, "a") for b in bufs],
        [
            struct((rows, width), F32),
            struct((rows, 128), F32),
            struct((rows, width), BF),
            struct((rows, wide), BF),
            struct((rows, wide), BF),
        ],
        [pltpu.VMEM((width, width + wide), BF), pltpu.SemaphoreType.DMA((32,))],
        2 * rows * width * (width + wide),
        2 * rows * wide,
    )


def down_forward(active, normed, vec, counts, pooled_grad, ids, bufs, sentences, length):
    rows, wide = active.shape
    width = normed.shape[1]
    shard = wide // 8
    group = 256

    def body(ids_ref, counts_ref, act_ref, n_ref, vec_ref, pg_ref, *rest):
        bufs_ref = rest[: len(bufs)]
        pooled_ref, gres_ref, glow_ref, vg_ref, send_ref, keep_ref, w_ref, dw_ref, sems = rest[len(bufs) :]
        place = Place(ids_ref)
        copies = piece_copies(place, bufs_ref, w_ref, sems, shard, False)
        for copy in copies:
            copy.start()
        for copy in copies:
            copy.wait()
        for g in range(width // group):
            gres_ref[:, g * group : (g + 1) * group] = dot(
                act_ref[...], w_ref[:, g * group : (g + 1) * group]
            )
        vg_ref[...] = jnp.zeros_like(vg_ref)

        def norm_rows(s, carry):
            here = pl.ds(aligned(s * length, length), length)
            hidden = n_ref[here, :] * row(vec_ref, 3) + row(vec_ref, 4)
            n2, inverse = layer_norm(hidden + (gres_ref[here, :] + row(vec_ref, 5)))
            valid = lax.broadcasted_iota(jnp.int32, (length, width), 0) < counts_ref[s]
            count = counts_ref[s].astype(F32)
            out = jnp.where(valid, n2 * row(vec_ref, 6) + row(vec_ref, 7), 0.0)
            pooled_ref[pl.ds(s, 1), :] = jnp.sum(out, 0, keepdims=True) / count
            grad = jnp.where(valid, pg_ref[pl.ds(s, 1), :] / count, 0.0)
            vg_ref[0:1, :] += jnp.sum(grad * n2, 0, keepdims=True)
            vg_ref[1:2, :] += jnp.sum(grad, 0, keepdims=True)
            gres = norm_back(grad, n2, inverse, row(vec_ref, 6))
            gres_ref[here, :] = gres
            glow = gres.astype(BF)
            glow_ref[here, :] = glow
            vg_ref[2:3, :] += jnp.sum(glow.astype(F32), 0, keepdims=True)
            return carry

        lax.fori_loop(0, sentences, norm_rows, 0)
        glow_t = glow_ref[...].T
        for f in range(8):
            dw_ref[...] = dot(glow_t, act_ref[:, f * shard : (f + 1) * shard])
            rel = lax.bitwise_xor(place.z * 2 + place.y, f)
            k, yy = lax.div(rel, 2), lax.rem(rel, 2)
            half = width // 2
            for cc, out in ((0, keep_ref), (1, send_ref)):
                core = lax.bitwise_xor(place.c, cc)
                out[0, yy, k] = dw_ref[pl.ds(aligned(core * half, half), half), :].astype(BF)

    return call(
        body,
        "down_norm_back",
        [(ids, "s"), (counts, "s"), (active, "v"), (normed, "v"), (vec, "v"), (pooled_grad, "v")]
        + [(b, "a") for b in bufs],
        [
            struct((sentences, width), F32),
            struct((rows, width), F32),
            struct((rows, width), BF),
            struct((8, width), F32),
            struct((1, 2, 4, width // 2, shard), BF),
            struct((1, 2, 4, width // 2, shard), BF),
        ],
        [pltpu.VMEM((wide, width), BF), pltpu.VMEM((width, shard), F32), pltpu.SemaphoreType.DMA((16,))],
        4 * rows * width * wide,
    )


def up_backward(glow, slope, low, ids, bufs):
    rows, width = glow.shape
    wide = slope.shape[1]
    shard = wide // 8
    group = 256

    def body(ids_ref, glow_ref, slope_ref, low_ref, *rest):
        bufs_ref = rest[: len(bufs)]
        gup_ref, gbias_ref, send_ref, keep_ref, w_ref, dw_ref, sems = rest[len(bufs) :]
        place = Place(ids_ref)
        copies = piece_copies(place, bufs_ref, w_ref, sems, shard, False)
        for copy in copies:
            copy.start()
        for copy in copies:
            copy.wait()
        low_t = low_ref[...].T

        def columns(g, carry):
            col = aligned(g * group, group)
            gact = dot_nt(glow_ref[...], w_ref[pl.ds(col, group), :])
            gup = (gact * slope_ref[:, pl.ds(col, group)].astype(F32)).astype(BF)
            gup_ref[:, pl.ds(col, group)] = gup
            gbias_ref[:, pl.ds(col, group)] = jnp.sum(gup.astype(F32), 0, keepdims=True)
            dw_ref[:, pl.ds(col, group)] = dot(low_t, gup)
            return carry

        lax.fori_loop(0, wide // group, columns, 0)
        emit_blocks(place, dw_ref, send_ref, keep_ref, width // 8, True)

    blocks = struct((2, 2, 4, width // 16, wide // 2), BF)
    return call(
        body,
        "up_back",
        [(ids, "s"), (glow, "v"), (slope, "v"), (low, "v")] + [(b, "a") for b in bufs],
        [struct((rows, wide), BF), struct((1, wide), F32), blocks, blocks],
        [pltpu.VMEM((wide, width), BF), pltpu.VMEM((width, wide), F32), pltpu.SemaphoreType.DMA((16,))],
        4 * rows * width * wide,
    )


def hidden_backward(gup, gres, normed, inverse, vec, ids, bufs, length):
    rows, wide = gup.shape
    width = gres.shape[1]
    group = 256

    def body(ids_ref, gup_ref, gres_ref, n_ref, inv_ref, vec_ref, *rest):
        bufs_ref = rest[: len(bufs)]
        gattn_ref, glow_ref, gctx_ref, vg_ref, w_ref, sems = rest[len(bufs) :]
        place = Place(ids_ref)
        copies = piece_copies(place, bufs_ref, w_ref, sems, width // 8, True)
        for copy in copies:
            copy.start()
        for copy in copies:
            copy.wait()
        for g in range(width // group):
            gattn_ref[:, g * group : (g + 1) * group] = dot_nt(
                gup_ref[...], w_ref[g * group : (g + 1) * group, width:]
            )
        vg_ref[...] = jnp.zeros_like(vg_ref)

        def norm_rows(s, carry):
            here = pl.ds(aligned(s * length, length), length)
            grad = gattn_ref[here, :] + gres_ref[here, :]
            normed = n_ref[here, :]
            vg_ref[0:1, :] += jnp.sum(grad * normed, 0, keepdims=True)
            vg_ref[1:2, :] += jnp.sum(grad, 0, keepdims=True)
            gattn = norm_back(grad, normed, inv_ref[here, 0:1], row(vec_ref, 3))
            gattn_ref[here, :] = gattn
            glow = gattn.astype(BF)
            glow_ref[here, :] = glow
            vg_ref[2:3, :] += jnp.sum(glow.astype(F32), 0, keepdims=True)
            return carry

        lax.fori_loop(0, rows // length, norm_rows, 0)
        for g in range(width // group):
            gctx_ref[:, g * group : (g + 1) * group] = dot_nt(
                glow_ref[...], w_ref[g * group : (g + 1) * group, :width]
            ).astype(BF)

    return call(
        body,
        "hidden_back",
        [(ids, "s"), (gup, "v"), (gres, "v"), (normed, "v"), (inverse, "v"), (vec, "v")]
        + [(b, "a") for b in bufs],
        [
            struct((rows, width), F32),
            struct((rows, width), BF),
            struct((rows, width), BF),
            struct((8, width), F32),
        ],
        [pltpu.VMEM((width, width + wide), BF), pltpu.SemaphoreType.DMA((32,))],
        2 * rows * width * (width + wide),
    )


def attend_backward(qkv, gctx, lse, tokens, context, glow, vgrads, counts, ids, sentences, length):
    rows, width = tokens.shape
    pairs = width // 128
    group = 256
    total = 4 * width + 256

    def body(ids_ref, counts_ref, qkv_ref, gctx_ref, lse_ref, x_ref, ctx_ref, glow_ref, vg_ref, gqkv_ref, send_ref, keep_ref, dw_ref, vs_ref):
        place = Place(ids_ref)
        vs_ref[...] = jnp.zeros_like(vs_ref)
        vs_ref[0:16, :] = vg_ref[...]

        def sentence(s, carry):
            here = pl.ds(aligned(s * length, length), length)
            count = counts_ref[s]
            lse_all = lse_ref[here, :]
            for p in range(pairs):
                cols = slice(p * 128, (p + 1) * 128)
                query = qkv_ref[here, cols] * jnp.asarray(HEAD**-0.5, BF)
                keys2 = two_heads(qkv_ref[here, width + p * 128 : width + (p + 1) * 128])
                values2 = two_heads(qkv_ref[here, 2 * width + p * 128 : 2 * width + (p + 1) * 128])
                gout = gctx_ref[here, cols]
                scores = masked_scores(query, keys2, count, length)
                lse2 = halves(lse_all[:, 2 * p : 2 * p + 1], lse_all[:, 2 * p + 1 : 2 * p + 2], length)
                probs = jnp.exp(scores - lse2)
                gprobs = dot_nt(gout, values2)
                weighted = gprobs * probs
                sums = halves(
                    jnp.sum(weighted[:, :length], -1, keepdims=True),
                    jnp.sum(weighted[:, length:], -1, keepdims=True),
                    length,
                )
                gscores = (probs * (gprobs - sums)).astype(BF)
                gq = dot(gscores, keys2) * HEAD**-0.5
                gk = one_of_two(dot_tn(gscores, query))
                gv = one_of_two(dot_tn(probs.astype(BF), gout))
                gq, gk, gv = gq.astype(BF), gk.astype(BF), gv.astype(BF)
                gqkv_ref[here, cols] = gq
                gqkv_ref[here, width + p * 128 : width + (p + 1) * 128] = gk
                gqkv_ref[here, 2 * width + p * 128 : 2 * width + (p + 1) * 128] = gv
                vs_ref[0:1, cols] += jnp.sum(gq.astype(F32), 0, keepdims=True)
                vs_ref[1:2, cols] += jnp.sum(gv.astype(F32), 0, keepdims=True)
            return carry

        lax.fori_loop(0, sentences, sentence, 0)
        x_t = x_ref[...].T

        def columns(g, carry):
            col = aligned(g * group, group)
            dw_ref[:, pl.ds(col, group)] = dot(x_t, gqkv_ref[:, pl.ds(col, group)])
            return carry

        lax.fori_loop(0, 3 * width // group, columns, 0)
        dw_ref[:, 3 * width : 4 * width] = dot_tn(ctx_ref[...], glow_ref[...])
        dw_ref[:, 4 * width : 4 * width + 128] = vs_ref[...].T
        dw_ref[:, 4 * width + 128 :] = jnp.zeros((width, 128), F32)
        emit_blocks(place, dw_ref, send_ref, keep_ref, width // 8, True)

    blocks = struct((2, 2, 4, width // 16, total // 2), BF)
    return call(
        body,
        "attention_back",
        [
            (ids, "s"),
            (counts, "s"),
            (qkv, "v"),
            (gctx, "v"),
            (lse, "v"),
            (tokens, "v"),
            (context, "v"),
            (glow, "v"),
            (vgrads, "v"),
        ],
        [struct((rows, 3 * width), BF), blocks, blocks],
        [pltpu.VMEM((width, total), F32), pltpu.VMEM((128, width), F32)],
        2 * rows * width * 4 * width + 20 * rows * length * width,
        rows * length * width // HEAD,
    )


def tokens_backward(gqkv, gattn, ids, bufs):
    rows, width = gattn.shape
    group = 256

    def body(ids_ref, gqkv_ref, gattn_ref, *rest):
        bufs_ref = rest[: len(bufs)]
        gx_ref, w_ref, sems = rest[len(bufs) :]
        place = Place(ids_ref)
        copies = piece_copies(place, bufs_ref, w_ref, sems, width // 8, False)
        for copy in copies:
            copy.start()
        for copy in copies:
            copy.wait()
        for g in range(width // group):
            gx_ref[:, g * group : (g + 1) * group] = (
                dot_nt(gqkv_ref[...], w_ref[g * group : (g + 1) * group, : 3 * width])
                + gattn_ref[:, g * group : (g + 1) * group]
            )

    return call(
        body,
        "tokens_back",
        [(ids, "s"), (gqkv, "v"), (gattn, "v")] + [(b, "a") for b in bufs],
        [struct((rows, width), F32)],
        [pltpu.VMEM((width, 3 * width + 128), BF), pltpu.SemaphoreType.DMA((16,))],
        2 * rows * width * 3 * width,
    )[0]


def norm_parts(token_rows, gain_vec, shift_vec):
    row_mean = jnp.mean(token_rows, -1, keepdims=True)
    centred = token_rows - row_mean
    inverse = lax.rsqrt(jnp.mean(centred * centred, -1, keepdims=True) + norm_eps)
    normed = centred * inverse
    return (normed * gain_vec + shift_vec, normed, inverse)


def plain_norm_back(grad_out, normed, inverse, gain_vec):
    grad_gain = jnp.sum(grad_out * normed, 0)
    grad_shift = jnp.sum(grad_out, 0)
    scaled = grad_out * gain_vec
    grad_in = inverse * (
        scaled
        - jnp.mean(scaled, -1, keepdims=True)
        - normed * jnp.mean(scaled * normed, -1, keepdims=True)
    )
    return (grad_in, grad_gain, grad_shift)


def attention_scores(query_rows, key_rows, key_valid):
    scores = jnp.einsum(
        "sqhd,skhd->shqk", query_rows, key_rows, preferred_element_type=jnp.float32
    ) * HEAD ** (-0.5)
    return jnp.where(key_valid[:, None, None, :], scores, -1000000000.0)


def forward(tokens, lengths, weights):
    (
        w_qkv,
        bias_query,
        bias_value,
        w_out,
        bias_out,
        gain_attn,
        shift_attn,
        w_in,
        bias_in,
        w_down,
        bias_down,
        gain_ffn,
        shift_ffn,
    ) = weights
    sentences, length, model_width = tokens.shape
    head_count = model_width // HEAD
    token_rows = tokens.reshape(sentences * length, model_width)
    bias_qkv = jnp.concatenate([bias_query, jnp.zeros_like(bias_query), bias_value]).astype(
        jnp.float32
    )
    packed = (jnp.dot(token_rows, w_qkv, preferred_element_type=jnp.float32) + bias_qkv).astype(
        jnp.bfloat16
    )
    packed = packed.reshape(sentences, length, 3, head_count, HEAD)
    query_rows = packed[:, :, 0]
    key_rows = packed[:, :, 1]
    value_rows = packed[:, :, 2]
    key_valid = jnp.arange(length)[None, :] < lengths[:, None]
    scores = attention_scores(query_rows, key_rows, key_valid)
    row_max = jnp.max(scores, -1, keepdims=True)
    log_total = row_max + jnp.log(jnp.sum(jnp.exp(scores - row_max), -1, keepdims=True))
    attn_probs = jnp.exp(scores - log_total)
    context = jnp.einsum(
        "shqk,skhd->sqhd",
        attn_probs.astype(jnp.bfloat16),
        value_rows,
        preferred_element_type=jnp.float32,
    )
    context = context.reshape(sentences * length, model_width).astype(jnp.bfloat16)
    attn_out = jnp.dot(context, w_out, preferred_element_type=jnp.float32) + bias_out.astype(
        jnp.float32
    )
    hidden, normed_attn, inverse_attn = norm_parts(
        token_rows.astype(jnp.float32) + attn_out,
        gain_attn.astype(jnp.float32),
        shift_attn.astype(jnp.float32),
    )
    hidden_low = hidden.astype(jnp.bfloat16)
    up_rows = jnp.dot(hidden_low, w_in, preferred_element_type=jnp.float32) + bias_in.astype(
        jnp.float32
    )
    active = jax.nn.gelu(up_rows, approximate=False).astype(jnp.bfloat16)
    ffn_out = jnp.dot(active, w_down, preferred_element_type=jnp.float32) + bias_down.astype(
        jnp.float32
    )
    output, normed_ffn, inverse_ffn = norm_parts(
        hidden + ffn_out, gain_ffn.astype(jnp.float32), shift_ffn.astype(jnp.float32)
    )
    valid_mask = key_valid.astype(jnp.float32)
    pooled = jnp.sum(
        output.reshape(sentences, length, model_width) * valid_mask[:, :, None], 1
    ) / lengths[:, None].astype(jnp.float32)
    kept = (
        key_valid,
        query_rows,
        key_rows,
        value_rows,
        log_total,
        context,
        normed_attn,
        inverse_attn,
        hidden_low,
        up_rows,
        active,
        normed_ffn,
        inverse_ffn,
    )
    return (pooled, kept)


def backward(tokens, lengths, pooled_grad, weights, kept):
    (
        w_qkv,
        bias_query,
        bias_value,
        w_out,
        bias_out,
        gain_attn,
        shift_attn,
        w_in,
        bias_in,
        w_down,
        bias_down,
        gain_ffn,
        shift_ffn,
    ) = weights
    (
        key_valid,
        query_rows,
        key_rows,
        value_rows,
        log_total,
        context,
        normed_attn,
        inverse_attn,
        hidden_low,
        up_rows,
        active,
        normed_ffn,
        inverse_ffn,
    ) = kept
    sentences, length, model_width = tokens.shape
    head_count = model_width // HEAD
    token_rows = tokens.reshape(sentences * length, model_width)
    valid_mask = key_valid.astype(jnp.float32)
    per_sentence = pooled_grad / lengths[:, None].astype(jnp.float32)
    grad_output = (valid_mask[:, :, None] * per_sentence[:, None, :]).reshape(
        sentences * length, model_width
    )
    grad_res_ffn, grad_gain_ffn, grad_shift_ffn = plain_norm_back(
        grad_output, normed_ffn, inverse_ffn, gain_ffn.astype(jnp.float32)
    )
    grad_ffn_low = grad_res_ffn.astype(jnp.bfloat16)
    grad_bias_down = jnp.sum(grad_ffn_low.astype(jnp.float32), 0)
    grad_w_down = jnp.einsum("tf,td->fd", active, grad_ffn_low, preferred_element_type=jnp.float32)
    grad_active = jnp.einsum("td,fd->tf", grad_ffn_low, w_down, preferred_element_type=jnp.float32)
    gelu_value, gelu_pull = jax.vjp(partial(jax.nn.gelu, approximate=False), up_rows)
    grad_up = gelu_pull(grad_active)[0].astype(jnp.bfloat16)
    grad_bias_in = jnp.sum(grad_up.astype(jnp.float32), 0)
    grad_w_in = jnp.einsum("td,tf->df", hidden_low, grad_up, preferred_element_type=jnp.float32)
    grad_hidden = (
        jnp.einsum("tf,df->td", grad_up, w_in, preferred_element_type=jnp.float32) + grad_res_ffn
    )
    grad_res_attn, grad_gain_attn, grad_shift_attn = plain_norm_back(
        grad_hidden, normed_attn, inverse_attn, gain_attn.astype(jnp.float32)
    )
    grad_attn_low = grad_res_attn.astype(jnp.bfloat16)
    grad_bias_out = jnp.sum(grad_attn_low.astype(jnp.float32), 0)
    grad_w_out = jnp.einsum("tc,td->cd", context, grad_attn_low, preferred_element_type=jnp.float32)
    grad_context = jnp.einsum("td,cd->tc", grad_attn_low, w_out, preferred_element_type=jnp.float32)
    grad_context = grad_context.astype(jnp.bfloat16).reshape(sentences, length, head_count, HEAD)
    scores = attention_scores(query_rows, key_rows, key_valid)
    attn_probs = jnp.exp(scores - log_total)
    grad_probs = jnp.einsum(
        "sqhd,skhd->shqk", grad_context, value_rows, preferred_element_type=jnp.float32
    )
    grad_values = jnp.einsum(
        "shqk,sqhd->skhd",
        attn_probs.astype(jnp.bfloat16),
        grad_context,
        preferred_element_type=jnp.float32,
    )
    grad_scores = (
        attn_probs * (grad_probs - jnp.sum(grad_probs * attn_probs, -1, keepdims=True))
    ).astype(jnp.bfloat16)
    grad_queries = jnp.einsum(
        "shqk,skhd->sqhd", grad_scores, key_rows, preferred_element_type=jnp.float32
    ) * HEAD ** (-0.5)
    grad_keys = jnp.einsum(
        "shqk,sqhd->skhd", grad_scores, query_rows, preferred_element_type=jnp.float32
    ) * HEAD ** (-0.5)
    grad_qkv = jnp.stack([grad_queries, grad_keys, grad_values], 2)
    grad_qkv = grad_qkv.reshape(sentences * length, 3 * model_width).astype(jnp.bfloat16)
    qkv_sums = jnp.sum(grad_qkv.astype(jnp.float32), 0)
    grad_bias_query = qkv_sums[:model_width]
    grad_bias_value = qkv_sums[2 * model_width :]
    grad_w_qkv = jnp.einsum("td,tc->dc", token_rows, grad_qkv, preferred_element_type=jnp.float32)
    grad_tokens = (
        jnp.einsum("tc,dc->td", grad_qkv, w_qkv, preferred_element_type=jnp.float32) + grad_res_attn
    )
    grad_tokens = grad_tokens.reshape(sentences, length, model_width)
    grad_terms = (
        grad_w_qkv,
        grad_bias_query,
        grad_bias_value,
        grad_w_out,
        grad_bias_out,
        grad_gain_attn,
        grad_shift_attn,
        grad_w_in,
        grad_bias_in,
        grad_w_down,
        grad_bias_down,
        grad_gain_ffn,
        grad_shift_ffn,
    )
    return (grad_terms, grad_tokens)


def on_device(
    tokens,
    lengths,
    pooled_grad,
    w_qkv,
    bias_query,
    bias_value,
    w_out,
    bias_out,
    gain_attn,
    shift_attn,
    w_in,
    bias_in,
    w_down,
    bias_down,
    gain_ffn,
    shift_ffn,
):
    weights = (
        lax.all_gather(w_qkv, "fsdp", axis=0, tiled=True),
        lax.all_gather(bias_query, "fsdp", axis=0, tiled=True),
        lax.all_gather(bias_value, "fsdp", axis=0, tiled=True),
        lax.all_gather(w_out, "fsdp", axis=0, tiled=True),
        lax.all_gather(bias_out, "fsdp", axis=0, tiled=True),
        lax.all_gather(gain_attn, "fsdp", axis=0, tiled=True),
        lax.all_gather(shift_attn, "fsdp", axis=0, tiled=True),
        lax.all_gather(w_in, "fsdp", axis=0, tiled=True),
        lax.all_gather(bias_in, "fsdp", axis=0, tiled=True),
        lax.all_gather(w_down, "fsdp", axis=0, tiled=True),
        lax.all_gather(bias_down, "fsdp", axis=0, tiled=True),
        lax.all_gather(gain_ffn, "fsdp", axis=0, tiled=True),
        lax.all_gather(shift_ffn, "fsdp", axis=0, tiled=True),
    )
    pooled, kept = forward(tokens, lengths, weights)
    grad_terms, grad_tokens = backward(tokens, lengths, pooled_grad, weights, kept)
    (
        grad_w_qkv,
        grad_bias_query,
        grad_bias_value,
        grad_w_out,
        grad_bias_out,
        grad_gain_attn,
        grad_shift_attn,
        grad_w_in,
        grad_bias_in,
        grad_w_down,
        grad_bias_down,
        grad_gain_ffn,
        grad_shift_ffn,
    ) = grad_terms
    shares = (
        lax.psum_scatter(grad_w_qkv, "fsdp", scatter_dimension=0, tiled=True),
        lax.psum_scatter(grad_bias_query, "fsdp", scatter_dimension=0, tiled=True),
        lax.psum_scatter(grad_bias_value, "fsdp", scatter_dimension=0, tiled=True),
        lax.psum_scatter(grad_w_out, "fsdp", scatter_dimension=0, tiled=True),
        lax.psum_scatter(grad_bias_out, "fsdp", scatter_dimension=0, tiled=True),
        lax.psum_scatter(grad_gain_attn, "fsdp", scatter_dimension=0, tiled=True),
        lax.psum_scatter(grad_shift_attn, "fsdp", scatter_dimension=0, tiled=True),
        lax.psum_scatter(grad_w_in, "fsdp", scatter_dimension=0, tiled=True),
        lax.psum_scatter(grad_bias_in, "fsdp", scatter_dimension=0, tiled=True),
        lax.psum_scatter(grad_w_down, "fsdp", scatter_dimension=0, tiled=True),
        lax.psum_scatter(grad_bias_down, "fsdp", scatter_dimension=0, tiled=True),
        lax.psum_scatter(grad_gain_ffn, "fsdp", scatter_dimension=0, tiled=True),
        lax.psum_scatter(grad_shift_ffn, "fsdp", scatter_dimension=0, tiled=True),
    )
    (
        share_w_qkv,
        share_bias_query,
        share_bias_value,
        share_w_out,
        share_bias_out,
        share_gain_attn,
        share_shift_attn,
        share_w_in,
        share_bias_in,
        share_w_down,
        share_bias_down,
        share_gain_ffn,
        share_shift_ffn,
    ) = shares
    totals = (
        lax.psum(share_w_qkv.astype(jnp.bfloat16), "dp").astype(jnp.float32),
        lax.psum(share_bias_query.astype(jnp.bfloat16), "dp").astype(jnp.float32),
        lax.psum(share_bias_value.astype(jnp.bfloat16), "dp").astype(jnp.float32),
        lax.psum(share_w_out.astype(jnp.bfloat16), "dp").astype(jnp.float32),
        lax.psum(share_bias_out.astype(jnp.bfloat16), "dp").astype(jnp.float32),
        lax.psum(share_gain_attn.astype(jnp.bfloat16), "dp").astype(jnp.float32),
        lax.psum(share_shift_attn.astype(jnp.bfloat16), "dp").astype(jnp.float32),
        lax.psum(share_w_in.astype(jnp.bfloat16), "dp").astype(jnp.float32),
        lax.psum(share_bias_in.astype(jnp.bfloat16), "dp").astype(jnp.float32),
        lax.psum(share_w_down.astype(jnp.bfloat16), "dp").astype(jnp.float32),
        lax.psum(share_bias_down.astype(jnp.bfloat16), "dp").astype(jnp.float32),
        lax.psum(share_gain_ffn.astype(jnp.bfloat16), "dp").astype(jnp.float32),
        lax.psum(share_shift_ffn.astype(jnp.bfloat16), "dp").astype(jnp.float32),
    )
    return (
        pooled,
        grad_tokens,
        totals[0],
        totals[1],
        totals[2],
        totals[3],
        totals[4],
        totals[5],
        totals[6],
        totals[7],
        totals[8],
        totals[9],
        totals[10],
        totals[11],
        totals[12],
    )


def swap(array, axis, bits):
    pairs = [(i, i ^ bits) for i in range(lax.axis_size(axis))]
    return lax.ppermute(array, axis, pairs)


def gather(piece, split_x):
    near = jnp.stack([piece] + [swap(piece, "fsdp", 2 * k) for k in range(1, 4)])
    far = swap(near, "fsdp", 1)
    mine = [near, far]
    if split_x:
        mine += [swap(near, "dp", 2), swap(far, "dp", 2)]
    return mine + [swap(m, "dp", 1) for m in mine]


def add(*terms):
    total = terms[0].astype(F32)
    for term in terms[1:]:
        total = total + term.astype(F32)
    return total.astype(BF)


def scatter(send, keep, split_x):
    total = add(keep, swap(send, "dp", 1))
    if split_x:
        total = add(total[0], swap(total[1], "dp", 2))
    else:
        total = total[0]
    total = add(total[0], swap(total[1], "fsdp", 1))
    total = add(total[0], *[swap(total[k], "fsdp", 2 * k) for k in range(1, 4)])
    if split_x:
        own = [total, swap(total, "dp", 2)]
    else:
        own = [add(total, swap(total, "dp", 2))]
    return own, [swap(part, "dp", 1) for part in own]


def in_order(own, other, bit, axis):
    first = jnp.where(bit == 0, own, other)
    second = jnp.where(bit == 0, other, own)
    return jnp.concatenate([first, second], axis=axis)


def on_device_split(
    tokens,
    lengths,
    pooled_grad,
    w_qkv,
    bias_query,
    bias_value,
    w_out,
    bias_out,
    gain_attn,
    shift_attn,
    w_in,
    bias_in,
    w_down,
    bias_down,
    gain_ffn,
    shift_ffn,
):
    sentences, length, width = tokens.shape
    rows = sentences * length
    wide = w_in.shape[1]
    part = width // 8
    dp, fsdp = lax.axis_index("dp"), lax.axis_index("fsdp")
    x, c = dp // 2, dp % 2
    ids = jnp.stack([fsdp // 2, fsdp % 2, x, c]).astype(jnp.int32)
    token_rows = tokens.reshape(rows, width)

    vectors = jnp.stack(
        [bias_query, bias_value, bias_out, gain_attn, shift_attn, bias_down, gain_ffn, shift_ffn]
    )
    vectors = jnp.concatenate([vectors, bias_in.reshape(wide // width, part)], 0)
    vectors = jnp.pad(vectors.T, ((0, 0), (0, 128 - vectors.shape[0])))
    first = jnp.concatenate([w_qkv, vectors], 1)
    second = jnp.concatenate([w_out, w_in], 1)
    half = part // 2
    first = lax.dynamic_slice(first, (c * half, 0), (half, first.shape[1]))
    span = second.shape[1] // 2
    second = lax.dynamic_slice(second, (c * half, x * span), (half, span))
    third = lax.dynamic_slice(w_down, (c * (w_down.shape[0] // 2), 0), (w_down.shape[0] // 2, width))
    first, second, third = gather(first, False), gather(second, True), gather(third, False)

    qkv, context, lse, vec = attend_forward(token_rows, lengths, ids, first, sentences, length)
    ratio = wide // width
    bias_up = vec[8 : 8 + ratio].reshape(ratio, 8, part).transpose(1, 0, 2).reshape(1, wide)
    normed, inverse, low, active, slope = up_forward(
        context, token_rows, vec, bias_up, ids, second, length
    )
    pooled, gres, glow, vg_ffn, send3, keep3 = down_forward(
        active, normed, vec, lengths, pooled_grad, ids, third, sentences, length
    )
    down = scatter(send3, keep3, False)
    gup, gbias_in, send2, keep2 = up_backward(glow, slope, low, ids, third)
    up = scatter(send2, keep2, True)
    gattn, gattn_low, gctx, vg_attn = hidden_backward(
        gup, gres, normed, inverse, vec, ids, second, length
    )
    vgrads = jnp.concatenate(
        [
            jnp.zeros((2, width), F32),
            vg_attn[2:3],
            vg_attn[0:2],
            vg_ffn[2:3],
            vg_ffn[0:2],
            gbias_in.reshape(8, ratio, part).transpose(1, 0, 2).reshape(ratio, width),
            jnp.zeros((8 - ratio, width), F32),
        ],
        0,
    )
    gqkv, send1, keep1 = attend_backward(
        qkv, gctx, lse, token_rows, context, gattn_low, vgrads, lengths, ids, sentences, length
    )
    rest = scatter(send1, keep1, True)
    gtokens = tokens_backward(gqkv, gattn, ids, first).reshape(sentences, length, width)

    def joined(parts, split_x):
        own, other = parts
        if split_x:
            own, other = in_order(*own, x, 1), in_order(*other, x, 1)
        else:
            own, other = own[0], other[0]
        return in_order(own, other, c, 0).astype(F32)

    g_down = joined(down, False).T
    g_in = joined(up, True)
    g_rest = joined(rest, True)
    g_vec = g_rest[:, 4 * width : 4 * width + 8 + ratio].T
    return (
        pooled,
        gtokens,
        g_rest[:, : 3 * width],
        g_vec[0],
        g_vec[1],
        g_rest[:, 3 * width : 4 * width],
        g_vec[2],
        g_vec[3],
        g_vec[4],
        g_in,
        g_vec[8:].reshape(wide // 8),
        g_down,
        g_vec[5],
        g_vec[6],
        g_vec[7],
    )


def solution(mesh):
    placed = (
        P(("dp", "fsdp"), None, None),
        P(("dp", "fsdp")),
        P(("dp", "fsdp"), None),
        P("fsdp", None),
        P("fsdp"),
        P("fsdp"),
        P("fsdp", None),
        P("fsdp"),
        P("fsdp"),
        P("fsdp"),
        P("fsdp", None),
        P("fsdp"),
        P("fsdp", None),
        P("fsdp"),
        P("fsdp"),
        P("fsdp"),
    )
    body = on_device_split if mesh.shape["fsdp"] == 8 and mesh.shape["dp"] == 4 else on_device
    return jax.shard_map(
        body,
        mesh=mesh,
        in_specs=placed,
        out_specs=(
            P(("dp", "fsdp"), None),
            P(("dp", "fsdp"), None, None),
            P("fsdp", None),
            P("fsdp"),
            P("fsdp"),
            P("fsdp", None),
            P("fsdp"),
            P("fsdp"),
            P("fsdp"),
            P("fsdp", None),
            P("fsdp"),
            P("fsdp", None),
            P("fsdp"),
            P("fsdp"),
            P("fsdp"),
        ),
        check_vma=False,
    )
```

```python
from functools import partial

import jax
import jax.numpy as jnp
from jax import lax
from jax.experimental import pallas as pl
from jax.experimental.pallas import tpu as pltpu
from jax.sharding import PartitionSpec as P

norm_eps = 1e-06

HEAD = 64
NORM_EPS = 1e-06
BF = jnp.bfloat16
F32 = jnp.float32
VMEM_LIMIT = 60 * 1024 * 1024


def dot(a, b):
    return lax.dot_general(a, b, (((1,), (0,)), ((), ())), preferred_element_type=F32)


def dot_nt(a, b):
    return lax.dot_general(a, b, (((1,), (1,)), ((), ())), preferred_element_type=F32)


def dot_tn(a, b):
    return lax.dot_general(a, b, (((0,), (0,)), ((), ())), preferred_element_type=F32)


def aligned(value, step):
    return pl.multiple_of(value, step)


class Place:
    def __init__(self, ids_ref):
        self.z, self.y, self.x, self.c = ids_ref[0], ids_ref[1], ids_ref[2], ids_ref[3]

    def shard(self, k, yy):
        return lax.bitwise_xor(self.z, k) * 2 + lax.bitwise_xor(self.y, yy)


def piece_copies(place, bufs, dst, sems, shard_rows, split_x):
    half = shard_rows // 2
    copies = []
    at = 0
    for cc in range(2):
        core = lax.bitwise_xor(place.c, cc)
        for xx in range(2 if split_x else 1):
            for yy in range(2):
                buf = bufs[at]
                at += 1
                width = buf.shape[-1]
                for k in range(4):
                    row = aligned(place.shard(k, yy) * shard_rows + core * half, 16)
                    if split_x:
                        col = aligned(lax.bitwise_xor(place.x, xx) * width, 128)
                        target = dst.at[pl.ds(row, half), pl.ds(col, width)]
                    else:
                        target = dst.at[pl.ds(row, half), :]
                    copies.append(
                        pltpu.make_async_copy(buf.at[k], target, sems.at[len(copies)])
                    )
    return copies


def call(body, name, ins, outs, scratch, flops, transcendentals=0):
    spaces = {
        "s": pl.BlockSpec(memory_space=pltpu.SMEM),
        "v": pl.BlockSpec(memory_space=pltpu.VMEM),
        "a": pl.BlockSpec(memory_space=pl.ANY),
    }
    moved = sum(a.size * a.dtype.itemsize for a, _ in ins) + sum(
        o.size * o.dtype.itemsize for o in outs
    )
    return pl.pallas_call(
        body,
        name=name,
        out_shape=tuple(outs),
        in_specs=[spaces[s] for _, s in ins],
        out_specs=tuple(spaces["v"] for _ in outs),
        scratch_shapes=scratch,
        compiler_params=pltpu.CompilerParams(vmem_limit_bytes=VMEM_LIMIT),
        cost_estimate=pl.CostEstimate(flops=1, transcendentals=0, bytes_accessed=1),
    )(*[a for a, _ in ins])


def struct(shape, dtype):
    return jax.ShapeDtypeStruct(shape, dtype)


def two_heads(block):
    low = lax.broadcasted_iota(jnp.int32, block.shape, 1) < HEAD
    zero = jnp.zeros_like(block)
    return jnp.concatenate([jnp.where(low, block, zero), jnp.where(low, zero, block)], axis=0)


def one_of_two(stacked):
    rows = stacked.shape[0] // 2
    low = lax.broadcasted_iota(jnp.int32, (rows, stacked.shape[1]), 1) < HEAD
    return jnp.where(low, stacked[:rows], stacked[rows:])


def masked_scores(query, keys2, count, length):
    scores = dot_nt(query, keys2)
    slot = lax.broadcasted_iota(jnp.int32, scores.shape, 1)
    slot = jnp.where(slot >= length, slot - length, slot)
    return jnp.where(slot < count, scores, -1000000000.0)


def halves(stat_a, stat_b, length):
    rows = stat_a.shape[0]
    return jnp.concatenate(
        [jnp.broadcast_to(stat_a, (rows, length)), jnp.broadcast_to(stat_b, (rows, length))], axis=1
    )


def attend_forward(tokens, counts, ids, bufs, sentences, length):
    rows, width = tokens.shape
    pairs = width // 128
    group = 256

    def body(ids_ref, counts_ref, x_ref, b0, b1, b2, b3, qkv_ref, ctx_ref, lse_ref, vec_ref, w_ref, sems):
        place = Place(ids_ref)
        copies = piece_copies(place, (b0, b1, b2, b3), w_ref, sems, width // 8, False)
        for copy in copies:
            copy.start()
        for copy in copies:
            copy.wait()
        vec_ref[...] = w_ref[:, 3 * width :].astype(F32).T[: vec_ref.shape[0]]
        x = x_ref[...]
        for part in range(3):
            for g in range(width // group):
                col = part * width + g * group
                y = dot(x, w_ref[:, col : col + group])
                if part != 1:
                    bias = vec_ref[part // 2 : part // 2 + 1, g * group : (g + 1) * group]
                    y = y + bias
                qkv_ref[:, col : col + group] = y.astype(BF)

        def sentence(s, carry):
            row = aligned(s * length, length)
            count = counts_ref[s]
            lane = lax.broadcasted_iota(jnp.int32, (length, 128), 1)
            lse_all = jnp.zeros((length, 128), F32)
            for p in range(pairs):
                here = pl.ds(row, length)
                query = qkv_ref[here, p * 128 : (p + 1) * 128] * jnp.asarray(HEAD**-0.5, BF)
                keys2 = two_heads(qkv_ref[here, width + p * 128 : width + (p + 1) * 128])
                values2 = two_heads(qkv_ref[here, 2 * width + p * 128 : 2 * width + (p + 1) * 128])
                scores = masked_scores(query, keys2, count, length)
                a, b = scores[:, :length], scores[:, length:]
                max_a = jnp.max(a, -1, keepdims=True)
                max_b = jnp.max(b, -1, keepdims=True)
                e_a, e_b = jnp.exp(a - max_a), jnp.exp(b - max_b)
                sum_a = jnp.sum(e_a, -1, keepdims=True)
                sum_b = jnp.sum(e_b, -1, keepdims=True)
                lse_all = jnp.where(lane == 2 * p, max_a + jnp.log(sum_a), lse_all)
                lse_all = jnp.where(lane == 2 * p + 1, max_b + jnp.log(sum_b), lse_all)
                probs = jnp.concatenate([e_a * (1.0 / sum_a), e_b * (1.0 / sum_b)], axis=1).astype(BF)
                ctx_ref[here, p * 128 : (p + 1) * 128] = dot(probs, values2).astype(BF)
            lse_ref[pl.ds(row, length), :] = lse_all
            return carry

        lax.fori_loop(0, sentences, sentence, 0)

    return call(
        body,
        "qkv_attention",
        [(ids, "s"), (counts, "s"), (tokens, "v")] + [(b, "a") for b in bufs],
        [
            struct((rows, 3 * width), BF),
            struct((rows, width), BF),
            struct((rows, 128), F32),
            struct((16, width), F32),
        ],
        [pltpu.VMEM((width, 3 * width + 128), BF), pltpu.SemaphoreType.DMA((16,))],
        2 * rows * width * 3 * width + 8 * rows * length * width,
        rows * length * width // HEAD,
    )


def layer_norm(v):
    centred = v - jnp.mean(v, -1, keepdims=True)
    inverse = lax.rsqrt(jnp.mean(centred * centred, -1, keepdims=True) + NORM_EPS)
    return centred * inverse, inverse


def norm_back(grad, normed, inverse, gain):
    scaled = grad * gain
    return inverse * (
        scaled
        - jnp.mean(scaled, -1, keepdims=True)
        - normed * jnp.mean(scaled * normed, -1, keepdims=True)
    )


def row(vec_ref, at):
    return vec_ref[at : at + 1, :]


def up_forward(context, tokens, vec, bias_in, ids, bufs, length):
    rows, width = tokens.shape
    wide = bias_in.shape[1]
    group = 256

    def body(ids_ref, ctx_ref, x_ref, vec_ref, bin_ref, *rest):
        bufs_ref = rest[: len(bufs)]
        n_ref, inv_ref, low_ref, act_ref, slope_ref, w_ref, sems = rest[len(bufs) :]
        place = Place(ids_ref)
        copies = piece_copies(place, bufs_ref, w_ref, sems, width // 8, True)
        for copy in copies:
            copy.start()
        for copy in copies:
            copy.wait()
        n_ref[...] = dot(ctx_ref[...], w_ref[:, :width])

        def norm_rows(s, carry):
            here = pl.ds(aligned(s * length, length), length)
            v = x_ref[here, :].astype(F32) + (n_ref[here, :] + row(vec_ref, 2))
            normed, inverse = layer_norm(v)
            n_ref[here, :] = normed
            inv_ref[here, :] = jnp.broadcast_to(inverse, (length, 128))
            low_ref[here, :] = (normed * row(vec_ref, 3) + row(vec_ref, 4)).astype(BF)
            return carry

        lax.fori_loop(0, rows // length, norm_rows, 0)

        def columns(g, carry):
            col = aligned(g * group, group)
            u = dot(low_ref[...], w_ref[:, pl.ds(width + col, group)]) + bin_ref[:, pl.ds(col, group)]
            cdf = 0.5 * (1.0 + lax.erf(u * (0.5**0.5)))
            pdf = jnp.exp(-0.5 * u * u) * 0.3989422804014327
            act_ref[:, pl.ds(col, group)] = (u * cdf).astype(BF)
            slope_ref[:, pl.ds(col, group)] = (cdf + u * pdf).astype(BF)
            return carry

        lax.fori_loop(0, wide // group, columns, 0)

    return call(
        body,
        "out_norm_up",
        [(ids, "s"), (context, "v"), (tokens, "v"), (vec, "v"), (bias_in, "v")]
        + [(b, "a") for b in bufs],
        [
            struct((rows, width), F32),
            struct((rows, 128), F32),
            struct((rows, width), BF),
            struct((rows, wide), BF),
            struct((rows, wide), BF),
        ],
        [pltpu.VMEM((width, width + wide), BF), pltpu.SemaphoreType.DMA((32,))],
        2 * rows * width * (width + wide),
        2 * rows * wide,
    )


def grid_call(body, name, grid, scalars, ins, outs, scratch, flops, transcendentals=0):
    def spec(block, index):
        if block is None:
            return pl.BlockSpec(memory_space=pl.ANY)
        return pl.BlockSpec(block, index)

    moved = sum(a.size * a.dtype.itemsize for a, _, _ in ins) + sum(
        o.size * o.dtype.itemsize for o, _, _ in outs
    )
    return pl.pallas_call(
        body,
        name=name,
        out_shape=tuple(o for o, _, _ in outs),
        grid_spec=pltpu.PrefetchScalarGridSpec(
            num_scalar_prefetch=len(scalars),
            grid=grid,
            in_specs=[spec(b, i) for _, b, i in ins],
            out_specs=tuple(spec(b, i) for _, b, i in outs),
            scratch_shapes=scratch,
        ),
        compiler_params=pltpu.CompilerParams(
            vmem_limit_bytes=VMEM_LIMIT, dimension_semantics=("arbitrary",) * len(grid)
        ),
        cost_estimate=pl.CostEstimate(flops=1, transcendentals=0, bytes_accessed=1),
    )(*scalars, *[a for a, _, _ in ins])


def whole(array):
    return (array, array.shape, lambda *_: (0,) * array.ndim)


def left(array):
    return (array, None, None)


def relative(ids, step):
    return lax.bitwise_xor(ids[0] * 2 + ids[1], step)


def put_relative(place, source, dst):
    half = source.shape[0] // 16
    for cc in range(2):
        core = lax.bitwise_xor(place.c, cc)
        for yy in range(2):
            for k in range(4):
                at = ((cc * 2 + yy) * 4 + k) * half
                here = aligned(place.shard(k, yy) * 2 * half + core * half, 16)
                dst[at : at + half, :] = source[pl.ds(here, half), :]


def natural_copies(place, bufs, dst, sems):
    half = bufs[0].shape[1]
    copies = []
    for cc in range(2):
        for yy in range(2):
            for k in range(4):
                at = place.shard(k, yy) * 2 * half + lax.bitwise_xor(place.c, cc) * half
                copies.append(
                    pltpu.make_async_copy(
                        bufs[2 * cc + yy].at[k], dst.at[pl.ds(aligned(at, 16), half), :], sems.at[len(copies)]
                    )
                )
    return copies


def down_and_back(active, slope, normed, vec, counts, pooled_grad, ids, bufs, sentences, length):
    rows, wide = active.shape
    width = normed.shape[1]
    shard = wide // 8
    half = width // 2
    group = 256

    def body(ids_ref, counts_ref, act_hbm, slope_ref, vec_ref, pg_ref, n_hbm, b0, b1, b2, b3, pooled_ref, vg_ref, send_ref, keep_ref, gup_ref, gbias_ref, gres_hbm, w_ref, acc_ref, n_ref, glow_ref, act_ref, t_ref, sems, more):
        step = pl.program_id(0)
        place = Place(ids_ref)
        bufs_ref = (b0, b1, b2, b3)
        load = pltpu.make_async_copy(n_hbm, n_ref, more.at[0])
        load_active = pltpu.make_async_copy(act_hbm, act_ref, more.at[1 + sentences])

        def columns_of(phase):
            return pl.ds(aligned(relative(ids_ref, step - phase) * shard, 128), shard)

        def out(s):
            here = pl.ds(aligned(s * length, length), length)
            return pltpu.make_async_copy(acc_ref.at[here, :], gres_hbm.at[here, :], more.at[1 + s])

        @pl.when(step == 0)
        def _():
            copies = natural_copies(place, bufs_ref, w_ref, sems)
            load_active.start()
            for copy in copies:
                copy.start()
            load.start()
            vg_ref[...] = jnp.zeros_like(vg_ref)
            for copy in copies:
                copy.wait()
            load_active.wait()
            for g in range(width // group):
                cols = slice(g * group, (g + 1) * group)
                acc_ref[:, cols] = dot(act_ref[...], w_ref[:, cols])
            load.wait()

            def norm_rows(s, carry):
                here = pl.ds(aligned(s * length, length), length)
                hidden = n_ref[here, :] * row(vec_ref, 3) + row(vec_ref, 4)
                n2, inverse = layer_norm(hidden + (acc_ref[here, :] + row(vec_ref, 5)))
                valid = lax.broadcasted_iota(jnp.int32, (length, width), 0) < counts_ref[s]
                count = counts_ref[s].astype(F32)
                out_rows = jnp.where(valid, n2 * row(vec_ref, 6) + row(vec_ref, 7), 0.0)
                pooled_ref[pl.ds(s, 1), :] = jnp.sum(out_rows, 0, keepdims=True) / count
                grad = jnp.where(valid, pg_ref[pl.ds(s, 1), :] / count, 0.0)
                vg_ref[0:1, :] += jnp.sum(grad * n2, 0, keepdims=True)
                vg_ref[1:2, :] += jnp.sum(grad, 0, keepdims=True)
                gres = norm_back(grad, n2, inverse, row(vec_ref, 6))
                acc_ref[here, :] = gres
                glow = gres.astype(BF)
                glow_ref[here, :] = glow
                vg_ref[2:3, :] += jnp.sum(glow.astype(F32), 0, keepdims=True)
                out(s).start()
                return carry

            lax.fori_loop(0, sentences, norm_rows, 0)
            t_ref[...] = glow_ref[...].T

        @pl.when(jnp.logical_and(step >= 1, step < 9))
        def _():
            for cc, out_ref in ((0, keep_ref), (1, send_ref)):
                core = lax.bitwise_xor(place.c, cc)
                out_ref[0, 0, 0] = dot(
                    t_ref[pl.ds(aligned(core * half, half), half), :], act_ref[:, columns_of(1)]
                ).astype(BF)

        @pl.when(step >= 9)
        def _():
            gact = dot_nt(glow_ref[...], w_ref[columns_of(9), :])
            gup = (gact * slope_ref[...].astype(F32)).astype(BF)
            gup_ref[...] = gup
            gbias_ref[...] = jnp.sum(gup.astype(F32), 0, keepdims=True)

        @pl.when(step == 16)
        def _():
            for s in range(sentences):
                out(s).wait()

    def at(step, phase):
        return jnp.clip(step - phase, 0, 7)

    def grad_block(step, ids, counts):
        r = at(step, 1)
        return (0, lax.rem(r, 2), lax.div(r, 2), 0, 0)

    def columns(phase):
        return lambda step, ids, counts: (0, relative(ids, at(step, phase)))

    grads = (struct((1, 2, 4, half, shard), BF), (1, 1, 1, half, shard), grad_block)
    return grid_call(
        body,
        "down_and_back",
        (17,),
        (ids, counts),
        [
            left(active),
            (slope, (rows, shard), columns(9)),
            whole(vec),
            whole(pooled_grad),
            left(normed),
        ]
        + [left(b) for b in bufs],
        [
            whole(struct((sentences, width), F32)),
            whole(struct((8, width), F32)),
            grads,
            grads,
            (struct((rows, wide), BF), (rows, shard), columns(9)),
            (struct((1, wide), F32), (1, shard), columns(9)),
            left(struct((rows, width), F32)),
        ],
        [
            pltpu.VMEM((wide, width), BF),
            pltpu.VMEM((rows, width), F32),
            pltpu.VMEM((rows, width), F32),
            pltpu.VMEM((rows, width), BF),
            pltpu.VMEM((rows, wide), BF),
            pltpu.VMEM((width, rows), BF),
            pltpu.SemaphoreType.DMA((16,)),
            pltpu.SemaphoreType.DMA((2 + sentences,)),
        ],
        6 * rows * width * wide,
    )


def up_and_back(low, gup, gres, normed, inverse, vec, ids, bufs, length):
    rows, wide = gup.shape
    width = gres.shape[1]
    sentences = rows // length
    group, block = 256, 512
    steps = wide // block
    per = steps // 2

    def body(ids_ref, low_ref, gup_ref, vec_ref, gres_hbm, n_hbm, inv_hbm, *rest):
        bufs_ref = rest[: len(bufs)]
        send_ref, keep_ref, gctx_ref, vg_ref, gattn_hbm, glow_hbm, w_ref, acc_ref, gres_ref, n_ref, inv_ref, glow_ref, t_ref, p_ref, gup_all, sems, more = rest[len(bufs) :]
        step = pl.program_id(0)
        place = Place(ids_ref)
        loads = [
            pltpu.make_async_copy(a, b, more.at[i])
            for i, (a, b) in enumerate(((gres_hbm, gres_ref), (n_hbm, n_ref), (inv_hbm, inv_ref)))
        ]
        copies = piece_copies(place, bufs_ref, w_ref, sems, width // 8, True)

        @pl.when(step == 0)
        def _():
            for copy in copies:
                copy.start()
            for load in loads:
                load.start()
            t_ref[...] = low_ref[...].T
            put_relative(place, t_ref, p_ref)

        put_halves(dot(p_ref[...], gup_ref[...]).astype(BF), send_ref, keep_ref)

        gup_all[:, pl.ds(aligned(step * block, 128), block)] = gup_ref[...]

        @pl.when(step == steps - 1)
        def _():
            for copy in copies:
                copy.wait()
            for g in range(width // group):
                cols = slice(g * group, (g + 1) * group)
                acc_ref[:, cols] = dot_nt(gup_all[...], w_ref[cols, width:])
            for load in loads:
                load.wait()
            vg_ref[...] = jnp.zeros_like(vg_ref)

            def outs(s):
                here = pl.ds(aligned(s * length, length), length)
                return (
                    pltpu.make_async_copy(acc_ref.at[here, :], gattn_hbm.at[here, :], more.at[3 + s]),
                    pltpu.make_async_copy(
                        glow_ref.at[here, :], glow_hbm.at[here, :], more.at[3 + sentences + s]
                    ),
                )

            def norm_rows(s, carry):
                here = pl.ds(aligned(s * length, length), length)
                grad = acc_ref[here, :] + gres_ref[here, :]
                normed = n_ref[here, :]
                vg_ref[0:1, :] += jnp.sum(grad * normed, 0, keepdims=True)
                vg_ref[1:2, :] += jnp.sum(grad, 0, keepdims=True)
                gattn = norm_back(grad, normed, inv_ref[here, 0:1], row(vec_ref, 3))
                acc_ref[here, :] = gattn
                glow = gattn.astype(BF)
                glow_ref[here, :] = glow
                vg_ref[2:3, :] += jnp.sum(glow.astype(F32), 0, keepdims=True)
                for copy in outs(s):
                    copy.start()
                return carry

            lax.fori_loop(0, sentences, norm_rows, 0)
            for g in range(width // group):
                gctx_ref[:, g * group : (g + 1) * group] = dot_nt(
                    glow_ref[...], w_ref[g * group : (g + 1) * group, :width]
                ).astype(BF)
            for s in range(sentences):
                for copy in outs(s):
                    copy.wait()

    blocks = weight_blocks(width, block, per)
    return grid_call(
        body,
        "up_and_back",
        (steps,),
        (ids,),
        [whole(low), (gup, (rows, block), lambda j, ids: (0, j)), whole(vec), left(gres), left(normed), left(inverse)]
        + [left(b) for b in bufs],
        [
            blocks,
            blocks,
            whole(struct((rows, width), BF)),
            whole(struct((8, width), F32)),
            left(struct((rows, width), F32)),
            left(struct((rows, width), BF)),
        ],
        [
            pltpu.VMEM((width, width + wide), BF),
            pltpu.VMEM((rows, width), F32),
            pltpu.VMEM((rows, width), F32),
            pltpu.VMEM((rows, width), F32),
            pltpu.VMEM((rows, 128), F32),
            pltpu.VMEM((rows, width), BF),
            pltpu.VMEM((width, rows), BF),
            pltpu.VMEM((width, rows), BF),
            pltpu.VMEM((rows, wide), BF),
            pltpu.SemaphoreType.DMA((32,)),
            pltpu.SemaphoreType.DMA((3 + 2 * sentences,)),
        ],
        2 * rows * width * (width + 2 * wide),
    )


def attend_backward(qkv, gctx, lse, counts, sentences, length, low, high, name):
    rows, width = gctx.shape
    span = (high - low) * 128
    twos = range(low // 2, high // 2)

    def body(counts_ref, *refs):
        parts = [refs[i * len(twos) : (i + 1) * len(twos)] for i in range(3)]
        gctx_ref, lse_ref, gqkv_ref, vs_ref = refs[3 * len(twos) :]
        s = pl.program_id(0)

        @pl.when(s == 0)
        def _():
            vs_ref[...] = jnp.zeros_like(vs_ref)

        count = counts_ref[s]
        for p in range(low, high):
            at = (p - low) * 128
            block, cols = (p - low) // 2, slice(p % 2 * 128, p % 2 * 128 + 128)
            query = parts[0][block][:, cols] * jnp.asarray(HEAD**-0.5, BF)
            keys2 = two_heads(parts[1][block][:, cols])
            values2 = two_heads(parts[2][block][:, cols])
            gout = gctx_ref[:, at : at + 128]
            scores = masked_scores(query, keys2, count, length)
            lse2 = halves(lse_ref[:, 2 * p : 2 * p + 1], lse_ref[:, 2 * p + 1 : 2 * p + 2], length)
            probs = jnp.exp(scores - lse2)
            gprobs = dot_nt(gout, values2)
            weighted = gprobs * probs
            sums = halves(
                jnp.sum(weighted[:, :length], -1, keepdims=True),
                jnp.sum(weighted[:, length:], -1, keepdims=True),
                length,
            )
            gscores = (probs * (gprobs - sums)).astype(BF)
            gq = (dot(gscores, keys2) * HEAD**-0.5).astype(BF)
            gk = one_of_two(dot_tn(gscores, query)).astype(BF)
            gv = one_of_two(dot_tn(probs.astype(BF), gout)).astype(BF)
            gqkv_ref[:, at : at + 128] = gq
            gqkv_ref[:, span + at : span + at + 128] = gk
            gqkv_ref[:, 2 * span + at : 2 * span + at + 128] = gv
            vs_ref[0:1, at : at + 128] += jnp.sum(gq.astype(F32), 0, keepdims=True)
            vs_ref[1:2, at : at + 128] += jnp.sum(gv.astype(F32), 0, keepdims=True)

    def by_rows(array):
        return (array, (length, array.shape[1]), lambda s, counts: (s, 0))

    return grid_call(
        body,
        name,
        (sentences,),
        (counts,),
        [
            (qkv, (length, 256), lambda s, counts, at=part * width // 256 + b: (s, at))
            for part in range(3)
            for b in twos
        ]
        + [(gctx, (length, span), lambda s, counts: (s, low * 128 // span)), by_rows(lse)],
        [by_rows(struct((rows, 3 * span), BF)), whole(struct((8, span), F32))],
        [],
        20 * rows * length * span,
    )


def weight_blocks(width, group, per):
    half = width // 16
    return (
        struct((2, 2, 4, half, per * group), BF),
        (1, 2, 4, half, group),
        lambda j, ids: (lax.bitwise_xor(ids[2], lax.div(j, per)), 0, 0, 0, lax.rem(j, per)),
    )


def put_halves(dw, send_ref, keep_ref):
    width, group = dw.shape
    shape = (2, 4, width // 16, group)
    keep_ref[0] = dw[: width // 2].reshape(shape)
    send_ref[0] = dw[width // 2 :].reshape(shape)


def attend_weight(gqkv, tokens, context, glow, ids):
    rows, width = tokens.shape
    group = 384
    first, second = gqkv.shape[1] // group, width // group
    groups = first + second

    def body(ids_ref, gqkv_ref, glow_ref, x_ref, ctx_ref, send_ref, keep_ref, t_ref, x_t):
        j = pl.program_id(0)
        place = Place(ids_ref)

        @pl.when(j == 0)
        def _():
            t_ref[...] = x_ref[...].T
            put_relative(place, t_ref, x_t)

        @pl.when(j == first)
        def _():
            t_ref[...] = ctx_ref[...].T
            put_relative(place, t_ref, x_t)

        @pl.when(j < first)
        def _():
            put_halves(dot(x_t[...], gqkv_ref[...]).astype(BF), send_ref, keep_ref)

        @pl.when(j >= first)
        def _():
            put_halves(dot(x_t[...], glow_ref[...]).astype(BF), send_ref, keep_ref)

    blocks = weight_blocks(width, group, groups // 2)
    return grid_call(
        body,
        "attention_weight",
        (groups,),
        (ids,),
        [
            (gqkv, (rows, group), lambda j, ids: (0, jnp.minimum(j, first - 1))),
            (glow, (rows, group), lambda j, ids: (0, jnp.maximum(j - first, 0))),
            whole(tokens),
            whole(context),
        ],
        [blocks, blocks],
        [pltpu.VMEM((width, rows), BF)] * 2,
        2 * rows * width * 4 * width,
    )


def last_weight(gqkv, tokens, vg_a, vg_b, vg_attn, vg_ffn, gbias_in, ids):
    rows, width = tokens.shape
    group = 256
    first = gqkv.shape[1] // group
    groups = first + 1
    cut, ratio = vg_a.shape[1], gbias_in.shape[0]

    def body(ids_ref, gqkv_ref, x_ref, va_ref, vb_ref, attn_ref, ffn_ref, bias_ref, send_ref, keep_ref, t_ref, x_t, r_ref, v_ref):
        j = pl.program_id(0)
        place = Place(ids_ref)

        @pl.when(j == 0)
        def _():
            t_ref[...] = x_ref[...].T
            put_relative(place, t_ref, x_t)

        @pl.when(j < first)
        def _():
            put_halves(dot(x_t[...], gqkv_ref[...]).astype(BF), send_ref, keep_ref)

        @pl.when(j == first)
        def _():
            r_ref[...] = jnp.zeros_like(r_ref)
            r_ref[0:2, :cut] = va_ref[0:2, :]
            r_ref[0:2, cut:] = vb_ref[0:2, :]
            r_ref[2:3, :] = attn_ref[2:3, :]
            r_ref[3:5, :] = attn_ref[0:2, :]
            r_ref[5:6, :] = ffn_ref[2:3, :]
            r_ref[6:8, :] = ffn_ref[0:2, :]
            r_ref[8 : 8 + ratio, :] = bias_ref[...]
            v_ref[0] = r_ref[...].T
            put_relative(place, v_ref.at[0], v_ref.at[1])
            both = jnp.concatenate([v_ref[1], jnp.zeros((width, group - 128), F32)], axis=1)
            put_halves(both.astype(BF), send_ref, keep_ref)

    blocks = weight_blocks(width, group, groups // 2)
    return grid_call(
        body,
        "last_weight",
        (groups,),
        (ids,),
        [
            (gqkv, (rows, group), lambda j, ids: (0, jnp.minimum(j, first - 1))),
            whole(tokens),
            whole(vg_a),
            whole(vg_b),
            whole(vg_attn),
            whole(vg_ffn),
            whole(gbias_in),
        ],
        [blocks, blocks],
        [pltpu.VMEM((width, rows), BF)] * 2
        + [pltpu.VMEM((128, width), F32), pltpu.VMEM((2, width, 128), F32)],
        2 * rows * width * width,
    )


def tokens_backward(gqkv_a, gqkv_b, gattn, ids, bufs):
    rows, width = gattn.shape
    group = 256
    span_a, span_b = gqkv_a.shape[1] // 3, gqkv_b.shape[1] // 3

    def body(ids_ref, ga_hbm, gb_hbm, gattn_ref, b0, b1, b2, b3, gx_ref, w_ref, g_ref, sems, more):
        copies = piece_copies(Place(ids_ref), (b0, b1, b2, b3), w_ref, sems, width // 8, False)
        for i in range(3):
            for at, span, source in ((0, span_a, ga_hbm), (span_a, span_b, gb_hbm)):
                copies.append(
                    pltpu.make_async_copy(
                        source.at[:, i * span : (i + 1) * span],
                        g_ref.at[:, i * width + at : i * width + at + span],
                        more.at[2 * i + at // span_a],
                    )
                )
        for copy in copies:
            copy.start()
        for copy in copies:
            copy.wait()
        for g in range(width // group):
            cols = slice(g * group, (g + 1) * group)
            gx_ref[:, cols] = gattn_ref[:, cols] + dot_nt(g_ref[...], w_ref[cols, : 3 * width])

    return call(
        body,
        "tokens_back",
        [(ids, "s"), (gqkv_a, "a"), (gqkv_b, "a"), (gattn, "v")] + [(b, "a") for b in bufs],
        [struct((rows, width), F32)],
        [
            pltpu.VMEM((width, 3 * width + 128), BF),
            pltpu.VMEM((rows, 3 * width), BF),
            pltpu.SemaphoreType.DMA((16,)),
            pltpu.SemaphoreType.DMA((6,)),
        ],
        2 * rows * width * 3 * width,
    )[0]


def norm_parts(token_rows, gain_vec, shift_vec):
    row_mean = jnp.mean(token_rows, -1, keepdims=True)
    centred = token_rows - row_mean
    inverse = lax.rsqrt(jnp.mean(centred * centred, -1, keepdims=True) + norm_eps)
    normed = centred * inverse
    return (normed * gain_vec + shift_vec, normed, inverse)


def plain_norm_back(grad_out, normed, inverse, gain_vec):
    grad_gain = jnp.sum(grad_out * normed, 0)
    grad_shift = jnp.sum(grad_out, 0)
    scaled = grad_out * gain_vec
    grad_in = inverse * (
        scaled
        - jnp.mean(scaled, -1, keepdims=True)
        - normed * jnp.mean(scaled * normed, -1, keepdims=True)
    )
    return (grad_in, grad_gain, grad_shift)


def attention_scores(query_rows, key_rows, key_valid):
    scores = jnp.einsum(
        "sqhd,skhd->shqk", query_rows, key_rows, preferred_element_type=jnp.float32
    ) * HEAD ** (-0.5)
    return jnp.where(key_valid[:, None, None, :], scores, -1000000000.0)


def forward(tokens, lengths, weights):
    (
        w_qkv,
        bias_query,
        bias_value,
        w_out,
        bias_out,
        gain_attn,
        shift_attn,
        w_in,
        bias_in,
        w_down,
        bias_down,
        gain_ffn,
        shift_ffn,
    ) = weights
    sentences, length, model_width = tokens.shape
    head_count = model_width // HEAD
    token_rows = tokens.reshape(sentences * length, model_width)
    bias_qkv = jnp.concatenate([bias_query, jnp.zeros_like(bias_query), bias_value]).astype(
        jnp.float32
    )
    packed = (jnp.dot(token_rows, w_qkv, preferred_element_type=jnp.float32) + bias_qkv).astype(
        jnp.bfloat16
    )
    packed = packed.reshape(sentences, length, 3, head_count, HEAD)
    query_rows = packed[:, :, 0]
    key_rows = packed[:, :, 1]
    value_rows = packed[:, :, 2]
    key_valid = jnp.arange(length)[None, :] < lengths[:, None]
    scores = attention_scores(query_rows, key_rows, key_valid)
    row_max = jnp.max(scores, -1, keepdims=True)
    log_total = row_max + jnp.log(jnp.sum(jnp.exp(scores - row_max), -1, keepdims=True))
    attn_probs = jnp.exp(scores - log_total)
    context = jnp.einsum(
        "shqk,skhd->sqhd",
        attn_probs.astype(jnp.bfloat16),
        value_rows,
        preferred_element_type=jnp.float32,
    )
    context = context.reshape(sentences * length, model_width).astype(jnp.bfloat16)
    attn_out = jnp.dot(context, w_out, preferred_element_type=jnp.float32) + bias_out.astype(
        jnp.float32
    )
    hidden, normed_attn, inverse_attn = norm_parts(
        token_rows.astype(jnp.float32) + attn_out,
        gain_attn.astype(jnp.float32),
        shift_attn.astype(jnp.float32),
    )
    hidden_low = hidden.astype(jnp.bfloat16)
    up_rows = jnp.dot(hidden_low, w_in, preferred_element_type=jnp.float32) + bias_in.astype(
        jnp.float32
    )
    active = jax.nn.gelu(up_rows, approximate=False).astype(jnp.bfloat16)
    ffn_out = jnp.dot(active, w_down, preferred_element_type=jnp.float32) + bias_down.astype(
        jnp.float32
    )
    output, normed_ffn, inverse_ffn = norm_parts(
        hidden + ffn_out, gain_ffn.astype(jnp.float32), shift_ffn.astype(jnp.float32)
    )
    valid_mask = key_valid.astype(jnp.float32)
    pooled = jnp.sum(
        output.reshape(sentences, length, model_width) * valid_mask[:, :, None], 1
    ) / lengths[:, None].astype(jnp.float32)
    kept = (
        key_valid,
        query_rows,
        key_rows,
        value_rows,
        log_total,
        context,
        normed_attn,
        inverse_attn,
        hidden_low,
        up_rows,
        active,
        normed_ffn,
        inverse_ffn,
    )
    return (pooled, kept)


def backward(tokens, lengths, pooled_grad, weights, kept):
    (
        w_qkv,
        bias_query,
        bias_value,
        w_out,
        bias_out,
        gain_attn,
        shift_attn,
        w_in,
        bias_in,
        w_down,
        bias_down,
        gain_ffn,
        shift_ffn,
    ) = weights
    (
        key_valid,
        query_rows,
        key_rows,
        value_rows,
        log_total,
        context,
        normed_attn,
        inverse_attn,
        hidden_low,
        up_rows,
        active,
        normed_ffn,
        inverse_ffn,
    ) = kept
    sentences, length, model_width = tokens.shape
    head_count = model_width // HEAD
    token_rows = tokens.reshape(sentences * length, model_width)
    valid_mask = key_valid.astype(jnp.float32)
    per_sentence = pooled_grad / lengths[:, None].astype(jnp.float32)
    grad_output = (valid_mask[:, :, None] * per_sentence[:, None, :]).reshape(
        sentences * length, model_width
    )
    grad_res_ffn, grad_gain_ffn, grad_shift_ffn = plain_norm_back(
        grad_output, normed_ffn, inverse_ffn, gain_ffn.astype(jnp.float32)
    )
    grad_ffn_low = grad_res_ffn.astype(jnp.bfloat16)
    grad_bias_down = jnp.sum(grad_ffn_low.astype(jnp.float32), 0)
    grad_w_down = jnp.einsum("tf,td->fd", active, grad_ffn_low, preferred_element_type=jnp.float32)
    grad_active = jnp.einsum("td,fd->tf", grad_ffn_low, w_down, preferred_element_type=jnp.float32)
    gelu_value, gelu_pull = jax.vjp(partial(jax.nn.gelu, approximate=False), up_rows)
    grad_up = gelu_pull(grad_active)[0].astype(jnp.bfloat16)
    grad_bias_in = jnp.sum(grad_up.astype(jnp.float32), 0)
    grad_w_in = jnp.einsum("td,tf->df", hidden_low, grad_up, preferred_element_type=jnp.float32)
    grad_hidden = (
        jnp.einsum("tf,df->td", grad_up, w_in, preferred_element_type=jnp.float32) + grad_res_ffn
    )
    grad_res_attn, grad_gain_attn, grad_shift_attn = plain_norm_back(
        grad_hidden, normed_attn, inverse_attn, gain_attn.astype(jnp.float32)
    )
    grad_attn_low = grad_res_attn.astype(jnp.bfloat16)
    grad_bias_out = jnp.sum(grad_attn_low.astype(jnp.float32), 0)
    grad_w_out = jnp.einsum("tc,td->cd", context, grad_attn_low, preferred_element_type=jnp.float32)
    grad_context = jnp.einsum("td,cd->tc", grad_attn_low, w_out, preferred_element_type=jnp.float32)
    grad_context = grad_context.astype(jnp.bfloat16).reshape(sentences, length, head_count, HEAD)
    scores = attention_scores(query_rows, key_rows, key_valid)
    attn_probs = jnp.exp(scores - log_total)
    grad_probs = jnp.einsum(
        "sqhd,skhd->shqk", grad_context, value_rows, preferred_element_type=jnp.float32
    )
    grad_values = jnp.einsum(
        "shqk,sqhd->skhd",
        attn_probs.astype(jnp.bfloat16),
        grad_context,
        preferred_element_type=jnp.float32,
    )
    grad_scores = (
        attn_probs * (grad_probs - jnp.sum(grad_probs * attn_probs, -1, keepdims=True))
    ).astype(jnp.bfloat16)
    grad_queries = jnp.einsum(
        "shqk,skhd->sqhd", grad_scores, key_rows, preferred_element_type=jnp.float32
    ) * HEAD ** (-0.5)
    grad_keys = jnp.einsum(
        "shqk,sqhd->skhd", grad_scores, query_rows, preferred_element_type=jnp.float32
    ) * HEAD ** (-0.5)
    grad_qkv = jnp.stack([grad_queries, grad_keys, grad_values], 2)
    grad_qkv = grad_qkv.reshape(sentences * length, 3 * model_width).astype(jnp.bfloat16)
    qkv_sums = jnp.sum(grad_qkv.astype(jnp.float32), 0)
    grad_bias_query = qkv_sums[:model_width]
    grad_bias_value = qkv_sums[2 * model_width :]
    grad_w_qkv = jnp.einsum("td,tc->dc", token_rows, grad_qkv, preferred_element_type=jnp.float32)
    grad_tokens = (
        jnp.einsum("tc,dc->td", grad_qkv, w_qkv, preferred_element_type=jnp.float32) + grad_res_attn
    )
    grad_tokens = grad_tokens.reshape(sentences, length, model_width)
    grad_terms = (
        grad_w_qkv,
        grad_bias_query,
        grad_bias_value,
        grad_w_out,
        grad_bias_out,
        grad_gain_attn,
        grad_shift_attn,
        grad_w_in,
        grad_bias_in,
        grad_w_down,
        grad_bias_down,
        grad_gain_ffn,
        grad_shift_ffn,
    )
    return (grad_terms, grad_tokens)


def on_device(
    tokens,
    lengths,
    pooled_grad,
    w_qkv,
    bias_query,
    bias_value,
    w_out,
    bias_out,
    gain_attn,
    shift_attn,
    w_in,
    bias_in,
    w_down,
    bias_down,
    gain_ffn,
    shift_ffn,
):
    weights = (
        lax.all_gather(w_qkv, "fsdp", axis=0, tiled=True),
        lax.all_gather(bias_query, "fsdp", axis=0, tiled=True),
        lax.all_gather(bias_value, "fsdp", axis=0, tiled=True),
        lax.all_gather(w_out, "fsdp", axis=0, tiled=True),
        lax.all_gather(bias_out, "fsdp", axis=0, tiled=True),
        lax.all_gather(gain_attn, "fsdp", axis=0, tiled=True),
        lax.all_gather(shift_attn, "fsdp", axis=0, tiled=True),
        lax.all_gather(w_in, "fsdp", axis=0, tiled=True),
        lax.all_gather(bias_in, "fsdp", axis=0, tiled=True),
        lax.all_gather(w_down, "fsdp", axis=0, tiled=True),
        lax.all_gather(bias_down, "fsdp", axis=0, tiled=True),
        lax.all_gather(gain_ffn, "fsdp", axis=0, tiled=True),
        lax.all_gather(shift_ffn, "fsdp", axis=0, tiled=True),
    )
    pooled, kept = forward(tokens, lengths, weights)
    grad_terms, grad_tokens = backward(tokens, lengths, pooled_grad, weights, kept)
    (
        grad_w_qkv,
        grad_bias_query,
        grad_bias_value,
        grad_w_out,
        grad_bias_out,
        grad_gain_attn,
        grad_shift_attn,
        grad_w_in,
        grad_bias_in,
        grad_w_down,
        grad_bias_down,
        grad_gain_ffn,
        grad_shift_ffn,
    ) = grad_terms
    shares = (
        lax.psum_scatter(grad_w_qkv, "fsdp", scatter_dimension=0, tiled=True),
        lax.psum_scatter(grad_bias_query, "fsdp", scatter_dimension=0, tiled=True),
        lax.psum_scatter(grad_bias_value, "fsdp", scatter_dimension=0, tiled=True),
        lax.psum_scatter(grad_w_out, "fsdp", scatter_dimension=0, tiled=True),
        lax.psum_scatter(grad_bias_out, "fsdp", scatter_dimension=0, tiled=True),
        lax.psum_scatter(grad_gain_attn, "fsdp", scatter_dimension=0, tiled=True),
        lax.psum_scatter(grad_shift_attn, "fsdp", scatter_dimension=0, tiled=True),
        lax.psum_scatter(grad_w_in, "fsdp", scatter_dimension=0, tiled=True),
        lax.psum_scatter(grad_bias_in, "fsdp", scatter_dimension=0, tiled=True),
        lax.psum_scatter(grad_w_down, "fsdp", scatter_dimension=0, tiled=True),
        lax.psum_scatter(grad_bias_down, "fsdp", scatter_dimension=0, tiled=True),
        lax.psum_scatter(grad_gain_ffn, "fsdp", scatter_dimension=0, tiled=True),
        lax.psum_scatter(grad_shift_ffn, "fsdp", scatter_dimension=0, tiled=True),
    )
    (
        share_w_qkv,
        share_bias_query,
        share_bias_value,
        share_w_out,
        share_bias_out,
        share_gain_attn,
        share_shift_attn,
        share_w_in,
        share_bias_in,
        share_w_down,
        share_bias_down,
        share_gain_ffn,
        share_shift_ffn,
    ) = shares
    totals = (
        lax.psum(share_w_qkv.astype(jnp.bfloat16), "dp").astype(jnp.float32),
        lax.psum(share_bias_query.astype(jnp.bfloat16), "dp").astype(jnp.float32),
        lax.psum(share_bias_value.astype(jnp.bfloat16), "dp").astype(jnp.float32),
        lax.psum(share_w_out.astype(jnp.bfloat16), "dp").astype(jnp.float32),
        lax.psum(share_bias_out.astype(jnp.bfloat16), "dp").astype(jnp.float32),
        lax.psum(share_gain_attn.astype(jnp.bfloat16), "dp").astype(jnp.float32),
        lax.psum(share_shift_attn.astype(jnp.bfloat16), "dp").astype(jnp.float32),
        lax.psum(share_w_in.astype(jnp.bfloat16), "dp").astype(jnp.float32),
        lax.psum(share_bias_in.astype(jnp.bfloat16), "dp").astype(jnp.float32),
        lax.psum(share_w_down.astype(jnp.bfloat16), "dp").astype(jnp.float32),
        lax.psum(share_bias_down.astype(jnp.bfloat16), "dp").astype(jnp.float32),
        lax.psum(share_gain_ffn.astype(jnp.bfloat16), "dp").astype(jnp.float32),
        lax.psum(share_shift_ffn.astype(jnp.bfloat16), "dp").astype(jnp.float32),
    )
    return (
        pooled,
        grad_tokens,
        totals[0],
        totals[1],
        totals[2],
        totals[3],
        totals[4],
        totals[5],
        totals[6],
        totals[7],
        totals[8],
        totals[9],
        totals[10],
        totals[11],
        totals[12],
    )


def swap(array, axis, bits):
    pairs = [(i, i ^ bits) for i in range(lax.axis_size(axis))]
    return lax.ppermute(array, axis, pairs)


def hold(value, *after):
    return lax.optimization_barrier((value, *after))[0]


def gather_z(piece, *after):
    return jnp.stack([hold(piece, *after)] + [swap(piece, "fsdp", 2 * k) for k in range(1, 4)])


def add(*terms):
    total = terms[0].astype(F32)
    for term in terms[1:]:
        total = total + term.astype(F32)
    return total.astype(BF)


def sum_core(send, keep, *after):
    return add(hold(keep, *after), swap(send, "dp", 1))


def sum_x(total, *after):
    return add(hold(total[0], *after), swap(total[1], "dp", 2))


def sum_y(total, *after):
    return add(hold(total[0], *after), swap(total[1], "fsdp", 1))


def sum_y_first(total, *after):
    return add(hold(total[:, 0], *after), swap(total[:, 1], "fsdp", 1))


def sum_z(total, *after):
    return add(hold(total[0], *after), *[swap(total[k], "fsdp", 2 * k) for k in range(1, 4)])


def in_order(own, other, bit, axis):
    first = jnp.where(bit == 0, own, other)
    second = jnp.where(bit == 0, other, own)
    return jnp.concatenate([first, second], axis=axis)


def share_core(own, c):
    return in_order(own, swap(own, "dp", 1), c, 0).astype(F32)


def on_device_split(
    tokens,
    lengths,
    pooled_grad,
    w_qkv,
    bias_query,
    bias_value,
    w_out,
    bias_out,
    gain_attn,
    shift_attn,
    w_in,
    bias_in,
    w_down,
    bias_down,
    gain_ffn,
    shift_ffn,
):
    sentences, length, width = tokens.shape
    rows = sentences * length
    wide = w_in.shape[1]
    part = width // 8
    dp, fsdp = lax.axis_index("dp"), lax.axis_index("fsdp")
    x, c = dp // 2, dp % 2
    ids = jnp.stack([fsdp // 2, fsdp % 2, x, c]).astype(jnp.int32)
    token_rows = tokens.reshape(rows, width)

    vectors = jnp.stack(
        [bias_query, bias_value, bias_out, gain_attn, shift_attn, bias_down, gain_ffn, shift_ffn]
    )
    vectors = jnp.concatenate([vectors, bias_in.reshape(wide // width, part)], 0)
    vectors = jnp.pad(vectors.T, ((0, 0), (0, 128 - vectors.shape[0])))
    first = jnp.concatenate([w_qkv, vectors], 1)
    second = jnp.concatenate([w_out, w_in], 1)
    half = part // 2
    first = lax.dynamic_slice(first, (c * half, 0), (half, first.shape[1]))
    span = second.shape[1] // 2
    second = lax.dynamic_slice(second, (c * half, x * span), (half, span))
    third = lax.dynamic_slice(w_down, (c * (w_down.shape[0] // 2), 0), (w_down.shape[0] // 2, width))

    near1 = gather_z(first)
    near2 = gather_z(hold(second, near1))
    far1 = hold(swap(near1, "fsdp", 1), near2)
    bufs1 = [near1, far1, swap(near1, "dp", 1), swap(far1, "dp", 1)]
    qkv, context, lse, vec = attend_forward(
        hold(token_rows, near2), lengths, ids, bufs1, sentences, length
    )
    near3 = gather_z(hold(third, near2), vec)
    far2 = hold(swap(near2, "fsdp", 1), vec)
    side2 = hold(swap(near2, "dp", 2), vec)
    far3 = swap(near3, "fsdp", 1)
    mine2 = [near2, far2, side2, swap(far2, "dp", 2)]
    bufs2 = mine2 + [swap(hold(m, vec), "dp", 1) for m in mine2]
    ratio = wide // width
    bias_up = vec[8 : 8 + ratio].reshape(ratio, 8, part).transpose(1, 0, 2).reshape(1, wide)
    normed, inverse, low, active, slope = up_forward(
        context, token_rows, vec, bias_up, ids, bufs2, length
    )
    far3 = hold(far3, low)
    bufs3 = [near3, far3, swap(near3, "dp", 1), swap(far3, "dp", 1)]
    pooled, vg_ffn, send3, keep3, gup, gbias_in, gres = down_and_back(
        active, slope, normed, vec, lengths, pooled_grad, ids, bufs3, sentences, length
    )
    sums3 = sum_core(send3, keep3)
    send2, keep2, gctx, vg_attn, gattn, gattn_low = up_and_back(
        low, hold(gup, sums3), gres, normed, inverse, vec, ids, bufs2, length
    )
    sums3 = sum_y(sums3[0], gctx)
    sums2 = sum_core(hold(send2, gctx, sums3), keep2)
    pairs = width // 128
    most = pairs * 2 // 3
    gqkv_a, vg_a = attend_backward(
        qkv, hold(gctx, sums3, sums2), lse, lengths, sentences, length, 0, most, "attention_back"
    )
    send_a, keep_a = attend_weight(gqkv_a, token_rows, context, gattn_low, ids)
    sums2 = sum_x(sums2, keep_a)
    sums3 = sum_z(sums3, keep_a)
    sums_a = sum_core(hold(send_a, sums2, sums3), keep_a)
    gqkv_b, vg_b = attend_backward(
        qkv, hold(gctx, sums_a), lse, lengths, sentences, length, most, pairs, "attention_back_rest"
    )
    gbias_in = gbias_in.reshape(8, ratio, part).transpose(1, 0, 2).reshape(ratio, width)
    send_b, keep_b = last_weight(gqkv_b, token_rows, vg_a, vg_b, vg_attn, vg_ffn, gbias_in, ids)
    sums2 = sum_y(sums2, gqkv_b)
    sums3 = add(hold(sums3, keep_b), swap(sums3, "dp", 2))
    sums_b = sum_core(send_b, keep_b)
    gtokens = tokens_backward(gqkv_a, hold(gqkv_b, sums_b, sums2, sums3), gattn, ids, bufs1)
    sums_a = sum_x(sums_a, gtokens)
    sums2 = sum_z(sums2, sums_a)
    sums_b = sum_y_first(sums_b, sums2)
    sums_a, sums2, sums_b = lax.optimization_barrier((sums_a, sums2, sums_b))
    sums_a = sum_y(sums_a)
    sums_b = sum_x(sums_b)
    g_in = in_order(sums2, swap(sums2, "dp", 2), x, 1)
    sums_a, sums_b, g_in = lax.optimization_barrier((sums_a, sums_b, g_in))
    g_down = share_core(sums3, c).T
    g_in = share_core(g_in, c)
    sums_a = sum_z(sums_a)
    sums_b = sum_z(sums_b)
    g_b = share_core(in_order(sums_b, swap(sums_b, "dp", 2), x, 1), c)
    g_a = share_core(in_order(sums_a, swap(sums_a, "dp", 2), x, 1), c)
    gtokens = gtokens.reshape(sentences, length, width)
    cut_a, cut_b = most * 128, (pairs - most) * 128
    g_qkv = [
        g[:, i * cut : (i + 1) * cut] for i in range(3) for g, cut in ((g_a, cut_a), (g_b, cut_b))
    ]
    g_vec = g_b[:, 3 * cut_b : 3 * cut_b + 8 + ratio].T
    return (
        pooled,
        gtokens,
        jnp.concatenate(g_qkv, 1),
        g_vec[0],
        g_vec[1],
        g_a[:, 3 * cut_a :],
        g_vec[2],
        g_vec[3],
        g_vec[4],
        g_in,
        g_vec[8:].reshape(wide // 8),
        g_down,
        g_vec[5],
        g_vec[6],
        g_vec[7],
    )


def solution(mesh):
    placed = (
        P(("dp", "fsdp"), None, None),
        P(("dp", "fsdp")),
        P(("dp", "fsdp"), None),
        P("fsdp", None),
        P("fsdp"),
        P("fsdp"),
        P("fsdp", None),
        P("fsdp"),
        P("fsdp"),
        P("fsdp"),
        P("fsdp", None),
        P("fsdp"),
        P("fsdp", None),
        P("fsdp"),
        P("fsdp"),
        P("fsdp"),
    )
    body = on_device_split if mesh.shape["fsdp"] == 8 and mesh.shape["dp"] == 4 else on_device
    return jax.shard_map(
        body,
        mesh=mesh,
        in_specs=placed,
        out_specs=(
            P(("dp", "fsdp"), None),
            P(("dp", "fsdp"), None, None),
            P("fsdp", None),
            P("fsdp"),
            P("fsdp"),
            P("fsdp", None),
            P("fsdp"),
            P("fsdp"),
            P("fsdp"),
            P("fsdp", None),
            P("fsdp"),
            P("fsdp", None),
            P("fsdp"),
            P("fsdp"),
            P("fsdp"),
        ),
        check_vma=False,
    )
```

```python
from functools import partial

import jax
import jax.numpy as jnp
from jax import lax
from jax.experimental import pallas as pl
from jax.experimental.pallas import tpu as pltpu
from jax.sharding import PartitionSpec as P

norm_eps = 1e-06

HEAD = 64
NORM_EPS = 1e-06
BF = jnp.bfloat16
F32 = jnp.float32
VMEM_LIMIT = 60 * 1024 * 1024


def dot(a, b):
    return lax.dot_general(a, b, (((1,), (0,)), ((), ())), preferred_element_type=F32)


def dot_nt(a, b):
    return lax.dot_general(a, b, (((1,), (1,)), ((), ())), preferred_element_type=F32)


def dot_tn(a, b):
    return lax.dot_general(a, b, (((0,), (0,)), ((), ())), preferred_element_type=F32)


def aligned(value, step):
    return pl.multiple_of(value, step)


class Place:
    def __init__(self, ids_ref):
        self.z, self.y, self.x, self.c = ids_ref[0], ids_ref[1], ids_ref[2], ids_ref[3]

    def shard(self, k, yy):
        return lax.bitwise_xor(self.z, k) * 2 + lax.bitwise_xor(self.y, yy)


def piece_copies(place, bufs, dst, sems, shard_rows, split_x):
    half = shard_rows // 2
    copies = []
    at = 0
    for cc in range(2):
        core = lax.bitwise_xor(place.c, cc)
        for xx in range(2 if split_x else 1):
            for yy in range(2):
                buf = bufs[at]
                at += 1
                width = buf.shape[-1]
                for k in range(4):
                    row = aligned(place.shard(k, yy) * shard_rows + core * half, 16)
                    if split_x:
                        col = aligned(lax.bitwise_xor(place.x, xx) * width, 128)
                        target = dst.at[pl.ds(row, half), pl.ds(col, width)]
                    else:
                        target = dst.at[pl.ds(row, half), :]
                    copies.append(
                        pltpu.make_async_copy(buf.at[k], target, sems.at[len(copies)])
                    )
    return copies


def call(body, name, ins, outs, scratch, flops, transcendentals=0):
    spaces = {
        "s": pl.BlockSpec(memory_space=pltpu.SMEM),
        "v": pl.BlockSpec(memory_space=pltpu.VMEM),
        "a": pl.BlockSpec(memory_space=pl.ANY),
    }
    moved = sum(a.size * a.dtype.itemsize for a, _ in ins) + sum(
        o.size * o.dtype.itemsize for o in outs
    )
    return pl.pallas_call(
        body,
        name=name,
        out_shape=tuple(outs),
        in_specs=[spaces[s] for _, s in ins],
        out_specs=tuple(spaces["v"] for _ in outs),
        scratch_shapes=scratch,
        compiler_params=pltpu.CompilerParams(vmem_limit_bytes=VMEM_LIMIT),
        cost_estimate=pl.CostEstimate(flops=1, transcendentals=0, bytes_accessed=1),
    )(*[a for a, _ in ins])


def struct(shape, dtype):
    return jax.ShapeDtypeStruct(shape, dtype)


def two_heads(block):
    low = lax.broadcasted_iota(jnp.int32, block.shape, 1) < HEAD
    zero = jnp.zeros_like(block)
    return jnp.concatenate([jnp.where(low, block, zero), jnp.where(low, zero, block)], axis=0)


def one_of_two(stacked):
    rows = stacked.shape[0] // 2
    low = lax.broadcasted_iota(jnp.int32, (rows, stacked.shape[1]), 1) < HEAD
    return jnp.where(low, stacked[:rows], stacked[rows:])


def masked_scores(query, keys2, count, length):
    scores = dot_nt(query, keys2)
    slot = lax.broadcasted_iota(jnp.int32, scores.shape, 1)
    slot = jnp.where(slot >= length, slot - length, slot)
    return jnp.where(slot < count, scores, -1000000000.0)


def halves(stat_a, stat_b, length):
    rows = stat_a.shape[0]
    return jnp.concatenate(
        [jnp.broadcast_to(stat_a, (rows, length)), jnp.broadcast_to(stat_b, (rows, length))], axis=1
    )


def layer_norm(v):
    centred = v - jnp.mean(v, -1, keepdims=True)
    inverse = lax.rsqrt(jnp.mean(centred * centred, -1, keepdims=True) + NORM_EPS)
    return centred * inverse, inverse


def norm_back(grad, normed, inverse, gain):
    scaled = grad * gain
    return inverse * (
        scaled
        - jnp.mean(scaled, -1, keepdims=True)
        - normed * jnp.mean(scaled * normed, -1, keepdims=True)
    )


def row(vec_ref, at):
    return vec_ref[at : at + 1, :]


def grid_call(body, name, grid, scalars, ins, outs, scratch, flops, transcendentals=0):
    def spec(block, index):
        if block is None:
            return pl.BlockSpec(memory_space=pl.ANY)
        return pl.BlockSpec(block, index)

    moved = sum(a.size * a.dtype.itemsize for a, _, _ in ins) + sum(
        o.size * o.dtype.itemsize for o, _, _ in outs
    )
    return pl.pallas_call(
        body,
        name=name,
        out_shape=tuple(o for o, _, _ in outs),
        grid_spec=pltpu.PrefetchScalarGridSpec(
            num_scalar_prefetch=len(scalars),
            grid=grid,
            in_specs=[spec(b, i) for _, b, i in ins],
            out_specs=tuple(spec(b, i) for _, b, i in outs),
            scratch_shapes=scratch,
        ),
        compiler_params=pltpu.CompilerParams(
            vmem_limit_bytes=VMEM_LIMIT, dimension_semantics=("arbitrary",) * len(grid)
        ),
        cost_estimate=pl.CostEstimate(flops=1, transcendentals=0, bytes_accessed=1),
    )(*scalars, *[a for a, _, _ in ins])


def whole(array):
    return (array, array.shape, lambda *_: (0,) * array.ndim)


def left(array):
    return (array, None, None)


def qkv_forward(tokens, ids, bufs):
    rows, width = tokens.shape
    group = 256

    def body(ids_ref, x_ref, b0, b1, b2, b3, qkv_hbm, vec_ref, w_ref, out_ref, sems, more):
        place = Place(ids_ref)
        copies = piece_copies(place, (b0, b1, b2, b3), w_ref, sems, width // 8, False)
        for copy in copies:
            copy.start()
        for copy in copies:
            copy.wait()
        vec_ref[...] = w_ref[:, 3 * width :].astype(F32).T[: vec_ref.shape[0]]
        x = x_ref[...]
        outs = []
        for part in range(3):
            for g in range(width // group):
                col = part * width + g * group
                y = dot(x, w_ref[:, col : col + group])
                if part != 1:
                    bias = vec_ref[part // 2 : part // 2 + 1, g * group : (g + 1) * group]
                    y = y + bias
                out_ref[:, col : col + group] = y.astype(BF)
            here = slice(part * width, (part + 1) * width)
            outs.append(
                pltpu.make_async_copy(out_ref.at[:, here], qkv_hbm.at[:, here], more.at[part])
            )
            outs[-1].start()
        for out in outs:
            out.wait()

    return grid_call(
        body,
        "qkv",
        (1,),
        (ids,),
        [whole(tokens)] + [left(b) for b in bufs],
        [left(struct((rows, 3 * width), BF)), whole(struct((16, width), F32))],
        [
            pltpu.VMEM((width, 3 * width + 128), BF),
            pltpu.VMEM((rows, 3 * width), BF),
            pltpu.SemaphoreType.DMA((16,)),
            pltpu.SemaphoreType.DMA((3,)),
        ],
        2 * rows * width * 3 * width,
    )


def attend_forward(qkv, counts, sentences, length):
    rows, width = qkv.shape[0], qkv.shape[1] // 3
    pairs = width // 128

    def body(counts_ref, qkv_ref, ctx_ref, lse_ref):
        count = counts_ref[pl.program_id(0)]
        lane = lax.broadcasted_iota(jnp.int32, (length, 128), 1)
        lse_all = jnp.zeros((length, 128), F32)
        for p in range(pairs):
            query = qkv_ref[:, p * 128 : (p + 1) * 128] * jnp.asarray(HEAD**-0.5, BF)
            keys2 = two_heads(qkv_ref[:, width + p * 128 : width + (p + 1) * 128])
            values2 = two_heads(qkv_ref[:, 2 * width + p * 128 : 2 * width + (p + 1) * 128])
            scores = masked_scores(query, keys2, count, length)
            a, b = scores[:, :length], scores[:, length:]
            max_a = jnp.max(a, -1, keepdims=True)
            max_b = jnp.max(b, -1, keepdims=True)
            e_a, e_b = jnp.exp(a - max_a), jnp.exp(b - max_b)
            sum_a = jnp.sum(e_a, -1, keepdims=True)
            sum_b = jnp.sum(e_b, -1, keepdims=True)
            lse_all = jnp.where(lane == 2 * p, max_a + jnp.log(sum_a), lse_all)
            lse_all = jnp.where(lane == 2 * p + 1, max_b + jnp.log(sum_b), lse_all)
            probs = jnp.concatenate([e_a * (1.0 / sum_a), e_b * (1.0 / sum_b)], axis=1).astype(BF)
            ctx_ref[:, p * 128 : (p + 1) * 128] = dot(probs, values2).astype(BF)
        lse_ref[...] = lse_all

    def by_rows(array):
        return (array, (length, array.shape[1]), lambda s, counts: (s, 0))

    return grid_call(
        body,
        "attention",
        (sentences,),
        (counts,),
        [by_rows(qkv)],
        [by_rows(struct((rows, width), BF)), by_rows(struct((rows, 128), F32))],
        [],
        8 * rows * length * width,
        rows * length * width // HEAD,
    )


CHUNK = 128


def up_forward(context, tokens, vec, bias_in, ids, bufs, length):
    rows, width = tokens.shape
    wide = bias_in.shape[1]
    group, block = 256, 512
    steps = wide // block

    def body(ids_ref, ctx_ref, x_ref, vec_ref, bin_ref, *rest):
        bufs_ref = rest[: len(bufs)]
        act_ref, slope_ref, n_hbm, inv_hbm, low_hbm, w_ref, n_ref, inv_ref, low_ref, sems, more = rest[len(bufs) :]
        step = pl.program_id(0)
        outs = [
            pltpu.make_async_copy(a, b, more.at[i])
            for i, (a, b) in enumerate(((n_ref, n_hbm), (inv_ref, inv_hbm), (low_ref, low_hbm)))
        ]

        @pl.when(step == 0)
        def _():
            copies = piece_copies(Place(ids_ref), bufs_ref, w_ref, sems, width // 8, True)
            for copy in copies:
                copy.start()
            for copy in copies:
                copy.wait()
            for g in range(width // group):
                cols = slice(g * group, (g + 1) * group)
                n_ref[:, cols] = dot(ctx_ref[...], w_ref[:, cols])

            def norm_rows(i, carry):
                here = pl.ds(aligned(i * CHUNK, CHUNK), CHUNK)
                v = x_ref[here, :].astype(F32) + (n_ref[here, :] + row(vec_ref, 2))
                normed, inverse = layer_norm(v)
                n_ref[here, :] = normed
                inv_ref[here, :] = jnp.broadcast_to(inverse, (CHUNK, 128))
                low_ref[here, :] = (normed * row(vec_ref, 3) + row(vec_ref, 4)).astype(BF)
                return carry

            lax.fori_loop(0, rows // CHUNK, norm_rows, 0)
            for out in outs:
                out.start()

        for g in range(block // group):
            cols = slice(g * group, (g + 1) * group)
            here = pl.ds(aligned(width + step * block + g * group, 128), group)
            u = dot(low_ref[...], w_ref[:, here]) + bin_ref[:, cols]
            cdf = 0.5 * (1.0 + lax.erf(u * (0.5**0.5)))
            pdf = jnp.exp(-0.5 * u * u) * 0.3989422804014327
            act_ref[:, cols] = (u * cdf).astype(BF)
            slope_ref[:, cols] = (cdf + u * pdf).astype(BF)

        @pl.when(step == steps - 1)
        def _():
            for out in outs:
                out.wait()

    active, slope, normed, inverse, low = grid_call(
        body,
        "out_norm_up",
        (steps,),
        (ids,),
        [whole(context), whole(tokens), whole(vec), (bias_in, (1, block), lambda j, ids: (0, j))]
        + [left(b) for b in bufs],
        [
            (struct((rows, wide), BF), (rows, block), lambda j, ids: (0, j)),
            (struct((rows, wide), BF), (rows, block), lambda j, ids: (0, j)),
            left(struct((rows, width), F32)),
            left(struct((rows, 128), F32)),
            left(struct((rows, width), BF)),
        ],
        [
            pltpu.VMEM((width, width + wide), BF),
            pltpu.VMEM((rows, width), F32),
            pltpu.VMEM((rows, 128), F32),
            pltpu.VMEM((rows, width), BF),
            pltpu.SemaphoreType.DMA((32,)),
            pltpu.SemaphoreType.DMA((3,)),
        ],
        2 * rows * width * (width + wide),
    )
    return normed, inverse, low, active, slope


def relative(ids, step):
    return lax.bitwise_xor(ids[0] * 2 + ids[1], step)


def put_relative(place, source, dst):
    half = source.shape[0] // 16
    for cc in range(2):
        core = lax.bitwise_xor(place.c, cc)
        for yy in range(2):
            for k in range(4):
                at = ((cc * 2 + yy) * 4 + k) * half
                here = aligned(place.shard(k, yy) * 2 * half + core * half, 16)
                dst[at : at + half, :] = source[pl.ds(here, half), :]


def natural_copies(place, bufs, dst, sems):
    half = bufs[0].shape[1]
    copies = []
    for cc in range(2):
        for yy in range(2):
            for k in range(4):
                at = place.shard(k, yy) * 2 * half + lax.bitwise_xor(place.c, cc) * half
                copies.append(
                    pltpu.make_async_copy(
                        bufs[2 * cc + yy].at[k], dst.at[pl.ds(aligned(at, 16), half), :], sems.at[len(copies)]
                    )
                )
    return copies


def down_and_back(active, slope, normed, vec, counts, pooled_grad, ids, bufs, sentences, length):
    rows, wide = active.shape
    width = normed.shape[1]
    shard = wide // 8
    half = width // 2
    group = 256

    def body(ids_ref, counts_ref, act_hbm, slope_ref, vec_ref, pg_ref, n_hbm, b0, b1, b2, b3, pooled_ref, vg_ref, send_ref, keep_ref, gup_ref, gbias_ref, gres_hbm, w_ref, acc_ref, n_ref, glow_ref, act_ref, t_ref, sems, more):
        step = pl.program_id(0)
        place = Place(ids_ref)
        bufs_ref = (b0, b1, b2, b3)
        load = pltpu.make_async_copy(n_hbm, n_ref, more.at[0])
        load_active = pltpu.make_async_copy(act_hbm, act_ref, more.at[1 + sentences])

        def columns_of(phase):
            return pl.ds(aligned(relative(ids_ref, step - phase) * shard, 128), shard)

        def out(s):
            here = pl.ds(aligned(s * length, length), length)
            return pltpu.make_async_copy(acc_ref.at[here, :], gres_hbm.at[here, :], more.at[1 + s])

        @pl.when(step == 0)
        def _():
            copies = natural_copies(place, bufs_ref, w_ref, sems)
            load_active.start()
            for copy in copies:
                copy.start()
            load.start()
            vg_ref[...] = jnp.zeros_like(vg_ref)
            for copy in copies:
                copy.wait()
            load_active.wait()
            for g in range(width // group):
                cols = slice(g * group, (g + 1) * group)
                acc_ref[:, cols] = dot(act_ref[...], w_ref[:, cols])
            load.wait()

            def norm_rows(s, carry):
                here = pl.ds(aligned(s * length, length), length)
                hidden = n_ref[here, :] * row(vec_ref, 3) + row(vec_ref, 4)
                n2, inverse = layer_norm(hidden + (acc_ref[here, :] + row(vec_ref, 5)))
                valid = lax.broadcasted_iota(jnp.int32, (length, width), 0) < counts_ref[s]
                count = counts_ref[s].astype(F32)
                out_rows = jnp.where(valid, n2 * row(vec_ref, 6) + row(vec_ref, 7), 0.0)
                pooled_ref[pl.ds(s, 1), :] = jnp.sum(out_rows, 0, keepdims=True) / count
                grad = jnp.where(valid, pg_ref[pl.ds(s, 1), :] / count, 0.0)
                vg_ref[0:1, :] += jnp.sum(grad * n2, 0, keepdims=True)
                vg_ref[1:2, :] += jnp.sum(grad, 0, keepdims=True)
                gres = norm_back(grad, n2, inverse, row(vec_ref, 6))
                acc_ref[here, :] = gres
                glow = gres.astype(BF)
                glow_ref[here, :] = glow
                vg_ref[2:3, :] += jnp.sum(glow.astype(F32), 0, keepdims=True)
                out(s).start()
                return carry

            lax.fori_loop(0, sentences, norm_rows, 0)
            t_ref[...] = glow_ref[...].T

        @pl.when(jnp.logical_and(step >= 1, step < 9))
        def _():
            for cc, out_ref in ((0, keep_ref), (1, send_ref)):
                core = lax.bitwise_xor(place.c, cc)
                out_ref[0, 0, 0] = dot(
                    t_ref[pl.ds(aligned(core * half, half), half), :], act_ref[:, columns_of(1)]
                ).astype(BF)

        @pl.when(step >= 9)
        def _():
            gact = dot_nt(glow_ref[...], w_ref[columns_of(9), :])
            gup = (gact * slope_ref[...].astype(F32)).astype(BF)
            gup_ref[...] = gup
            gbias_ref[...] = jnp.sum(gup.astype(F32), 0, keepdims=True)

        @pl.when(step == 16)
        def _():
            for s in range(sentences):
                out(s).wait()

    def at(step, phase):
        return jnp.clip(step - phase, 0, 7)

    def grad_block(step, ids, counts):
        r = at(step, 1)
        return (0, lax.rem(r, 2), lax.div(r, 2), 0, 0)

    def columns(phase):
        return lambda step, ids, counts: (0, relative(ids, at(step, phase)))

    grads = (struct((1, 2, 4, half, shard), BF), (1, 1, 1, half, shard), grad_block)
    return grid_call(
        body,
        "down_and_back",
        (17,),
        (ids, counts),
        [
            left(active),
            (slope, (rows, shard), columns(9)),
            whole(vec),
            whole(pooled_grad),
            left(normed),
        ]
        + [left(b) for b in bufs],
        [
            whole(struct((sentences, width), F32)),
            whole(struct((8, width), F32)),
            grads,
            grads,
            (struct((rows, wide), BF), (rows, shard), columns(9)),
            (struct((1, wide), F32), (1, shard), columns(9)),
            left(struct((rows, width), F32)),
        ],
        [
            pltpu.VMEM((wide, width), BF),
            pltpu.VMEM((rows, width), F32),
            pltpu.VMEM((rows, width), F32),
            pltpu.VMEM((rows, width), BF),
            pltpu.VMEM((rows, wide), BF),
            pltpu.VMEM((width, rows), BF),
            pltpu.SemaphoreType.DMA((16,)),
            pltpu.SemaphoreType.DMA((2 + sentences,)),
        ],
        6 * rows * width * wide,
    )


def up_and_back(low, gup, gres, normed, inverse, vec, ids, bufs, length):
    rows, wide = gup.shape
    width = gres.shape[1]
    sentences = rows // length
    group, block = 256, 512
    steps = wide // block
    per = steps // 2

    def body(ids_ref, low_ref, gup_ref, vec_ref, gres_hbm, n_hbm, inv_hbm, *rest):
        bufs_ref = rest[: len(bufs)]
        send_ref, keep_ref, gctx_ref, vg_ref, gattn_hbm, glow_hbm, w_ref, acc_ref, gres_ref, n_ref, inv_ref, glow_ref, t_ref, p_ref, gup_all, sems, more = rest[len(bufs) :]
        step = pl.program_id(0)
        place = Place(ids_ref)
        loads = [
            pltpu.make_async_copy(a, b, more.at[i])
            for i, (a, b) in enumerate(((gres_hbm, gres_ref), (n_hbm, n_ref), (inv_hbm, inv_ref)))
        ]
        copies = piece_copies(place, bufs_ref, w_ref, sems, width // 8, True)

        @pl.when(step == 0)
        def _():
            for copy in copies:
                copy.start()
            for load in loads:
                load.start()
            t_ref[...] = low_ref[...].T
            put_relative(place, t_ref, p_ref)

        put_halves(dot(p_ref[...], gup_ref[...]).astype(BF), send_ref, keep_ref)

        gup_all[:, pl.ds(aligned(step * block, 128), block)] = gup_ref[...]

        @pl.when(step == steps - 1)
        def _():
            for copy in copies:
                copy.wait()
            for g in range(width // group):
                cols = slice(g * group, (g + 1) * group)
                acc_ref[:, cols] = dot_nt(gup_all[...], w_ref[cols, width:])
            for load in loads:
                load.wait()
            vg_ref[...] = jnp.zeros_like(vg_ref)

            def outs(s):
                here = pl.ds(aligned(s * length, length), length)
                return (
                    pltpu.make_async_copy(acc_ref.at[here, :], gattn_hbm.at[here, :], more.at[3 + s]),
                    pltpu.make_async_copy(
                        glow_ref.at[here, :], glow_hbm.at[here, :], more.at[3 + sentences + s]
                    ),
                )

            def norm_rows(s, carry):
                here = pl.ds(aligned(s * length, length), length)
                grad = acc_ref[here, :] + gres_ref[here, :]
                normed = n_ref[here, :]
                vg_ref[0:1, :] += jnp.sum(grad * normed, 0, keepdims=True)
                vg_ref[1:2, :] += jnp.sum(grad, 0, keepdims=True)
                gattn = norm_back(grad, normed, inv_ref[here, 0:1], row(vec_ref, 3))
                acc_ref[here, :] = gattn
                glow = gattn.astype(BF)
                glow_ref[here, :] = glow
                vg_ref[2:3, :] += jnp.sum(glow.astype(F32), 0, keepdims=True)
                for copy in outs(s):
                    copy.start()
                return carry

            lax.fori_loop(0, sentences, norm_rows, 0)
            for g in range(width // group):
                gctx_ref[:, g * group : (g + 1) * group] = dot_nt(
                    glow_ref[...], w_ref[g * group : (g + 1) * group, :width]
                ).astype(BF)
            for s in range(sentences):
                for copy in outs(s):
                    copy.wait()

    blocks = weight_blocks(width, block, per)
    return grid_call(
        body,
        "up_and_back",
        (steps,),
        (ids,),
        [whole(low), (gup, (rows, block), lambda j, ids: (0, j)), whole(vec), left(gres), left(normed), left(inverse)]
        + [left(b) for b in bufs],
        [
            blocks,
            blocks,
            whole(struct((rows, width), BF)),
            whole(struct((8, width), F32)),
            left(struct((rows, width), F32)),
            left(struct((rows, width), BF)),
        ],
        [
            pltpu.VMEM((width, width + wide), BF),
            pltpu.VMEM((rows, width), F32),
            pltpu.VMEM((rows, width), F32),
            pltpu.VMEM((rows, width), F32),
            pltpu.VMEM((rows, 128), F32),
            pltpu.VMEM((rows, width), BF),
            pltpu.VMEM((width, rows), BF),
            pltpu.VMEM((width, rows), BF),
            pltpu.VMEM((rows, wide), BF),
            pltpu.SemaphoreType.DMA((32,)),
            pltpu.SemaphoreType.DMA((3 + 2 * sentences,)),
        ],
        2 * rows * width * (width + 2 * wide),
    )


def attend_backward(qkv, gctx, lse, counts, sentences, length, low, high, name):
    rows, width = gctx.shape
    span = (high - low) * 128
    twos = range(low // 2, high // 2)

    def body(counts_ref, *refs):
        parts = [refs[i * len(twos) : (i + 1) * len(twos)] for i in range(3)]
        gctx_ref, lse_ref, gqkv_ref, vs_ref = refs[3 * len(twos) :]
        s = pl.program_id(0)

        @pl.when(s == 0)
        def _():
            vs_ref[...] = jnp.zeros_like(vs_ref)

        count = counts_ref[s]
        for p in range(low, high):
            at = (p - low) * 128
            block, cols = (p - low) // 2, slice(p % 2 * 128, p % 2 * 128 + 128)
            query = parts[0][block][:, cols] * jnp.asarray(HEAD**-0.5, BF)
            keys2 = two_heads(parts[1][block][:, cols])
            values2 = two_heads(parts[2][block][:, cols])
            gout = gctx_ref[:, at : at + 128]
            scores = masked_scores(query, keys2, count, length)
            lse2 = halves(lse_ref[:, 2 * p : 2 * p + 1], lse_ref[:, 2 * p + 1 : 2 * p + 2], length)
            probs = jnp.exp(scores - lse2)
            gprobs = dot_nt(gout, values2)
            weighted = gprobs * probs
            sums = halves(
                jnp.sum(weighted[:, :length], -1, keepdims=True),
                jnp.sum(weighted[:, length:], -1, keepdims=True),
                length,
            )
            gscores = (probs * (gprobs - sums)).astype(BF)
            gq = (dot(gscores, keys2) * HEAD**-0.5).astype(BF)
            gk = one_of_two(dot_tn(gscores, query)).astype(BF)
            gv = one_of_two(dot_tn(probs.astype(BF), gout)).astype(BF)
            gqkv_ref[:, at : at + 128] = gq
            gqkv_ref[:, span + at : span + at + 128] = gk
            gqkv_ref[:, 2 * span + at : 2 * span + at + 128] = gv
            vs_ref[0:1, at : at + 128] += jnp.sum(gq.astype(F32), 0, keepdims=True)
            vs_ref[1:2, at : at + 128] += jnp.sum(gv.astype(F32), 0, keepdims=True)

    def by_rows(array):
        return (array, (length, array.shape[1]), lambda s, counts: (s, 0))

    return grid_call(
        body,
        name,
        (sentences,),
        (counts,),
        [
            (qkv, (length, 256), lambda s, counts, at=part * width // 256 + b: (s, at))
            for part in range(3)
            for b in twos
        ]
        + [(gctx, (length, span), lambda s, counts: (s, low * 128 // span)), by_rows(lse)],
        [by_rows(struct((rows, 3 * span), BF)), whole(struct((8, span), F32))],
        [],
        20 * rows * length * span,
    )


def weight_blocks(width, group, per):
    half = width // 16
    return (
        struct((2, 2, 4, half, per * group), BF),
        (1, 2, 4, half, group),
        lambda j, ids: (lax.bitwise_xor(ids[2], lax.div(j, per)), 0, 0, 0, lax.rem(j, per)),
    )


def put_halves(dw, send_ref, keep_ref):
    width, group = dw.shape
    shape = (2, 4, width // 16, group)
    keep_ref[0] = dw[: width // 2].reshape(shape)
    send_ref[0] = dw[width // 2 :].reshape(shape)


def attend_weight(gqkv, tokens, context, glow, ids):
    rows, width = tokens.shape
    group = 384
    first, second = gqkv.shape[1] // group, width // group
    groups = first + second

    def body(ids_ref, gqkv_ref, glow_ref, x_ref, ctx_ref, send_ref, keep_ref, t_ref, x_t):
        j = pl.program_id(0)
        place = Place(ids_ref)

        @pl.when(j == 0)
        def _():
            t_ref[...] = x_ref[...].T
            put_relative(place, t_ref, x_t)

        @pl.when(j == first)
        def _():
            t_ref[...] = ctx_ref[...].T
            put_relative(place, t_ref, x_t)

        @pl.when(j < first)
        def _():
            put_halves(dot(x_t[...], gqkv_ref[...]).astype(BF), send_ref, keep_ref)

        @pl.when(j >= first)
        def _():
            put_halves(dot(x_t[...], glow_ref[...]).astype(BF), send_ref, keep_ref)

    blocks = weight_blocks(width, group, groups // 2)
    return grid_call(
        body,
        "attention_weight",
        (groups,),
        (ids,),
        [
            (gqkv, (rows, group), lambda j, ids: (0, jnp.minimum(j, first - 1))),
            (glow, (rows, group), lambda j, ids: (0, jnp.maximum(j - first, 0))),
            whole(tokens),
            whole(context),
        ],
        [blocks, blocks],
        [pltpu.VMEM((width, rows), BF)] * 2,
        2 * rows * width * 4 * width,
    )


def last_weight(gqkv, tokens, vg_a, vg_b, vg_attn, vg_ffn, gbias_in, ids):
    rows, width = tokens.shape
    group = 256
    first = gqkv.shape[1] // group
    groups = first + 1
    cut, ratio, part = vg_a.shape[1], gbias_in.shape[1] // width, width // 8

    def body(ids_ref, gqkv_ref, x_ref, va_ref, vb_ref, attn_ref, ffn_ref, bias_ref, send_ref, keep_ref, t_ref, x_t, r_ref, v_ref):
        j = pl.program_id(0)
        place = Place(ids_ref)

        @pl.when(j == 0)
        def _():
            t_ref[...] = x_ref[...].T
            put_relative(place, t_ref, x_t)

        @pl.when(j < first)
        def _():
            put_halves(dot(x_t[...], gqkv_ref[...]).astype(BF), send_ref, keep_ref)

        @pl.when(j == first)
        def _():
            r_ref[...] = jnp.zeros_like(r_ref)
            r_ref[0:2, :cut] = va_ref[0:2, :]
            r_ref[0:2, cut:] = vb_ref[0:2, :]
            r_ref[2:3, :] = attn_ref[2:3, :]
            r_ref[3:5, :] = attn_ref[0:2, :]
            r_ref[5:6, :] = ffn_ref[2:3, :]
            r_ref[6:8, :] = ffn_ref[0:2, :]
            for shard in range(8):
                for i in range(ratio):
                    at = (shard * ratio + i) * part
                    r_ref[8 + i : 9 + i, shard * part : (shard + 1) * part] = bias_ref[:, at : at + part]
            v_ref[0] = r_ref[...].T
            put_relative(place, v_ref.at[0], v_ref.at[1])
            both = jnp.concatenate([v_ref[1], jnp.zeros((width, group - 128), F32)], axis=1)
            put_halves(both.astype(BF), send_ref, keep_ref)

    blocks = weight_blocks(width, group, groups // 2)
    return grid_call(
        body,
        "last_weight",
        (groups,),
        (ids,),
        [
            (gqkv, (rows, group), lambda j, ids: (0, jnp.minimum(j, first - 1))),
            whole(tokens),
            whole(vg_a),
            whole(vg_b),
            whole(vg_attn),
            whole(vg_ffn),
            whole(gbias_in),
        ],
        [blocks, blocks],
        [pltpu.VMEM((width, rows), BF)] * 2
        + [pltpu.VMEM((128, width), F32), pltpu.VMEM((2, width, 128), F32)],
        2 * rows * width * width,
    )


def tokens_backward(gqkv_a, gqkv_b, gattn, ids, bufs):
    rows, width = gattn.shape
    group = 256
    span_a, span_b = gqkv_a.shape[1] // 3, gqkv_b.shape[1] // 3

    def body(ids_ref, ga_hbm, gb_hbm, gattn_ref, b0, b1, b2, b3, gx_ref, w_ref, g_ref, sems, more):
        copies = piece_copies(Place(ids_ref), (b0, b1, b2, b3), w_ref, sems, width // 8, False)
        for i in range(3):
            for at, span, source in ((0, span_a, ga_hbm), (span_a, span_b, gb_hbm)):
                copies.append(
                    pltpu.make_async_copy(
                        source.at[:, i * span : (i + 1) * span],
                        g_ref.at[:, i * width + at : i * width + at + span],
                        more.at[2 * i + at // span_a],
                    )
                )
        for copy in copies:
            copy.start()
        for copy in copies:
            copy.wait()
        for g in range(width // group):
            cols = slice(g * group, (g + 1) * group)
            gx_ref[:, cols] = gattn_ref[:, cols] + dot_nt(g_ref[...], w_ref[cols, : 3 * width])

    return call(
        body,
        "tokens_back",
        [(ids, "s"), (gqkv_a, "a"), (gqkv_b, "a"), (gattn, "v")] + [(b, "a") for b in bufs],
        [struct((rows, width), F32)],
        [
            pltpu.VMEM((width, 3 * width + 128), BF),
            pltpu.VMEM((rows, 3 * width), BF),
            pltpu.SemaphoreType.DMA((16,)),
            pltpu.SemaphoreType.DMA((6,)),
        ],
        2 * rows * width * 3 * width,
    )[0]


def norm_parts(token_rows, gain_vec, shift_vec):
    row_mean = jnp.mean(token_rows, -1, keepdims=True)
    centred = token_rows - row_mean
    inverse = lax.rsqrt(jnp.mean(centred * centred, -1, keepdims=True) + norm_eps)
    normed = centred * inverse
    return (normed * gain_vec + shift_vec, normed, inverse)


def plain_norm_back(grad_out, normed, inverse, gain_vec):
    grad_gain = jnp.sum(grad_out * normed, 0)
    grad_shift = jnp.sum(grad_out, 0)
    scaled = grad_out * gain_vec
    grad_in = inverse * (
        scaled
        - jnp.mean(scaled, -1, keepdims=True)
        - normed * jnp.mean(scaled * normed, -1, keepdims=True)
    )
    return (grad_in, grad_gain, grad_shift)


def attention_scores(query_rows, key_rows, key_valid):
    scores = jnp.einsum(
        "sqhd,skhd->shqk", query_rows, key_rows, preferred_element_type=jnp.float32
    ) * HEAD ** (-0.5)
    return jnp.where(key_valid[:, None, None, :], scores, -1000000000.0)


def forward(tokens, lengths, weights):
    (
        w_qkv,
        bias_query,
        bias_value,
        w_out,
        bias_out,
        gain_attn,
        shift_attn,
        w_in,
        bias_in,
        w_down,
        bias_down,
        gain_ffn,
        shift_ffn,
    ) = weights
    sentences, length, model_width = tokens.shape
    head_count = model_width // HEAD
    token_rows = tokens.reshape(sentences * length, model_width)
    bias_qkv = jnp.concatenate([bias_query, jnp.zeros_like(bias_query), bias_value]).astype(
        jnp.float32
    )
    packed = (jnp.dot(token_rows, w_qkv, preferred_element_type=jnp.float32) + bias_qkv).astype(
        jnp.bfloat16
    )
    packed = packed.reshape(sentences, length, 3, head_count, HEAD)
    query_rows = packed[:, :, 0]
    key_rows = packed[:, :, 1]
    value_rows = packed[:, :, 2]
    key_valid = jnp.arange(length)[None, :] < lengths[:, None]
    scores = attention_scores(query_rows, key_rows, key_valid)
    row_max = jnp.max(scores, -1, keepdims=True)
    log_total = row_max + jnp.log(jnp.sum(jnp.exp(scores - row_max), -1, keepdims=True))
    attn_probs = jnp.exp(scores - log_total)
    context = jnp.einsum(
        "shqk,skhd->sqhd",
        attn_probs.astype(jnp.bfloat16),
        value_rows,
        preferred_element_type=jnp.float32,
    )
    context = context.reshape(sentences * length, model_width).astype(jnp.bfloat16)
    attn_out = jnp.dot(context, w_out, preferred_element_type=jnp.float32) + bias_out.astype(
        jnp.float32
    )
    hidden, normed_attn, inverse_attn = norm_parts(
        token_rows.astype(jnp.float32) + attn_out,
        gain_attn.astype(jnp.float32),
        shift_attn.astype(jnp.float32),
    )
    hidden_low = hidden.astype(jnp.bfloat16)
    up_rows = jnp.dot(hidden_low, w_in, preferred_element_type=jnp.float32) + bias_in.astype(
        jnp.float32
    )
    active = jax.nn.gelu(up_rows, approximate=False).astype(jnp.bfloat16)
    ffn_out = jnp.dot(active, w_down, preferred_element_type=jnp.float32) + bias_down.astype(
        jnp.float32
    )
    output, normed_ffn, inverse_ffn = norm_parts(
        hidden + ffn_out, gain_ffn.astype(jnp.float32), shift_ffn.astype(jnp.float32)
    )
    valid_mask = key_valid.astype(jnp.float32)
    pooled = jnp.sum(
        output.reshape(sentences, length, model_width) * valid_mask[:, :, None], 1
    ) / lengths[:, None].astype(jnp.float32)
    kept = (
        key_valid,
        query_rows,
        key_rows,
        value_rows,
        log_total,
        context,
        normed_attn,
        inverse_attn,
        hidden_low,
        up_rows,
        active,
        normed_ffn,
        inverse_ffn,
    )
    return (pooled, kept)


def backward(tokens, lengths, pooled_grad, weights, kept):
    (
        w_qkv,
        bias_query,
        bias_value,
        w_out,
        bias_out,
        gain_attn,
        shift_attn,
        w_in,
        bias_in,
        w_down,
        bias_down,
        gain_ffn,
        shift_ffn,
    ) = weights
    (
        key_valid,
        query_rows,
        key_rows,
        value_rows,
        log_total,
        context,
        normed_attn,
        inverse_attn,
        hidden_low,
        up_rows,
        active,
        normed_ffn,
        inverse_ffn,
    ) = kept
    sentences, length, model_width = tokens.shape
    head_count = model_width // HEAD
    token_rows = tokens.reshape(sentences * length, model_width)
    valid_mask = key_valid.astype(jnp.float32)
    per_sentence = pooled_grad / lengths[:, None].astype(jnp.float32)
    grad_output = (valid_mask[:, :, None] * per_sentence[:, None, :]).reshape(
        sentences * length, model_width
    )
    grad_res_ffn, grad_gain_ffn, grad_shift_ffn = plain_norm_back(
        grad_output, normed_ffn, inverse_ffn, gain_ffn.astype(jnp.float32)
    )
    grad_ffn_low = grad_res_ffn.astype(jnp.bfloat16)
    grad_bias_down = jnp.sum(grad_ffn_low.astype(jnp.float32), 0)
    grad_w_down = jnp.einsum("tf,td->fd", active, grad_ffn_low, preferred_element_type=jnp.float32)
    grad_active = jnp.einsum("td,fd->tf", grad_ffn_low, w_down, preferred_element_type=jnp.float32)
    gelu_value, gelu_pull = jax.vjp(partial(jax.nn.gelu, approximate=False), up_rows)
    grad_up = gelu_pull(grad_active)[0].astype(jnp.bfloat16)
    grad_bias_in = jnp.sum(grad_up.astype(jnp.float32), 0)
    grad_w_in = jnp.einsum("td,tf->df", hidden_low, grad_up, preferred_element_type=jnp.float32)
    grad_hidden = (
        jnp.einsum("tf,df->td", grad_up, w_in, preferred_element_type=jnp.float32) + grad_res_ffn
    )
    grad_res_attn, grad_gain_attn, grad_shift_attn = plain_norm_back(
        grad_hidden, normed_attn, inverse_attn, gain_attn.astype(jnp.float32)
    )
    grad_attn_low = grad_res_attn.astype(jnp.bfloat16)
    grad_bias_out = jnp.sum(grad_attn_low.astype(jnp.float32), 0)
    grad_w_out = jnp.einsum("tc,td->cd", context, grad_attn_low, preferred_element_type=jnp.float32)
    grad_context = jnp.einsum("td,cd->tc", grad_attn_low, w_out, preferred_element_type=jnp.float32)
    grad_context = grad_context.astype(jnp.bfloat16).reshape(sentences, length, head_count, HEAD)
    scores = attention_scores(query_rows, key_rows, key_valid)
    attn_probs = jnp.exp(scores - log_total)
    grad_probs = jnp.einsum(
        "sqhd,skhd->shqk", grad_context, value_rows, preferred_element_type=jnp.float32
    )
    grad_values = jnp.einsum(
        "shqk,sqhd->skhd",
        attn_probs.astype(jnp.bfloat16),
        grad_context,
        preferred_element_type=jnp.float32,
    )
    grad_scores = (
        attn_probs * (grad_probs - jnp.sum(grad_probs * attn_probs, -1, keepdims=True))
    ).astype(jnp.bfloat16)
    grad_queries = jnp.einsum(
        "shqk,skhd->sqhd", grad_scores, key_rows, preferred_element_type=jnp.float32
    ) * HEAD ** (-0.5)
    grad_keys = jnp.einsum(
        "shqk,sqhd->skhd", grad_scores, query_rows, preferred_element_type=jnp.float32
    ) * HEAD ** (-0.5)
    grad_qkv = jnp.stack([grad_queries, grad_keys, grad_values], 2)
    grad_qkv = grad_qkv.reshape(sentences * length, 3 * model_width).astype(jnp.bfloat16)
    qkv_sums = jnp.sum(grad_qkv.astype(jnp.float32), 0)
    grad_bias_query = qkv_sums[:model_width]
    grad_bias_value = qkv_sums[2 * model_width :]
    grad_w_qkv = jnp.einsum("td,tc->dc", token_rows, grad_qkv, preferred_element_type=jnp.float32)
    grad_tokens = (
        jnp.einsum("tc,dc->td", grad_qkv, w_qkv, preferred_element_type=jnp.float32) + grad_res_attn
    )
    grad_tokens = grad_tokens.reshape(sentences, length, model_width)
    grad_terms = (
        grad_w_qkv,
        grad_bias_query,
        grad_bias_value,
        grad_w_out,
        grad_bias_out,
        grad_gain_attn,
        grad_shift_attn,
        grad_w_in,
        grad_bias_in,
        grad_w_down,
        grad_bias_down,
        grad_gain_ffn,
        grad_shift_ffn,
    )
    return (grad_terms, grad_tokens)


def on_device(
    tokens,
    lengths,
    pooled_grad,
    w_qkv,
    bias_query,
    bias_value,
    w_out,
    bias_out,
    gain_attn,
    shift_attn,
    w_in,
    bias_in,
    w_down,
    bias_down,
    gain_ffn,
    shift_ffn,
):
    weights = (
        lax.all_gather(w_qkv, "fsdp", axis=0, tiled=True),
        lax.all_gather(bias_query, "fsdp", axis=0, tiled=True),
        lax.all_gather(bias_value, "fsdp", axis=0, tiled=True),
        lax.all_gather(w_out, "fsdp", axis=0, tiled=True),
        lax.all_gather(bias_out, "fsdp", axis=0, tiled=True),
        lax.all_gather(gain_attn, "fsdp", axis=0, tiled=True),
        lax.all_gather(shift_attn, "fsdp", axis=0, tiled=True),
        lax.all_gather(w_in, "fsdp", axis=0, tiled=True),
        lax.all_gather(bias_in, "fsdp", axis=0, tiled=True),
        lax.all_gather(w_down, "fsdp", axis=0, tiled=True),
        lax.all_gather(bias_down, "fsdp", axis=0, tiled=True),
        lax.all_gather(gain_ffn, "fsdp", axis=0, tiled=True),
        lax.all_gather(shift_ffn, "fsdp", axis=0, tiled=True),
    )
    pooled, kept = forward(tokens, lengths, weights)
    grad_terms, grad_tokens = backward(tokens, lengths, pooled_grad, weights, kept)
    (
        grad_w_qkv,
        grad_bias_query,
        grad_bias_value,
        grad_w_out,
        grad_bias_out,
        grad_gain_attn,
        grad_shift_attn,
        grad_w_in,
        grad_bias_in,
        grad_w_down,
        grad_bias_down,
        grad_gain_ffn,
        grad_shift_ffn,
    ) = grad_terms
    shares = (
        lax.psum_scatter(grad_w_qkv, "fsdp", scatter_dimension=0, tiled=True),
        lax.psum_scatter(grad_bias_query, "fsdp", scatter_dimension=0, tiled=True),
        lax.psum_scatter(grad_bias_value, "fsdp", scatter_dimension=0, tiled=True),
        lax.psum_scatter(grad_w_out, "fsdp", scatter_dimension=0, tiled=True),
        lax.psum_scatter(grad_bias_out, "fsdp", scatter_dimension=0, tiled=True),
        lax.psum_scatter(grad_gain_attn, "fsdp", scatter_dimension=0, tiled=True),
        lax.psum_scatter(grad_shift_attn, "fsdp", scatter_dimension=0, tiled=True),
        lax.psum_scatter(grad_w_in, "fsdp", scatter_dimension=0, tiled=True),
        lax.psum_scatter(grad_bias_in, "fsdp", scatter_dimension=0, tiled=True),
        lax.psum_scatter(grad_w_down, "fsdp", scatter_dimension=0, tiled=True),
        lax.psum_scatter(grad_bias_down, "fsdp", scatter_dimension=0, tiled=True),
        lax.psum_scatter(grad_gain_ffn, "fsdp", scatter_dimension=0, tiled=True),
        lax.psum_scatter(grad_shift_ffn, "fsdp", scatter_dimension=0, tiled=True),
    )
    (
        share_w_qkv,
        share_bias_query,
        share_bias_value,
        share_w_out,
        share_bias_out,
        share_gain_attn,
        share_shift_attn,
        share_w_in,
        share_bias_in,
        share_w_down,
        share_bias_down,
        share_gain_ffn,
        share_shift_ffn,
    ) = shares
    totals = (
        lax.psum(share_w_qkv.astype(jnp.bfloat16), "dp").astype(jnp.float32),
        lax.psum(share_bias_query.astype(jnp.bfloat16), "dp").astype(jnp.float32),
        lax.psum(share_bias_value.astype(jnp.bfloat16), "dp").astype(jnp.float32),
        lax.psum(share_w_out.astype(jnp.bfloat16), "dp").astype(jnp.float32),
        lax.psum(share_bias_out.astype(jnp.bfloat16), "dp").astype(jnp.float32),
        lax.psum(share_gain_attn.astype(jnp.bfloat16), "dp").astype(jnp.float32),
        lax.psum(share_shift_attn.astype(jnp.bfloat16), "dp").astype(jnp.float32),
        lax.psum(share_w_in.astype(jnp.bfloat16), "dp").astype(jnp.float32),
        lax.psum(share_bias_in.astype(jnp.bfloat16), "dp").astype(jnp.float32),
        lax.psum(share_w_down.astype(jnp.bfloat16), "dp").astype(jnp.float32),
        lax.psum(share_bias_down.astype(jnp.bfloat16), "dp").astype(jnp.float32),
        lax.psum(share_gain_ffn.astype(jnp.bfloat16), "dp").astype(jnp.float32),
        lax.psum(share_shift_ffn.astype(jnp.bfloat16), "dp").astype(jnp.float32),
    )
    return (
        pooled,
        grad_tokens,
        totals[0],
        totals[1],
        totals[2],
        totals[3],
        totals[4],
        totals[5],
        totals[6],
        totals[7],
        totals[8],
        totals[9],
        totals[10],
        totals[11],
        totals[12],
    )


def swap(array, axis, bits):
    pairs = [(i, i ^ bits) for i in range(lax.axis_size(axis))]
    return lax.ppermute(array, axis, pairs)


def hold(value, *after):
    return lax.optimization_barrier((value, *after))[0]


def gather_z(piece, *after):
    return jnp.stack([hold(piece, *after)] + [swap(piece, "fsdp", 2 * k) for k in range(1, 4)])


def add(*terms):
    total = terms[0].astype(F32)
    for term in terms[1:]:
        total = total + term.astype(F32)
    return total.astype(BF)


def sum_core(send, keep, *after):
    return add(hold(keep, *after), swap(send, "dp", 1))


def sum_x(total, *after):
    return add(hold(total[0], *after), swap(total[1], "dp", 2))


def sum_y(total, *after):
    return add(hold(total[0], *after), swap(total[1], "fsdp", 1))


def sum_z(total, *after):
    return add(hold(total[0], *after), *[swap(total[k], "fsdp", 2 * k) for k in range(1, 4)])


def in_order_parts(own, other, bit):
    return jnp.where(bit == 0, own, other), jnp.where(bit == 0, other, own)


def in_order(own, other, bit, axis):
    first = jnp.where(bit == 0, own, other)
    second = jnp.where(bit == 0, other, own)
    return jnp.concatenate([first, second], axis=axis)


def share_core(own, c):
    return in_order(own, swap(own, "dp", 1), c, 0).astype(F32)


def on_device_split(
    tokens,
    lengths,
    pooled_grad,
    w_qkv,
    bias_query,
    bias_value,
    w_out,
    bias_out,
    gain_attn,
    shift_attn,
    w_in,
    bias_in,
    w_down,
    bias_down,
    gain_ffn,
    shift_ffn,
):
    sentences, length, width = tokens.shape
    rows = sentences * length
    wide = w_in.shape[1]
    part = width // 8
    dp, fsdp = lax.axis_index("dp"), lax.axis_index("fsdp")
    x, c = dp // 2, dp % 2
    ids = jnp.stack([fsdp // 2, fsdp % 2, x, c]).astype(jnp.int32)
    token_rows = tokens.reshape(rows, width)

    vectors = jnp.stack(
        [bias_query, bias_value, bias_out, gain_attn, shift_attn, bias_down, gain_ffn, shift_ffn]
    )
    vectors = jnp.concatenate([vectors, bias_in.reshape(wide // width, part)], 0)
    vectors = jnp.pad(vectors.T, ((0, 0), (0, 128 - vectors.shape[0])))
    first = jnp.concatenate([w_qkv, vectors], 1)
    second = jnp.concatenate([w_out, w_in], 1)
    half = part // 2
    first = lax.dynamic_slice(first, (c * half, 0), (half, first.shape[1]))
    span = second.shape[1] // 2
    second = lax.dynamic_slice(second, (c * half, x * span), (half, span))
    third = lax.dynamic_slice(w_down, (c * (w_down.shape[0] // 2), 0), (w_down.shape[0] // 2, width))

    near1 = gather_z(first)
    near2 = gather_z(hold(second, near1))
    far1 = hold(swap(near1, "fsdp", 1), near2)
    bufs1 = [near1, far1, swap(near1, "dp", 1), swap(far1, "dp", 1)]
    side2 = swap(near2, "dp", 2)
    qkv, vec = qkv_forward(hold(token_rows, near2), ids, bufs1)
    far2 = hold(swap(near2, "fsdp", 1), vec)
    context, lse = attend_forward(hold(qkv, side2), lengths, sentences, length)
    near3 = gather_z(hold(third, near2), context)
    side2 = hold(side2, context)
    far3 = swap(near3, "fsdp", 1)
    mine2 = [near2, far2, side2, swap(far2, "dp", 2)]
    bufs2 = mine2 + [swap(hold(m, context), "dp", 1) for m in mine2]
    ratio = wide // width
    bias_up = vec[8 : 8 + ratio].reshape(ratio, 8, part).transpose(1, 0, 2).reshape(1, wide)
    normed, inverse, low, active, slope = up_forward(
        context, token_rows, vec, bias_up, ids, bufs2, length
    )
    far3 = hold(far3, low)
    bufs3 = [near3, far3, swap(near3, "dp", 1), swap(far3, "dp", 1)]
    pooled, vg_ffn, send3, keep3, gup, gbias_in, gres = down_and_back(
        active, slope, normed, vec, lengths, pooled_grad, ids, bufs3, sentences, length
    )
    send2, keep2, gctx, vg_attn, gattn, gattn_low = up_and_back(
        low, gup, gres, normed, inverse, vec, ids, bufs2, length
    )
    sums3 = sum_core(send3, keep3, gctx)
    sums2 = sum_core(send2, keep2, sums3)
    pairs = width // 128
    most = pairs * 2 // 3
    gqkv_a, vg_a = attend_backward(
        qkv, hold(gctx, sums3, sums2), lse, lengths, sentences, length, 0, most, "attention_back"
    )
    send_a, keep_a = attend_weight(gqkv_a, token_rows, context, gattn_low, ids)
    sums2 = sum_x(sums2, keep_a)
    sums3 = sum_y(sums3[0], keep_a)
    sums_a = sum_core(hold(send_a, sums2, sums3), keep_a)
    gqkv_b, vg_b = attend_backward(
        qkv, hold(gctx, sums_a), lse, lengths, sentences, length, most, pairs, "attention_back_rest"
    )
    send_b, keep_b = last_weight(gqkv_b, token_rows, vg_a, vg_b, vg_attn, vg_ffn, gbias_in, ids)
    sums2 = sum_y(sums2, keep_b)
    sums3 = sum_z(sums3, keep_b)
    sums_a = sum_x(sums_a, keep_b)
    sums_b = sum_core(hold(send_b, sums_a), keep_b)
    gtokens = tokens_backward(gqkv_a, hold(gqkv_b, sums_b, sums2, sums3), gattn, ids, bufs1)
    sums2 = sum_z(sums2, gtokens)
    sums_b = sum_x(sums_b, sums2)
    sums_a = sum_y(sums_a, sums2)
    sums3 = add(hold(sums3, sums2), swap(sums3, "dp", 2))
    sums_a, sums2, sums3, sums_b = lax.optimization_barrier((sums_a, sums2, sums3, sums_b))
    sums_b = sum_y(sums_b)
    g_in = in_order(sums2, swap(sums2, "dp", 2), x, 1)
    sums_a, sums3, sums_b, g_in = lax.optimization_barrier((sums_a, sums3, sums_b, g_in))
    g_down = share_core(sums3, c).T
    g_in = share_core(g_in, c)
    sums = sum_z(jnp.concatenate([sums_a, sums_b], 2))
    wide_a = sums_a.shape[2]
    sums, other = in_order_parts(sums, swap(sums, "dp", 2), x)
    g_a = share_core(jnp.concatenate([sums[:, :wide_a], other[:, :wide_a]], 1), c)
    g_b = share_core(jnp.concatenate([sums[:, wide_a:], other[:, wide_a:]], 1), c)
    gtokens = gtokens.reshape(sentences, length, width)
    cut_a, cut_b = most * 128, (pairs - most) * 128
    g_qkv = [
        g[:, i * cut : (i + 1) * cut] for i in range(3) for g, cut in ((g_a, cut_a), (g_b, cut_b))
    ]
    g_vec = g_b[:, 3 * cut_b : 3 * cut_b + 8 + ratio].T
    return (
        pooled,
        gtokens,
        jnp.concatenate(g_qkv, 1),
        g_vec[0],
        g_vec[1],
        g_a[:, 3 * cut_a :],
        g_vec[2],
        g_vec[3],
        g_vec[4],
        g_in,
        g_vec[8:].reshape(wide // 8),
        g_down,
        g_vec[5],
        g_vec[6],
        g_vec[7],
    )


def solution(mesh):
    placed = (
        P(("dp", "fsdp"), None, None),
        P(("dp", "fsdp")),
        P(("dp", "fsdp"), None),
        P("fsdp", None),
        P("fsdp"),
        P("fsdp"),
        P("fsdp", None),
        P("fsdp"),
        P("fsdp"),
        P("fsdp"),
        P("fsdp", None),
        P("fsdp"),
        P("fsdp", None),
        P("fsdp"),
        P("fsdp"),
        P("fsdp"),
    )
    body = on_device_split if mesh.shape["fsdp"] == 8 and mesh.shape["dp"] == 4 else on_device
    return jax.shard_map(
        body,
        mesh=mesh,
        in_specs=placed,
        out_specs=(
            P(("dp", "fsdp"), None),
            P(("dp", "fsdp"), None, None),
            P("fsdp", None),
            P("fsdp"),
            P("fsdp"),
            P("fsdp", None),
            P("fsdp"),
            P("fsdp"),
            P("fsdp"),
            P("fsdp", None),
            P("fsdp"),
            P("fsdp", None),
            P("fsdp"),
            P("fsdp"),
            P("fsdp"),
        ),
        check_vma=False,
    )
```

```python
from functools import partial

import jax
import jax.numpy as jnp
from jax import lax
from jax.experimental import pallas as pl
from jax.experimental.pallas import tpu as pltpu
from jax.sharding import PartitionSpec as P

norm_eps = 1e-06

HEAD = 64
NORM_EPS = 1e-06
BF = jnp.bfloat16
F32 = jnp.float32
VMEM_LIMIT = 60 * 1024 * 1024


def dot(a, b):
    return lax.dot_general(a, b, (((1,), (0,)), ((), ())), preferred_element_type=F32)


def dot_nt(a, b):
    return lax.dot_general(a, b, (((1,), (1,)), ((), ())), preferred_element_type=F32)


def dot_tn(a, b):
    return lax.dot_general(a, b, (((0,), (0,)), ((), ())), preferred_element_type=F32)


def aligned(value, step):
    return pl.multiple_of(value, step)


class Place:
    def __init__(self, ids_ref):
        self.z, self.y, self.x, self.c = ids_ref[0], ids_ref[1], ids_ref[2], ids_ref[3]

    def shard(self, k, yy):
        return lax.bitwise_xor(self.z, k) * 2 + lax.bitwise_xor(self.y, yy)


def piece_copies(place, bufs, dst, sems, shard_rows, split_x):
    half = shard_rows // 2
    copies = []
    at = 0
    for cc in range(2):
        core = lax.bitwise_xor(place.c, cc)
        for xx in range(2 if split_x else 1):
            for yy in range(2):
                buf = bufs[at]
                at += 1
                width = buf.shape[-1]
                for k in range(4):
                    row = aligned(place.shard(k, yy) * shard_rows + core * half, 16)
                    if split_x:
                        col = aligned(lax.bitwise_xor(place.x, xx) * width, 128)
                        target = dst.at[pl.ds(row, half), pl.ds(col, width)]
                    else:
                        target = dst.at[pl.ds(row, half), :]
                    copies.append(
                        pltpu.make_async_copy(buf.at[k], target, sems.at[len(copies)])
                    )
    return copies


def call(body, name, ins, outs, scratch, flops, transcendentals=0):
    spaces = {
        "s": pl.BlockSpec(memory_space=pltpu.SMEM),
        "v": pl.BlockSpec(memory_space=pltpu.VMEM),
        "a": pl.BlockSpec(memory_space=pl.ANY),
    }
    moved = sum(a.size * a.dtype.itemsize for a, _ in ins) + sum(
        o.size * o.dtype.itemsize for o in outs
    )
    return pl.pallas_call(
        body,
        name=name,
        out_shape=tuple(outs),
        in_specs=[spaces[s] for _, s in ins],
        out_specs=tuple(spaces["v"] for _ in outs),
        scratch_shapes=scratch,
        compiler_params=pltpu.CompilerParams(vmem_limit_bytes=VMEM_LIMIT),
        cost_estimate=pl.CostEstimate(flops=1, transcendentals=0, bytes_accessed=1),
    )(*[a for a, _ in ins])


def struct(shape, dtype):
    return jax.ShapeDtypeStruct(shape, dtype)


def two_heads(block):
    low = lax.broadcasted_iota(jnp.int32, block.shape, 1) < HEAD
    zero = jnp.zeros_like(block)
    return jnp.concatenate([jnp.where(low, block, zero), jnp.where(low, zero, block)], axis=0)


def one_of_two(stacked):
    rows = stacked.shape[0] // 2
    low = lax.broadcasted_iota(jnp.int32, (rows, stacked.shape[1]), 1) < HEAD
    return jnp.where(low, stacked[:rows], stacked[rows:])


def masked_scores(query, keys2, count, length):
    scores = dot_nt(query, keys2)
    slot = lax.broadcasted_iota(jnp.int32, scores.shape, 1)
    slot = jnp.where(slot >= length, slot - length, slot)
    return jnp.where(slot < count, scores, -1000000000.0)


def halves(stat_a, stat_b, length):
    rows = stat_a.shape[0]
    return jnp.concatenate(
        [jnp.broadcast_to(stat_a, (rows, length)), jnp.broadcast_to(stat_b, (rows, length))], axis=1
    )


def layer_norm(v):
    centred = v - jnp.mean(v, -1, keepdims=True)
    inverse = lax.rsqrt(jnp.mean(centred * centred, -1, keepdims=True) + NORM_EPS)
    return centred * inverse, inverse


def norm_back(grad, normed, inverse, gain):
    scaled = grad * gain
    return inverse * (
        scaled
        - jnp.mean(scaled, -1, keepdims=True)
        - normed * jnp.mean(scaled * normed, -1, keepdims=True)
    )


def row(vec_ref, at):
    return vec_ref[at : at + 1, :]


def grid_call(body, name, grid, scalars, ins, outs, scratch, flops, transcendentals=0):
    def spec(block, index):
        if block is None:
            return pl.BlockSpec(memory_space=pl.ANY)
        return pl.BlockSpec(block, index)

    moved = sum(a.size * a.dtype.itemsize for a, _, _ in ins) + sum(
        o.size * o.dtype.itemsize for o, _, _ in outs
    )
    return pl.pallas_call(
        body,
        name=name,
        out_shape=tuple(o for o, _, _ in outs),
        grid_spec=pltpu.PrefetchScalarGridSpec(
            num_scalar_prefetch=len(scalars),
            grid=grid,
            in_specs=[spec(b, i) for _, b, i in ins],
            out_specs=tuple(spec(b, i) for _, b, i in outs),
            scratch_shapes=scratch,
        ),
        compiler_params=pltpu.CompilerParams(
            vmem_limit_bytes=VMEM_LIMIT, dimension_semantics=("arbitrary",) * len(grid)
        ),
        cost_estimate=pl.CostEstimate(flops=1, transcendentals=0, bytes_accessed=1),
    )(*scalars, *[a for a, _, _ in ins])


def whole(array):
    return (array, array.shape, lambda *_: (0,) * array.ndim)


def left(array):
    return (array, None, None)


def qkv_forward(tokens, ids, bufs):
    rows, width = tokens.shape
    group = 256

    def body(ids_ref, x_ref, b0, b1, b2, b3, qkv_hbm, vec_ref, w_ref, out_ref, sems, more):
        place = Place(ids_ref)
        copies = piece_copies(place, (b0, b1, b2, b3), w_ref, sems, width // 8, False)
        for copy in copies:
            copy.start()
        for copy in copies:
            copy.wait()
        vec_ref[...] = w_ref[:, 3 * width :].astype(F32).T[: vec_ref.shape[0]]
        x = x_ref[...]
        outs = []
        for part in range(3):
            for g in range(width // group):
                col = part * width + g * group
                y = dot(x, w_ref[:, col : col + group])
                if part != 1:
                    bias = vec_ref[part // 2 : part // 2 + 1, g * group : (g + 1) * group]
                    y = y + bias
                out_ref[:, col : col + group] = y.astype(BF)
            here = slice(part * width, (part + 1) * width)
            outs.append(
                pltpu.make_async_copy(out_ref.at[:, here], qkv_hbm.at[:, here], more.at[part])
            )
            outs[-1].start()
        for out in outs:
            out.wait()

    return grid_call(
        body,
        "qkv",
        (1,),
        (ids,),
        [whole(tokens)] + [left(b) for b in bufs],
        [left(struct((rows, 3 * width), BF)), whole(struct((16, width), F32))],
        [
            pltpu.VMEM((width, 3 * width + 128), BF),
            pltpu.VMEM((rows, 3 * width), BF),
            pltpu.SemaphoreType.DMA((16,)),
            pltpu.SemaphoreType.DMA((3,)),
        ],
        2 * rows * width * 3 * width,
    )


def attend_forward(qkv, counts, sentences, length):
    rows, width = qkv.shape[0], qkv.shape[1] // 3
    pairs = width // 128

    def body(counts_ref, qkv_ref, ctx_ref, lse_ref):
        count = counts_ref[pl.program_id(0)]
        lane = lax.broadcasted_iota(jnp.int32, (length, 128), 1)
        lse_all = jnp.zeros((length, 128), F32)
        for p in range(pairs):
            query = qkv_ref[:, p * 128 : (p + 1) * 128] * jnp.asarray(HEAD**-0.5, BF)
            keys2 = two_heads(qkv_ref[:, width + p * 128 : width + (p + 1) * 128])
            values2 = two_heads(qkv_ref[:, 2 * width + p * 128 : 2 * width + (p + 1) * 128])
            scores = masked_scores(query, keys2, count, length)
            a, b = scores[:, :length], scores[:, length:]
            max_a = jnp.max(a, -1, keepdims=True)
            max_b = jnp.max(b, -1, keepdims=True)
            e_a, e_b = jnp.exp(a - max_a), jnp.exp(b - max_b)
            sum_a = jnp.sum(e_a, -1, keepdims=True)
            sum_b = jnp.sum(e_b, -1, keepdims=True)
            lse_all = jnp.where(lane == 2 * p, max_a + jnp.log(sum_a), lse_all)
            lse_all = jnp.where(lane == 2 * p + 1, max_b + jnp.log(sum_b), lse_all)
            probs = jnp.concatenate([e_a * (1.0 / sum_a), e_b * (1.0 / sum_b)], axis=1).astype(BF)
            ctx_ref[:, p * 128 : (p + 1) * 128] = dot(probs, values2).astype(BF)
        lse_ref[...] = lse_all

    def by_rows(array):
        return (array, (length, array.shape[1]), lambda s, counts: (s, 0))

    return grid_call(
        body,
        "attention",
        (sentences,),
        (counts,),
        [by_rows(qkv)],
        [by_rows(struct((rows, width), BF)), by_rows(struct((rows, 128), F32))],
        [],
        8 * rows * length * width,
        rows * length * width // HEAD,
    )


CHUNK = 128


def up_forward(context, tokens, vec, bias_in, ids, bufs, length):
    rows, width = tokens.shape
    wide = bias_in.shape[1]
    group, block = 256, 512
    steps = wide // block

    def body(ids_ref, ctx_ref, x_ref, vec_ref, bin_ref, *rest):
        bufs_ref = rest[: len(bufs)]
        act_ref, slope_ref, n_hbm, inv_hbm, low_hbm, w_ref, n_ref, inv_ref, low_ref, sems, more = rest[len(bufs) :]
        step = pl.program_id(0)
        outs = [
            pltpu.make_async_copy(a, b, more.at[i])
            for i, (a, b) in enumerate(((n_ref, n_hbm), (inv_ref, inv_hbm), (low_ref, low_hbm)))
        ]

        @pl.when(step == 0)
        def _():
            copies = piece_copies(Place(ids_ref), bufs_ref, w_ref, sems, width // 8, True)
            for copy in copies:
                copy.start()
            for copy in copies:
                copy.wait()
            for g in range(width // group):
                cols = slice(g * group, (g + 1) * group)
                n_ref[:, cols] = dot(ctx_ref[...], w_ref[:, cols])

            def norm_rows(i, carry):
                here = pl.ds(aligned(i * CHUNK, CHUNK), CHUNK)
                v = x_ref[here, :].astype(F32) + (n_ref[here, :] + row(vec_ref, 2))
                normed, inverse = layer_norm(v)
                n_ref[here, :] = normed
                inv_ref[here, :] = jnp.broadcast_to(inverse, (CHUNK, 128))
                low_ref[here, :] = (normed * row(vec_ref, 3) + row(vec_ref, 4)).astype(BF)
                return carry

            lax.fori_loop(0, rows // CHUNK, norm_rows, 0)
            for out in outs:
                out.start()

        for g in range(block // group):
            cols = slice(g * group, (g + 1) * group)
            here = pl.ds(aligned(width + step * block + g * group, 128), group)
            u = dot(low_ref[...], w_ref[:, here]) + bin_ref[:, cols]
            cdf = 0.5 * (1.0 + lax.erf(u * (0.5**0.5)))
            pdf = jnp.exp(-0.5 * u * u) * 0.3989422804014327
            act_ref[:, cols] = (u * cdf).astype(BF)
            slope_ref[:, cols] = (cdf + u * pdf).astype(BF)

        @pl.when(step == steps - 1)
        def _():
            for out in outs:
                out.wait()

    active, slope, normed, inverse, low = grid_call(
        body,
        "out_norm_up",
        (steps,),
        (ids,),
        [whole(context), whole(tokens), whole(vec), (bias_in, (1, block), lambda j, ids: (0, j))]
        + [left(b) for b in bufs],
        [
            (struct((rows, wide), BF), (rows, block), lambda j, ids: (0, j)),
            (struct((rows, wide), BF), (rows, block), lambda j, ids: (0, j)),
            left(struct((rows, width), F32)),
            left(struct((rows, 128), F32)),
            left(struct((rows, width), BF)),
        ],
        [
            pltpu.VMEM((width, width + wide), BF),
            pltpu.VMEM((rows, width), F32),
            pltpu.VMEM((rows, 128), F32),
            pltpu.VMEM((rows, width), BF),
            pltpu.SemaphoreType.DMA((32,)),
            pltpu.SemaphoreType.DMA((3,)),
        ],
        2 * rows * width * (width + wide),
    )
    return normed, inverse, low, active, slope


def relative(ids, step):
    return lax.bitwise_xor(ids[0] * 2 + ids[1], step)


def put_relative(place, source, dst):
    half = source.shape[0] // 16
    for cc in range(2):
        core = lax.bitwise_xor(place.c, cc)
        for yy in range(2):
            for k in range(4):
                at = ((cc * 2 + yy) * 4 + k) * half
                here = aligned(place.shard(k, yy) * 2 * half + core * half, 16)
                dst[at : at + half, :] = source[pl.ds(here, half), :]


def natural_copies(place, bufs, dst, sems):
    half = bufs[0].shape[1]
    copies = []
    for cc in range(2):
        for yy in range(2):
            for k in range(4):
                at = place.shard(k, yy) * 2 * half + lax.bitwise_xor(place.c, cc) * half
                copies.append(
                    pltpu.make_async_copy(
                        bufs[2 * cc + yy].at[k], dst.at[pl.ds(aligned(at, 16), half), :], sems.at[len(copies)]
                    )
                )
    return copies


def down_and_back(active, slope, normed, vec, counts, pooled_grad, ids, bufs, sentences, length):
    rows, wide = active.shape
    width = normed.shape[1]
    shard = wide // 8
    half = width // 2
    group = 256

    def body(ids_ref, counts_ref, act_hbm, slope_ref, vec_ref, pg_ref, n_hbm, b0, b1, b2, b3, pooled_ref, vg_ref, send_ref, keep_ref, gup_ref, gbias_ref, gres_hbm, w_ref, acc_ref, n_ref, glow_ref, act_ref, t_ref, sems, more):
        step = pl.program_id(0)
        place = Place(ids_ref)
        bufs_ref = (b0, b1, b2, b3)
        load = pltpu.make_async_copy(n_hbm, n_ref, more.at[0])
        load_active = pltpu.make_async_copy(act_hbm, act_ref, more.at[1 + sentences])

        def columns_of(phase):
            return pl.ds(aligned(relative(ids_ref, step - phase) * shard, 128), shard)

        def out(s):
            here = pl.ds(aligned(s * length, length), length)
            return pltpu.make_async_copy(acc_ref.at[here, :], gres_hbm.at[here, :], more.at[1 + s])

        @pl.when(step == 0)
        def _():
            copies = natural_copies(place, bufs_ref, w_ref, sems)
            load_active.start()
            for copy in copies:
                copy.start()
            load.start()
            vg_ref[...] = jnp.zeros_like(vg_ref)
            for copy in copies:
                copy.wait()
            load_active.wait()
            for g in range(width // group):
                cols = slice(g * group, (g + 1) * group)
                acc_ref[:, cols] = dot(act_ref[...], w_ref[:, cols])
            load.wait()

            def norm_rows(s, carry):
                here = pl.ds(aligned(s * length, length), length)
                hidden = n_ref[here, :] * row(vec_ref, 3) + row(vec_ref, 4)
                n2, inverse = layer_norm(hidden + (acc_ref[here, :] + row(vec_ref, 5)))
                valid = lax.broadcasted_iota(jnp.int32, (length, width), 0) < counts_ref[s]
                count = counts_ref[s].astype(F32)
                out_rows = jnp.where(valid, n2 * row(vec_ref, 6) + row(vec_ref, 7), 0.0)
                pooled_ref[pl.ds(s, 1), :] = jnp.sum(out_rows, 0, keepdims=True) / count
                grad = jnp.where(valid, pg_ref[pl.ds(s, 1), :] / count, 0.0)
                vg_ref[0:1, :] += jnp.sum(grad * n2, 0, keepdims=True)
                vg_ref[1:2, :] += jnp.sum(grad, 0, keepdims=True)
                gres = norm_back(grad, n2, inverse, row(vec_ref, 6))
                acc_ref[here, :] = gres
                glow = gres.astype(BF)
                glow_ref[here, :] = glow
                vg_ref[2:3, :] += jnp.sum(glow.astype(F32), 0, keepdims=True)
                out(s).start()
                return carry

            lax.fori_loop(0, sentences, norm_rows, 0)
            t_ref[...] = glow_ref[...].T

        @pl.when(jnp.logical_and(step >= 1, step < 9))
        def _():
            for cc, out_ref in ((0, keep_ref), (1, send_ref)):
                core = lax.bitwise_xor(place.c, cc)
                out_ref[0, 0, 0] = dot(
                    t_ref[pl.ds(aligned(core * half, half), half), :], act_ref[:, columns_of(1)]
                ).astype(BF)

        @pl.when(step >= 9)
        def _():
            gact = dot_nt(glow_ref[...], w_ref[columns_of(9), :])
            gup = (gact * slope_ref[...].astype(F32)).astype(BF)
            gup_ref[...] = gup
            gbias_ref[...] = jnp.sum(gup.astype(F32), 0, keepdims=True)

        @pl.when(step == 16)
        def _():
            for s in range(sentences):
                out(s).wait()

    def at(step, phase):
        return jnp.clip(step - phase, 0, 7)

    def grad_block(step, ids, counts):
        r = at(step, 1)
        return (0, lax.rem(r, 2), lax.div(r, 2), 0, 0)

    def columns(phase):
        return lambda step, ids, counts: (0, relative(ids, at(step, phase)))

    grads = (struct((1, 2, 4, half, shard), BF), (1, 1, 1, half, shard), grad_block)
    return grid_call(
        body,
        "down_and_back",
        (17,),
        (ids, counts),
        [
            left(active),
            (slope, (rows, shard), columns(9)),
            whole(vec),
            whole(pooled_grad),
            left(normed),
        ]
        + [left(b) for b in bufs],
        [
            whole(struct((sentences, width), F32)),
            whole(struct((8, width), F32)),
            grads,
            grads,
            (struct((rows, wide), BF), (rows, shard), columns(9)),
            (struct((1, wide), F32), (1, shard), columns(9)),
            left(struct((rows, width), F32)),
        ],
        [
            pltpu.VMEM((wide, width), BF),
            pltpu.VMEM((rows, width), F32),
            pltpu.VMEM((rows, width), F32),
            pltpu.VMEM((rows, width), BF),
            pltpu.VMEM((rows, wide), BF),
            pltpu.VMEM((width, rows), BF),
            pltpu.SemaphoreType.DMA((16,)),
            pltpu.SemaphoreType.DMA((2 + sentences,)),
        ],
        6 * rows * width * wide,
    )


def up_and_back(low, gup, gres, normed, inverse, vec, ids, bufs, length):
    rows, wide = gup.shape
    width = gres.shape[1]
    sentences = rows // length
    group, block = 256, 512
    steps = wide // block
    per = steps // 2

    def body(ids_ref, low_ref, gup_ref, vec_ref, gres_hbm, n_hbm, inv_hbm, *rest):
        bufs_ref = rest[: len(bufs)]
        send_ref, keep_ref, gctx_ref, vg_ref, gattn_hbm, glow_hbm, w_ref, acc_ref, gres_ref, n_ref, inv_ref, glow_ref, t_ref, p_ref, gup_all, sems, more = rest[len(bufs) :]
        step = pl.program_id(0)
        place = Place(ids_ref)
        loads = [
            pltpu.make_async_copy(a, b, more.at[i])
            for i, (a, b) in enumerate(((gres_hbm, gres_ref), (n_hbm, n_ref), (inv_hbm, inv_ref)))
        ]
        copies = piece_copies(place, bufs_ref, w_ref, sems, width // 8, True)

        @pl.when(step == 0)
        def _():
            for copy in copies:
                copy.start()
            for load in loads:
                load.start()
            t_ref[...] = low_ref[...].T
            put_relative(place, t_ref, p_ref)

        put_halves(dot(p_ref[...], gup_ref[...]).astype(BF), send_ref, keep_ref)

        gup_all[:, pl.ds(aligned(step * block, 128), block)] = gup_ref[...]

        @pl.when(step == steps - 1)
        def _():
            for copy in copies:
                copy.wait()
            for g in range(width // group):
                cols = slice(g * group, (g + 1) * group)
                acc_ref[:, cols] = dot_nt(gup_all[...], w_ref[cols, width:])
            for load in loads:
                load.wait()
            vg_ref[...] = jnp.zeros_like(vg_ref)

            def outs(s):
                here = pl.ds(aligned(s * length, length), length)
                return (
                    pltpu.make_async_copy(acc_ref.at[here, :], gattn_hbm.at[here, :], more.at[3 + s]),
                    pltpu.make_async_copy(
                        glow_ref.at[here, :], glow_hbm.at[here, :], more.at[3 + sentences + s]
                    ),
                )

            def norm_rows(s, carry):
                here = pl.ds(aligned(s * length, length), length)
                grad = acc_ref[here, :] + gres_ref[here, :]
                normed = n_ref[here, :]
                vg_ref[0:1, :] += jnp.sum(grad * normed, 0, keepdims=True)
                vg_ref[1:2, :] += jnp.sum(grad, 0, keepdims=True)
                gattn = norm_back(grad, normed, inv_ref[here, 0:1], row(vec_ref, 3))
                acc_ref[here, :] = gattn
                glow = gattn.astype(BF)
                glow_ref[here, :] = glow
                vg_ref[2:3, :] += jnp.sum(glow.astype(F32), 0, keepdims=True)
                for copy in outs(s):
                    copy.start()
                return carry

            lax.fori_loop(0, sentences, norm_rows, 0)
            for g in range(width // group):
                gctx_ref[:, g * group : (g + 1) * group] = dot_nt(
                    glow_ref[...], w_ref[g * group : (g + 1) * group, :width]
                ).astype(BF)
            for s in range(sentences):
                for copy in outs(s):
                    copy.wait()

    blocks = weight_blocks(width, block, per)
    return grid_call(
        body,
        "up_and_back",
        (steps,),
        (ids,),
        [whole(low), (gup, (rows, block), lambda j, ids: (0, j)), whole(vec), left(gres), left(normed), left(inverse)]
        + [left(b) for b in bufs],
        [
            blocks,
            blocks,
            whole(struct((rows, width), BF)),
            whole(struct((8, width), F32)),
            left(struct((rows, width), F32)),
            left(struct((rows, width), BF)),
        ],
        [
            pltpu.VMEM((width, width + wide), BF),
            pltpu.VMEM((rows, width), F32),
            pltpu.VMEM((rows, width), F32),
            pltpu.VMEM((rows, width), F32),
            pltpu.VMEM((rows, 128), F32),
            pltpu.VMEM((rows, width), BF),
            pltpu.VMEM((width, rows), BF),
            pltpu.VMEM((width, rows), BF),
            pltpu.VMEM((rows, wide), BF),
            pltpu.SemaphoreType.DMA((32,)),
            pltpu.SemaphoreType.DMA((3 + 2 * sentences,)),
        ],
        2 * rows * width * (width + 2 * wide),
    )


def attend_backward(qkv, gctx, lse, counts, sentences, length, low, high, name):
    rows, width = gctx.shape
    span = (high - low) * 128
    twos = range(low // 2, high // 2)

    def body(counts_ref, *refs):
        parts = [refs[i * len(twos) : (i + 1) * len(twos)] for i in range(3)]
        gctx_ref, lse_ref, gqkv_ref, vs_ref = refs[3 * len(twos) :]
        s = pl.program_id(0)

        @pl.when(s == 0)
        def _():
            vs_ref[...] = jnp.zeros_like(vs_ref)

        count = counts_ref[s]
        for p in range(low, high):
            at = (p - low) * 128
            block, cols = (p - low) // 2, slice(p % 2 * 128, p % 2 * 128 + 128)
            query = parts[0][block][:, cols] * jnp.asarray(HEAD**-0.5, BF)
            keys2 = two_heads(parts[1][block][:, cols])
            values2 = two_heads(parts[2][block][:, cols])
            gout = gctx_ref[:, at : at + 128]
            scores = masked_scores(query, keys2, count, length)
            lse2 = halves(lse_ref[:, 2 * p : 2 * p + 1], lse_ref[:, 2 * p + 1 : 2 * p + 2], length)
            probs = jnp.exp(scores - lse2)
            gprobs = dot_nt(gout, values2)
            weighted = gprobs * probs
            sums = halves(
                jnp.sum(weighted[:, :length], -1, keepdims=True),
                jnp.sum(weighted[:, length:], -1, keepdims=True),
                length,
            )
            gscores = (probs * (gprobs - sums)).astype(BF)
            gq = (dot(gscores, keys2) * HEAD**-0.5).astype(BF)
            gk = one_of_two(dot_tn(gscores, query)).astype(BF)
            gv = one_of_two(dot_tn(probs.astype(BF), gout)).astype(BF)
            gqkv_ref[:, at : at + 128] = gq
            gqkv_ref[:, span + at : span + at + 128] = gk
            gqkv_ref[:, 2 * span + at : 2 * span + at + 128] = gv
            vs_ref[0:1, at : at + 128] += jnp.sum(gq.astype(F32), 0, keepdims=True)
            vs_ref[1:2, at : at + 128] += jnp.sum(gv.astype(F32), 0, keepdims=True)

    def by_rows(array):
        return (array, (length, array.shape[1]), lambda s, counts: (s, 0))

    return grid_call(
        body,
        name,
        (sentences,),
        (counts,),
        [
            (qkv, (length, 256), lambda s, counts, at=part * width // 256 + b: (s, at))
            for part in range(3)
            for b in twos
        ]
        + [(gctx, (length, span), lambda s, counts: (s, low * 128 // span)), by_rows(lse)],
        [by_rows(struct((rows, 3 * span), BF)), whole(struct((8, span), F32))],
        [],
        20 * rows * length * span,
    )


def weight_blocks(width, group, per):
    half = width // 16
    return (
        struct((2, 2, 4, half, per * group), BF),
        (1, 2, 4, half, group),
        lambda j, ids: (lax.bitwise_xor(ids[2], lax.div(j, per)), 0, 0, 0, lax.rem(j, per)),
    )


def put_halves(dw, send_ref, keep_ref):
    width, group = dw.shape
    shape = (2, 4, width // 16, group)
    keep_ref[0] = dw[: width // 2].reshape(shape)
    send_ref[0] = dw[width // 2 :].reshape(shape)


def attend_weight(gqkv, tokens, context, glow, ids):
    rows, width = tokens.shape
    group = 384
    first, second = gqkv.shape[1] // group, width // group
    groups = first + second

    def body(ids_ref, gqkv_ref, glow_ref, x_ref, ctx_ref, send_ref, keep_ref, t_ref, x_t):
        j = pl.program_id(0)
        place = Place(ids_ref)

        @pl.when(j == 0)
        def _():
            t_ref[...] = x_ref[...].T
            put_relative(place, t_ref, x_t)

        @pl.when(j == first)
        def _():
            t_ref[...] = ctx_ref[...].T
            put_relative(place, t_ref, x_t)

        @pl.when(j < first)
        def _():
            put_halves(dot(x_t[...], gqkv_ref[...]).astype(BF), send_ref, keep_ref)

        @pl.when(j >= first)
        def _():
            put_halves(dot(x_t[...], glow_ref[...]).astype(BF), send_ref, keep_ref)

    blocks = weight_blocks(width, group, groups // 2)
    return grid_call(
        body,
        "attention_weight",
        (groups,),
        (ids,),
        [
            (gqkv, (rows, group), lambda j, ids: (0, jnp.minimum(j, first - 1))),
            (glow, (rows, group), lambda j, ids: (0, jnp.maximum(j - first, 0))),
            whole(tokens),
            whole(context),
        ],
        [blocks, blocks],
        [pltpu.VMEM((width, rows), BF)] * 2,
        2 * rows * width * 4 * width,
    )


def last_weight(gqkv, tokens, vg_a, vg_b, vg_attn, vg_ffn, gbias_in, ids):
    rows, width = tokens.shape
    group = 256
    first = gqkv.shape[1] // group
    groups = first + 1
    cut, ratio, part = vg_a.shape[1], gbias_in.shape[1] // width, width // 8

    def body(ids_ref, gqkv_ref, x_ref, va_ref, vb_ref, attn_ref, ffn_ref, bias_ref, send_ref, keep_ref, t_ref, x_t, r_ref, v_ref):
        j = pl.program_id(0)
        place = Place(ids_ref)

        @pl.when(j == 0)
        def _():
            t_ref[...] = x_ref[...].T
            put_relative(place, t_ref, x_t)

        @pl.when(j < first)
        def _():
            put_halves(dot(x_t[...], gqkv_ref[...]).astype(BF), send_ref, keep_ref)

        @pl.when(j == first)
        def _():
            r_ref[...] = jnp.zeros_like(r_ref)
            r_ref[0:2, :cut] = va_ref[0:2, :]
            r_ref[0:2, cut:] = vb_ref[0:2, :]
            r_ref[2:3, :] = attn_ref[2:3, :]
            r_ref[3:5, :] = attn_ref[0:2, :]
            r_ref[5:6, :] = ffn_ref[2:3, :]
            r_ref[6:8, :] = ffn_ref[0:2, :]
            for shard in range(8):
                for i in range(ratio):
                    at = (shard * ratio + i) * part
                    r_ref[8 + i : 9 + i, shard * part : (shard + 1) * part] = bias_ref[:, at : at + part]
            v_ref[0] = r_ref[...].T
            put_relative(place, v_ref.at[0], v_ref.at[1])
            both = jnp.concatenate([v_ref[1], jnp.zeros((width, group - 128), F32)], axis=1)
            put_halves(both.astype(BF), send_ref, keep_ref)

    blocks = weight_blocks(width, group, groups // 2)
    return grid_call(
        body,
        "last_weight",
        (groups,),
        (ids,),
        [
            (gqkv, (rows, group), lambda j, ids: (0, jnp.minimum(j, first - 1))),
            whole(tokens),
            whole(vg_a),
            whole(vg_b),
            whole(vg_attn),
            whole(vg_ffn),
            whole(gbias_in),
        ],
        [blocks, blocks],
        [pltpu.VMEM((width, rows), BF)] * 2
        + [pltpu.VMEM((128, width), F32), pltpu.VMEM((2, width, 128), F32)],
        2 * rows * width * width,
    )


def tokens_backward(gqkv_a, gqkv_b, gattn, ids, bufs):
    rows, width = gattn.shape
    group = 256
    span_a, span_b = gqkv_a.shape[1] // 3, gqkv_b.shape[1] // 3

    def body(ids_ref, ga_hbm, gb_hbm, gattn_ref, b0, b1, b2, b3, gx_ref, w_ref, g_ref, sems, more):
        copies = piece_copies(Place(ids_ref), (b0, b1, b2, b3), w_ref, sems, width // 8, False)
        for i in range(3):
            for at, span, source in ((0, span_a, ga_hbm), (span_a, span_b, gb_hbm)):
                copies.append(
                    pltpu.make_async_copy(
                        source.at[:, i * span : (i + 1) * span],
                        g_ref.at[:, i * width + at : i * width + at + span],
                        more.at[2 * i + at // span_a],
                    )
                )
        for copy in copies:
            copy.start()
        for copy in copies:
            copy.wait()
        for g in range(width // group):
            cols = slice(g * group, (g + 1) * group)
            gx_ref[:, cols] = gattn_ref[:, cols] + dot_nt(g_ref[...], w_ref[cols, : 3 * width])

    return call(
        body,
        "tokens_back",
        [(ids, "s"), (gqkv_a, "a"), (gqkv_b, "a"), (gattn, "v")] + [(b, "a") for b in bufs],
        [struct((rows, width), F32)],
        [
            pltpu.VMEM((width, 3 * width + 128), BF),
            pltpu.VMEM((rows, 3 * width), BF),
            pltpu.SemaphoreType.DMA((16,)),
            pltpu.SemaphoreType.DMA((6,)),
        ],
        2 * rows * width * 3 * width,
    )[0]


def norm_parts(token_rows, gain_vec, shift_vec):
    row_mean = jnp.mean(token_rows, -1, keepdims=True)
    centred = token_rows - row_mean
    inverse = lax.rsqrt(jnp.mean(centred * centred, -1, keepdims=True) + norm_eps)
    normed = centred * inverse
    return (normed * gain_vec + shift_vec, normed, inverse)


def plain_norm_back(grad_out, normed, inverse, gain_vec):
    grad_gain = jnp.sum(grad_out * normed, 0)
    grad_shift = jnp.sum(grad_out, 0)
    scaled = grad_out * gain_vec
    grad_in = inverse * (
        scaled
        - jnp.mean(scaled, -1, keepdims=True)
        - normed * jnp.mean(scaled * normed, -1, keepdims=True)
    )
    return (grad_in, grad_gain, grad_shift)


def attention_scores(query_rows, key_rows, key_valid):
    scores = jnp.einsum(
        "sqhd,skhd->shqk", query_rows, key_rows, preferred_element_type=jnp.float32
    ) * HEAD ** (-0.5)
    return jnp.where(key_valid[:, None, None, :], scores, -1000000000.0)


def forward(tokens, lengths, weights):
    (
        w_qkv,
        bias_query,
        bias_value,
        w_out,
        bias_out,
        gain_attn,
        shift_attn,
        w_in,
        bias_in,
        w_down,
        bias_down,
        gain_ffn,
        shift_ffn,
    ) = weights
    sentences, length, model_width = tokens.shape
    head_count = model_width // HEAD
    token_rows = tokens.reshape(sentences * length, model_width)
    bias_qkv = jnp.concatenate([bias_query, jnp.zeros_like(bias_query), bias_value]).astype(
        jnp.float32
    )
    packed = (jnp.dot(token_rows, w_qkv, preferred_element_type=jnp.float32) + bias_qkv).astype(
        jnp.bfloat16
    )
    packed = packed.reshape(sentences, length, 3, head_count, HEAD)
    query_rows = packed[:, :, 0]
    key_rows = packed[:, :, 1]
    value_rows = packed[:, :, 2]
    key_valid = jnp.arange(length)[None, :] < lengths[:, None]
    scores = attention_scores(query_rows, key_rows, key_valid)
    row_max = jnp.max(scores, -1, keepdims=True)
    log_total = row_max + jnp.log(jnp.sum(jnp.exp(scores - row_max), -1, keepdims=True))
    attn_probs = jnp.exp(scores - log_total)
    context = jnp.einsum(
        "shqk,skhd->sqhd",
        attn_probs.astype(jnp.bfloat16),
        value_rows,
        preferred_element_type=jnp.float32,
    )
    context = context.reshape(sentences * length, model_width).astype(jnp.bfloat16)
    attn_out = jnp.dot(context, w_out, preferred_element_type=jnp.float32) + bias_out.astype(
        jnp.float32
    )
    hidden, normed_attn, inverse_attn = norm_parts(
        token_rows.astype(jnp.float32) + attn_out,
        gain_attn.astype(jnp.float32),
        shift_attn.astype(jnp.float32),
    )
    hidden_low = hidden.astype(jnp.bfloat16)
    up_rows = jnp.dot(hidden_low, w_in, preferred_element_type=jnp.float32) + bias_in.astype(
        jnp.float32
    )
    active = jax.nn.gelu(up_rows, approximate=False).astype(jnp.bfloat16)
    ffn_out = jnp.dot(active, w_down, preferred_element_type=jnp.float32) + bias_down.astype(
        jnp.float32
    )
    output, normed_ffn, inverse_ffn = norm_parts(
        hidden + ffn_out, gain_ffn.astype(jnp.float32), shift_ffn.astype(jnp.float32)
    )
    valid_mask = key_valid.astype(jnp.float32)
    pooled = jnp.sum(
        output.reshape(sentences, length, model_width) * valid_mask[:, :, None], 1
    ) / lengths[:, None].astype(jnp.float32)
    kept = (
        key_valid,
        query_rows,
        key_rows,
        value_rows,
        log_total,
        context,
        normed_attn,
        inverse_attn,
        hidden_low,
        up_rows,
        active,
        normed_ffn,
        inverse_ffn,
    )
    return (pooled, kept)


def backward(tokens, lengths, pooled_grad, weights, kept):
    (
        w_qkv,
        bias_query,
        bias_value,
        w_out,
        bias_out,
        gain_attn,
        shift_attn,
        w_in,
        bias_in,
        w_down,
        bias_down,
        gain_ffn,
        shift_ffn,
    ) = weights
    (
        key_valid,
        query_rows,
        key_rows,
        value_rows,
        log_total,
        context,
        normed_attn,
        inverse_attn,
        hidden_low,
        up_rows,
        active,
        normed_ffn,
        inverse_ffn,
    ) = kept
    sentences, length, model_width = tokens.shape
    head_count = model_width // HEAD
    token_rows = tokens.reshape(sentences * length, model_width)
    valid_mask = key_valid.astype(jnp.float32)
    per_sentence = pooled_grad / lengths[:, None].astype(jnp.float32)
    grad_output = (valid_mask[:, :, None] * per_sentence[:, None, :]).reshape(
        sentences * length, model_width
    )
    grad_res_ffn, grad_gain_ffn, grad_shift_ffn = plain_norm_back(
        grad_output, normed_ffn, inverse_ffn, gain_ffn.astype(jnp.float32)
    )
    grad_ffn_low = grad_res_ffn.astype(jnp.bfloat16)
    grad_bias_down = jnp.sum(grad_ffn_low.astype(jnp.float32), 0)
    grad_w_down = jnp.einsum("tf,td->fd", active, grad_ffn_low, preferred_element_type=jnp.float32)
    grad_active = jnp.einsum("td,fd->tf", grad_ffn_low, w_down, preferred_element_type=jnp.float32)
    gelu_value, gelu_pull = jax.vjp(partial(jax.nn.gelu, approximate=False), up_rows)
    grad_up = gelu_pull(grad_active)[0].astype(jnp.bfloat16)
    grad_bias_in = jnp.sum(grad_up.astype(jnp.float32), 0)
    grad_w_in = jnp.einsum("td,tf->df", hidden_low, grad_up, preferred_element_type=jnp.float32)
    grad_hidden = (
        jnp.einsum("tf,df->td", grad_up, w_in, preferred_element_type=jnp.float32) + grad_res_ffn
    )
    grad_res_attn, grad_gain_attn, grad_shift_attn = plain_norm_back(
        grad_hidden, normed_attn, inverse_attn, gain_attn.astype(jnp.float32)
    )
    grad_attn_low = grad_res_attn.astype(jnp.bfloat16)
    grad_bias_out = jnp.sum(grad_attn_low.astype(jnp.float32), 0)
    grad_w_out = jnp.einsum("tc,td->cd", context, grad_attn_low, preferred_element_type=jnp.float32)
    grad_context = jnp.einsum("td,cd->tc", grad_attn_low, w_out, preferred_element_type=jnp.float32)
    grad_context = grad_context.astype(jnp.bfloat16).reshape(sentences, length, head_count, HEAD)
    scores = attention_scores(query_rows, key_rows, key_valid)
    attn_probs = jnp.exp(scores - log_total)
    grad_probs = jnp.einsum(
        "sqhd,skhd->shqk", grad_context, value_rows, preferred_element_type=jnp.float32
    )
    grad_values = jnp.einsum(
        "shqk,sqhd->skhd",
        attn_probs.astype(jnp.bfloat16),
        grad_context,
        preferred_element_type=jnp.float32,
    )
    grad_scores = (
        attn_probs * (grad_probs - jnp.sum(grad_probs * attn_probs, -1, keepdims=True))
    ).astype(jnp.bfloat16)
    grad_queries = jnp.einsum(
        "shqk,skhd->sqhd", grad_scores, key_rows, preferred_element_type=jnp.float32
    ) * HEAD ** (-0.5)
    grad_keys = jnp.einsum(
        "shqk,sqhd->skhd", grad_scores, query_rows, preferred_element_type=jnp.float32
    ) * HEAD ** (-0.5)
    grad_qkv = jnp.stack([grad_queries, grad_keys, grad_values], 2)
    grad_qkv = grad_qkv.reshape(sentences * length, 3 * model_width).astype(jnp.bfloat16)
    qkv_sums = jnp.sum(grad_qkv.astype(jnp.float32), 0)
    grad_bias_query = qkv_sums[:model_width]
    grad_bias_value = qkv_sums[2 * model_width :]
    grad_w_qkv = jnp.einsum("td,tc->dc", token_rows, grad_qkv, preferred_element_type=jnp.float32)
    grad_tokens = (
        jnp.einsum("tc,dc->td", grad_qkv, w_qkv, preferred_element_type=jnp.float32) + grad_res_attn
    )
    grad_tokens = grad_tokens.reshape(sentences, length, model_width)
    grad_terms = (
        grad_w_qkv,
        grad_bias_query,
        grad_bias_value,
        grad_w_out,
        grad_bias_out,
        grad_gain_attn,
        grad_shift_attn,
        grad_w_in,
        grad_bias_in,
        grad_w_down,
        grad_bias_down,
        grad_gain_ffn,
        grad_shift_ffn,
    )
    return (grad_terms, grad_tokens)


def on_device(
    tokens,
    lengths,
    pooled_grad,
    w_qkv,
    bias_query,
    bias_value,
    w_out,
    bias_out,
    gain_attn,
    shift_attn,
    w_in,
    bias_in,
    w_down,
    bias_down,
    gain_ffn,
    shift_ffn,
):
    weights = (
        lax.all_gather(w_qkv, "fsdp", axis=0, tiled=True),
        lax.all_gather(bias_query, "fsdp", axis=0, tiled=True),
        lax.all_gather(bias_value, "fsdp", axis=0, tiled=True),
        lax.all_gather(w_out, "fsdp", axis=0, tiled=True),
        lax.all_gather(bias_out, "fsdp", axis=0, tiled=True),
        lax.all_gather(gain_attn, "fsdp", axis=0, tiled=True),
        lax.all_gather(shift_attn, "fsdp", axis=0, tiled=True),
        lax.all_gather(w_in, "fsdp", axis=0, tiled=True),
        lax.all_gather(bias_in, "fsdp", axis=0, tiled=True),
        lax.all_gather(w_down, "fsdp", axis=0, tiled=True),
        lax.all_gather(bias_down, "fsdp", axis=0, tiled=True),
        lax.all_gather(gain_ffn, "fsdp", axis=0, tiled=True),
        lax.all_gather(shift_ffn, "fsdp", axis=0, tiled=True),
    )
    pooled, kept = forward(tokens, lengths, weights)
    grad_terms, grad_tokens = backward(tokens, lengths, pooled_grad, weights, kept)
    (
        grad_w_qkv,
        grad_bias_query,
        grad_bias_value,
        grad_w_out,
        grad_bias_out,
        grad_gain_attn,
        grad_shift_attn,
        grad_w_in,
        grad_bias_in,
        grad_w_down,
        grad_bias_down,
        grad_gain_ffn,
        grad_shift_ffn,
    ) = grad_terms
    shares = (
        lax.psum_scatter(grad_w_qkv, "fsdp", scatter_dimension=0, tiled=True),
        lax.psum_scatter(grad_bias_query, "fsdp", scatter_dimension=0, tiled=True),
        lax.psum_scatter(grad_bias_value, "fsdp", scatter_dimension=0, tiled=True),
        lax.psum_scatter(grad_w_out, "fsdp", scatter_dimension=0, tiled=True),
        lax.psum_scatter(grad_bias_out, "fsdp", scatter_dimension=0, tiled=True),
        lax.psum_scatter(grad_gain_attn, "fsdp", scatter_dimension=0, tiled=True),
        lax.psum_scatter(grad_shift_attn, "fsdp", scatter_dimension=0, tiled=True),
        lax.psum_scatter(grad_w_in, "fsdp", scatter_dimension=0, tiled=True),
        lax.psum_scatter(grad_bias_in, "fsdp", scatter_dimension=0, tiled=True),
        lax.psum_scatter(grad_w_down, "fsdp", scatter_dimension=0, tiled=True),
        lax.psum_scatter(grad_bias_down, "fsdp", scatter_dimension=0, tiled=True),
        lax.psum_scatter(grad_gain_ffn, "fsdp", scatter_dimension=0, tiled=True),
        lax.psum_scatter(grad_shift_ffn, "fsdp", scatter_dimension=0, tiled=True),
    )
    (
        share_w_qkv,
        share_bias_query,
        share_bias_value,
        share_w_out,
        share_bias_out,
        share_gain_attn,
        share_shift_attn,
        share_w_in,
        share_bias_in,
        share_w_down,
        share_bias_down,
        share_gain_ffn,
        share_shift_ffn,
    ) = shares
    totals = (
        lax.psum(share_w_qkv.astype(jnp.bfloat16), "dp").astype(jnp.float32),
        lax.psum(share_bias_query.astype(jnp.bfloat16), "dp").astype(jnp.float32),
        lax.psum(share_bias_value.astype(jnp.bfloat16), "dp").astype(jnp.float32),
        lax.psum(share_w_out.astype(jnp.bfloat16), "dp").astype(jnp.float32),
        lax.psum(share_bias_out.astype(jnp.bfloat16), "dp").astype(jnp.float32),
        lax.psum(share_gain_attn.astype(jnp.bfloat16), "dp").astype(jnp.float32),
        lax.psum(share_shift_attn.astype(jnp.bfloat16), "dp").astype(jnp.float32),
        lax.psum(share_w_in.astype(jnp.bfloat16), "dp").astype(jnp.float32),
        lax.psum(share_bias_in.astype(jnp.bfloat16), "dp").astype(jnp.float32),
        lax.psum(share_w_down.astype(jnp.bfloat16), "dp").astype(jnp.float32),
        lax.psum(share_bias_down.astype(jnp.bfloat16), "dp").astype(jnp.float32),
        lax.psum(share_gain_ffn.astype(jnp.bfloat16), "dp").astype(jnp.float32),
        lax.psum(share_shift_ffn.astype(jnp.bfloat16), "dp").astype(jnp.float32),
    )
    return (
        pooled,
        grad_tokens,
        totals[0],
        totals[1],
        totals[2],
        totals[3],
        totals[4],
        totals[5],
        totals[6],
        totals[7],
        totals[8],
        totals[9],
        totals[10],
        totals[11],
        totals[12],
    )


def swap(array, axis, bits):
    pairs = [(i, i ^ bits) for i in range(lax.axis_size(axis))]
    return lax.ppermute(array, axis, pairs)


def hold(value, *after):
    return lax.optimization_barrier((value, *after))[0]


def gather_z(piece, *after):
    return jnp.stack([hold(piece, *after)] + [swap(piece, "fsdp", 2 * k) for k in range(1, 4)])


def add(*terms):
    total = terms[0].astype(F32)
    for term in terms[1:]:
        total = total + term.astype(F32)
    return total.astype(BF)


def sum_core(send, keep, *after):
    return add(hold(keep, *after), swap(send, "dp", 1))


def sum_x(total, *after):
    return add(hold(total[0], *after), swap(total[1], "dp", 2))


def sum_y(total, *after):
    return add(hold(total[0], *after), swap(total[1], "fsdp", 1))


def sum_z(total, *after):
    return add(hold(total[0], *after), *[swap(total[k], "fsdp", 2 * k) for k in range(1, 4)])


def in_order_parts(own, other, bit):
    return jnp.where(bit == 0, own, other), jnp.where(bit == 0, other, own)


def in_order(own, other, bit, axis):
    first = jnp.where(bit == 0, own, other)
    second = jnp.where(bit == 0, other, own)
    return jnp.concatenate([first, second], axis=axis)


def share_core(own, c):
    return in_order(own, swap(own, "dp", 1), c, 0).astype(F32)


def on_device_split(
    tokens,
    lengths,
    pooled_grad,
    w_qkv,
    bias_query,
    bias_value,
    w_out,
    bias_out,
    gain_attn,
    shift_attn,
    w_in,
    bias_in,
    w_down,
    bias_down,
    gain_ffn,
    shift_ffn,
):
    sentences, length, width = tokens.shape
    rows = sentences * length
    wide = w_in.shape[1]
    part = width // 8
    dp, fsdp = lax.axis_index("dp"), lax.axis_index("fsdp")
    x, c = dp // 2, dp % 2
    ids = jnp.stack([fsdp // 2, fsdp % 2, x, c]).astype(jnp.int32)
    token_rows = tokens.reshape(rows, width)

    vectors = jnp.stack(
        [bias_query, bias_value, bias_out, gain_attn, shift_attn, bias_down, gain_ffn, shift_ffn]
    )
    vectors = jnp.concatenate([vectors, bias_in.reshape(wide // width, part)], 0)
    vectors = jnp.pad(vectors.T, ((0, 0), (0, 128 - vectors.shape[0])))
    first = jnp.concatenate([w_qkv, vectors], 1)
    second = jnp.concatenate([w_out, w_in], 1)
    half = part // 2
    first = lax.dynamic_slice(first, (c * half, 0), (half, first.shape[1]))
    span = second.shape[1] // 2
    second = lax.dynamic_slice(second, (c * half, x * span), (half, span))
    third = lax.dynamic_slice(w_down, (c * (w_down.shape[0] // 2), 0), (w_down.shape[0] // 2, width))

    near1 = gather_z(first)
    near2 = gather_z(hold(second, near1))
    far1 = hold(swap(near1, "fsdp", 1), near2)
    bufs1 = [near1, far1, swap(near1, "dp", 1), swap(far1, "dp", 1)]
    side2 = swap(near2, "dp", 2)
    qkv, vec = qkv_forward(hold(token_rows, near2), ids, bufs1)
    far2 = hold(swap(near2, "fsdp", 1), vec)
    context, lse = attend_forward(hold(qkv, side2), lengths, sentences, length)
    near3 = gather_z(hold(third, near2), context)
    side2 = hold(side2, context)
    far3 = swap(near3, "fsdp", 1)
    mine2 = [near2, far2, side2, swap(far2, "dp", 2)]
    bufs2 = mine2 + [swap(hold(m, context), "dp", 1) for m in mine2]
    ratio = wide // width
    bias_up = vec[8 : 8 + ratio].reshape(ratio, 8, part).transpose(1, 0, 2).reshape(1, wide)
    normed, inverse, low, active, slope = up_forward(
        context, token_rows, vec, bias_up, ids, bufs2, length
    )
    far3 = hold(far3, low)
    bufs3 = [near3, far3, swap(near3, "dp", 1), swap(far3, "dp", 1)]
    pooled, vg_ffn, send3, keep3, gup, gbias_in, gres = down_and_back(
        active, slope, normed, vec, lengths, pooled_grad, ids, bufs3, sentences, length
    )
    send2, keep2, gctx, vg_attn, gattn, gattn_low = up_and_back(
        low, gup, gres, normed, inverse, vec, ids, bufs2, length
    )
    sums3 = sum_core(send3, keep3, gctx)
    sums2 = sum_core(send2, keep2, sums3)
    pairs = width // 128
    most = pairs * 2 // 3
    gqkv_a, vg_a = attend_backward(
        qkv, hold(gctx, sums3, sums2), lse, lengths, sentences, length, 0, most, "attention_back"
    )
    send_a, keep_a = attend_weight(gqkv_a, token_rows, context, gattn_low, ids)
    sums2 = sum_x(sums2, keep_a)
    sums3 = sum_y(sums3[0], keep_a)
    sums_a = sum_core(hold(send_a, sums2, sums3), keep_a)
    gqkv_b, vg_b = attend_backward(
        qkv, hold(gctx, sums_a), lse, lengths, sentences, length, most, pairs, "attention_back_rest"
    )
    send_b, keep_b = last_weight(gqkv_b, token_rows, vg_a, vg_b, vg_attn, vg_ffn, gbias_in, ids)
    sums2 = sum_y(sums2, keep_b)
    sums3 = sum_z(sums3, keep_b)
    sums_a = sum_x(sums_a, keep_b)
    sums_b = sum_core(hold(send_b, sums_a), keep_b)
    gtokens = tokens_backward(gqkv_a, hold(gqkv_b, sums_b, sums2, sums3), gattn, ids, bufs1)
    sums2 = sum_z(sums2, gtokens)
    sums_b = sum_x(sums_b, sums2)
    sums_a = sum_y(sums_a, sums_b)
    sums3 = add(hold(sums3, sums_a), swap(sums3, "dp", 2))
    sums_a, sums2, sums3, sums_b = lax.optimization_barrier((sums_a, sums2, sums3, sums_b))
    sums_b = sum_y(sums_b)
    g_in = in_order(sums2, swap(sums2, "dp", 2), x, 1)
    sums_a, sums3, sums_b, g_in = lax.optimization_barrier((sums_a, sums3, sums_b, g_in))
    g_down = share_core(sums3, c).T
    g_in = share_core(g_in, c)
    sums = sum_z(jnp.concatenate([sums_a, sums_b], 2))
    wide_a = sums_a.shape[2]
    sums, other = in_order_parts(sums, swap(sums, "dp", 2), x)
    g_a = share_core(jnp.concatenate([sums[:, :wide_a], other[:, :wide_a]], 1), c)
    g_b = share_core(jnp.concatenate([sums[:, wide_a:], other[:, wide_a:]], 1), c)
    gtokens = gtokens.reshape(sentences, length, width)
    cut_a, cut_b = most * 128, (pairs - most) * 128
    g_qkv = [
        g[:, i * cut : (i + 1) * cut] for i in range(3) for g, cut in ((g_a, cut_a), (g_b, cut_b))
    ]
    g_vec = g_b[:, 3 * cut_b : 3 * cut_b + 8 + ratio].T
    return (
        pooled,
        gtokens,
        jnp.concatenate(g_qkv, 1),
        g_vec[0],
        g_vec[1],
        g_a[:, 3 * cut_a :],
        g_vec[2],
        g_vec[3],
        g_vec[4],
        g_in,
        g_vec[8:].reshape(wide // 8),
        g_down,
        g_vec[5],
        g_vec[6],
        g_vec[7],
    )


def solution(mesh):
    placed = (
        P(("dp", "fsdp"), None, None),
        P(("dp", "fsdp")),
        P(("dp", "fsdp"), None),
        P("fsdp", None),
        P("fsdp"),
        P("fsdp"),
        P("fsdp", None),
        P("fsdp"),
        P("fsdp"),
        P("fsdp"),
        P("fsdp", None),
        P("fsdp"),
        P("fsdp", None),
        P("fsdp"),
        P("fsdp"),
        P("fsdp"),
    )
    body = on_device_split if mesh.shape["fsdp"] == 8 and mesh.shape["dp"] == 4 else on_device
    return jax.shard_map(
        body,
        mesh=mesh,
        in_specs=placed,
        out_specs=(
            P(("dp", "fsdp"), None),
            P(("dp", "fsdp"), None, None),
            P("fsdp", None),
            P("fsdp"),
            P("fsdp"),
            P("fsdp", None),
            P("fsdp"),
            P("fsdp"),
            P("fsdp"),
            P("fsdp", None),
            P("fsdp"),
            P("fsdp", None),
            P("fsdp"),
            P("fsdp"),
            P("fsdp"),
        ),
        check_vma=False,
    )
```
